32 devices in a mesh: groups: 2 (over y), seq: 4 (over z), segment: 2 (over x), owner: 2 (over core).
Axes of the slice: x: 2, y: 2, z: 4, core: 2. Of those that a mesh axis runs over, the one named last changes fastest.
Arguments:
- layer_input_rows: bfloat16 [2, 512, 5376], P('segment', ('groups', 'seq')), parts along dimension 1, may hold values from -40 to 40
- encoded_query_rows: bfloat16 [2, 512, 2048], P('segment', ('groups', 'seq'), 'owner'), parts along dimension 1, may hold values from -213 to 213
- encoded_key_rows: bfloat16 [2, 512, 1024], P('segment', ('groups', 'seq'), 'owner'), parts along dimension 1, may hold values from -6 to 6
- layer_norm_gain: float32 [2, 5376], P('segment'), may hold values from 0.25 to 1.75
- base_value_matrix: bfloat16 [2, 5376, 1024], P('segment', ('seq', 'owner')), may hold values from -0.078125 to 0.078125
- adapter_down_panels: bfloat16 [2, 8, 5376, 64], P('segment', 'seq', 'owner'), may hold values from -0.078125 to 0.078125
- adapter_up_panels: bfloat16 [2, 8, 64, 1024], P('segment', 'seq', None, 'owner'), may hold values from -0.75 to 0.75
- request_token_lengths: int32 [8], P('groups'), parts along dimension 0, may hold values from 1 to 128, 256 in all
- adapter_per_request: int32 [8], P('groups'), parts along dimension 0, may hold values from 0 to 7
- rank_per_adapter: int32 [8], replicated, may hold values from 16 to 64
- slot_per_adapter: int32 [8], replicated, may hold values from 0 to 7, each once
Outputs:
- layer_output: bfloat16 [2, 512, 2048], P('segment', ('groups', 'seq'), 'owner'), parts along dimension 1
The draws below stay inside these ranges and needn't reach their ends.
There are 2 independent parts, one for each index of `groups`. The reference program is written for one: setup_inputs(seed, part) draws one part's arguments, and reference() takes and returns one part's arrays. A program takes and returns all parts, laid end to end along the dimension named above; an argument that names none is the same for every part. Nothing has to cross between parts.
All inputs are finite; a program needn't handle non-finite values.
Results may differ from the reference program's by a relative error of at most 0.0065.
Values may be sent and summed in bfloat16 or wider, within the bound.
A program may use at most 128 MiB of HBM per device.

```python
import math
import jax
import jax.numpy as jnp
import numpy as np
from jax import lax

TOK_DEV = 64
MODEL_WIDTH = 5376
WINDOW = 1024
HEADS = 16
KEY_VALUE_HEADS = 8
HEAD_SIZE = 128
MAX_RANK = 64
REQUESTS = 4
LAYER_COUNT = 2
SLOT_COUNT = 8
TOKEN_COUNT = 256


def draw_layer_input_rows(key, part):
    first_key, second_key, third_key = jax.random.split(key, 3)
    column_scale = jnp.exp(jax.random.uniform(second_key, (1, 1, MODEL_WIDTH), jnp.float32, math.log(0.3), math.log(3.0)))
    row_scale = jnp.exp(jax.random.uniform(third_key, (LAYER_COUNT, TOKEN_COUNT, 1), jnp.float32, math.log(0.5), math.log(2.0)))
    drawn = jnp.clip(jax.random.normal(first_key, (LAYER_COUNT, TOKEN_COUNT, MODEL_WIDTH), jnp.float32), -6.0, 6.0)
    return (drawn * column_scale * row_scale).astype(jnp.bfloat16)


def attention_pair(key):
    folded = jax.random.fold_in(key, 11)
    draw_query, draw_keys = jax.random.split(folded, 2)
    group_size = HEADS // KEY_VALUE_HEADS
    key_draw = jnp.clip(jax.random.normal(draw_keys, (LAYER_COUNT, TOKEN_COUNT, KEY_VALUE_HEADS, HEAD_SIZE), jnp.float32), -6.0, 6.0)
    queries = jnp.clip(jax.random.normal(draw_query, (LAYER_COUNT, TOKEN_COUNT, KEY_VALUE_HEADS, group_size, HEAD_SIZE), jnp.float32), -6.0, 6.0)
    return (queries.reshape(LAYER_COUNT, TOKEN_COUNT, HEADS * HEAD_SIZE), key_draw.reshape(LAYER_COUNT, TOKEN_COUNT, KEY_VALUE_HEADS * HEAD_SIZE))


def draw_encoded_query_rows(key, part):
    return attention_pair(key)[0].astype(jnp.bfloat16)


def draw_encoded_key_rows(key, part):
    return attention_pair(key)[1].astype(jnp.bfloat16)


def set_ends(array, key, low, high):
    shape = array.shape
    spot = [jax.random.randint(jax.random.fold_in(key, axis), (), 0, shape[axis]) for axis in range(len(shape))]
    array = array.at[tuple(spot)].set(low)
    longest = shape.index(max(shape))
    spot[longest] = (spot[longest] + 1) % shape[longest]
    return array.at[tuple(spot)].set(high)


def level_of(key, dims, shards, low, high):
    factor_of = 1.0
    for axis_at, shards_of in shards:
        steps = jax.random.uniform(jax.random.fold_in(jax.random.fold_in(key, 6), axis_at), (shards_of,), jnp.float32, low / len(shards), high / len(shards))
        factor_of = factor_of * jnp.repeat(jnp.exp(steps), dims[axis_at] // shards_of).reshape((-1,) + (1,) * (len(dims) - 1 - axis_at))
    return factor_of


def length_profile(amount, total, reach, skew):
    weights = [(1 << 20) // math.isqrt(standing ** skew) + 1 for standing in range(2, amount + 1)]
    surplus, holding = total - reach - (amount - 1), [1] * (amount - 1)
    while surplus > 0:
        free = [i for i in range(amount - 1) if holding[i] < reach]
        pool, remaining = sum([weights[i] for i in free]), surplus
        for i in free:
            addition = min(reach - holding[i], max(1, remaining * weights[i] // pool), surplus)
            holding[i] = holding[i] + addition
            surplus = surplus - addition
    return np.array([reach] + holding)


def uneven_parts(rng, amount, total, limit, slope):
    if amount == 2:
        one = jax.random.randint(rng, (), max(1, total - limit), min(limit, total - 1) + 1)
        return jnp.stack([one, total - one])
    tallies = jnp.asarray(length_profile(amount, total, limit, slope), jnp.int32)
    twos = (amount - 1) // 2
    source_of, sink = tallies[1:1 + 2 * twos:2], tallies[2:2 + 2 * twos:2]
    margin = jnp.minimum(source_of - 1, limit - sink)
    moved = jax.random.randint(jax.random.fold_in(rng, 1), (twos,), 0, 1 << 20) % (margin + 1)
    tallies = tallies.at[1:1 + 2 * twos:2].set(source_of - moved).at[2:2 + 2 * twos:2].set(sink + moved)
    return tallies[jax.random.permutation(jax.random.fold_in(rng, 2), amount)]


def normal_values(rng, extent, deviation, bound, cuts=(), kind=jnp.bfloat16):
    array = deviation * jax.random.normal(rng, extent, jnp.float32)
    if cuts:
        array = array * level_of(rng, extent, cuts, -0.22, 0.18)
    return jnp.clip(array, -bound, bound).astype(kind)


def setup_inputs(seed: int = 0, part: int = 0) -> dict:
    arg_keys = jax.random.split(jax.random.key(seed), 12)
    own_keys = jax.random.split(jax.random.fold_in(arg_keys[11], part), 12)
    return {
        "layer_input_rows": draw_layer_input_rows(jax.random.fold_in(jax.random.fold_in(arg_keys[11], part), 71), part),
        "encoded_query_rows": draw_encoded_query_rows(jax.random.fold_in(jax.random.fold_in(arg_keys[11], part), 71), part),
        "encoded_key_rows": draw_encoded_key_rows(jax.random.fold_in(jax.random.fold_in(arg_keys[11], part), 71), part),
        "layer_norm_gain": jnp.clip(1.0 + 0.15 * jax.random.normal(arg_keys[3], (LAYER_COUNT, MODEL_WIDTH), jnp.float32), 0.25, 1.75),
        "base_value_matrix": normal_values(arg_keys[4], (LAYER_COUNT, MODEL_WIDTH, KEY_VALUE_HEADS * HEAD_SIZE), MODEL_WIDTH ** -0.5, 0.078125, ((0, 2), (1, 8))),
        "adapter_down_panels": normal_values(arg_keys[5], (LAYER_COUNT, SLOT_COUNT, MODEL_WIDTH, MAX_RANK), MODEL_WIDTH ** -0.5, 0.078125, ((0, 2), (1, 4), (2, 2))),
        "adapter_up_panels": normal_values(arg_keys[6], (LAYER_COUNT, SLOT_COUNT, MAX_RANK, KEY_VALUE_HEADS * HEAD_SIZE), MAX_RANK ** -0.5, 0.75, ((0, 2), (1, 4), (3, 2))),
        "request_token_lengths": uneven_parts(own_keys[7], REQUESTS, TOKEN_COUNT, TOKEN_COUNT // 2, 2).astype(jnp.int32),
        "adapter_per_request": set_ends(jax.random.randint(own_keys[8], (REQUESTS,), 0, SLOT_COUNT), jax.random.fold_in(own_keys[8], 1), 0, SLOT_COUNT - 1).astype(jnp.int32),
        "rank_per_adapter": set_ends(jax.random.randint(arg_keys[9], (SLOT_COUNT,), MAX_RANK // 4, MAX_RANK + 1), jax.random.fold_in(arg_keys[9], 1), MAX_RANK // 4, MAX_RANK).astype(jnp.int32),
        "slot_per_adapter": jax.random.permutation(arg_keys[10], SLOT_COUNT).astype(jnp.int32),
    }


query_scale = 168.0 ** (-0.5)
adapter_strength = 32.0
norm_eps = 1e-06

def requests_of(positions, request_token_lengths):
    request_ends = jnp.cumsum(request_token_lengths).astype(jnp.int32)
    return lax.optimization_barrier(jnp.sum((positions[:, None] >= request_ends[None, :]).astype(jnp.int32), axis=1))

def attend(queries, key_block_all, value_block_all, request_lookup):
    group_size = HEADS // KEY_VALUE_HEADS
    key_width = key_block_all.shape[1]
    keys_padded = jnp.concatenate([jnp.zeros((WINDOW, key_width), key_block_all.dtype), key_block_all], axis=0)
    values_padded = jnp.concatenate([jnp.zeros((WINDOW, key_width), value_block_all.dtype), value_block_all], axis=0)
    request_padded = jnp.concatenate([jnp.full((WINDOW,), -1, jnp.int32), request_lookup.astype(jnp.int32)], axis=0)
    key_span = WINDOW + TOK_DEV

    def one_block(block_index):
        first_row = (block_index * TOK_DEV).astype(jnp.int32)
        query_block = lax.dynamic_slice_in_dim(queries, first_row, TOK_DEV, 0).astype(jnp.float32)
        query_block = query_block.reshape(TOK_DEV, KEY_VALUE_HEADS, group_size, HEAD_SIZE)
        key_block = lax.dynamic_slice_in_dim(keys_padded, first_row, key_span, 0).astype(jnp.float32)
        key_block = key_block.reshape(key_span, KEY_VALUE_HEADS, HEAD_SIZE)
        value_block = lax.dynamic_slice_in_dim(values_padded, first_row, key_span, 0).astype(jnp.float32)
        value_block = value_block.reshape(key_span, KEY_VALUE_HEADS, HEAD_SIZE)
        own_requests = lax.dynamic_slice_in_dim(request_lookup.astype(jnp.int32), first_row, TOK_DEV, 0)
        seen_requests = lax.dynamic_slice_in_dim(request_padded, first_row, key_span, 0)
        query_place = first_row + jnp.arange(TOK_DEV, dtype=jnp.int32)
        key_place = first_row - WINDOW + jnp.arange(key_span, dtype=jnp.int32)
        live_mask = (key_place[None, :] <= query_place[:, None]) & (key_place[None, :] > query_place[:, None] - WINDOW)
        live_mask = live_mask & (seen_requests[None, :] == own_requests[:, None])
        scores = jnp.einsum('tgcd,jgd->gctj', query_block, key_block) * query_scale
        scores = jnp.where(live_mask[None, None], scores, jnp.float32(-1e+30))
        row_max = lax.optimization_barrier(jnp.max(scores, axis=-1, keepdims=True))
        weights = jnp.exp(scores - row_max)
        row_total = lax.optimization_barrier(jnp.sum(weights, axis=-1, keepdims=True))
        softmax_rows = (weights / row_total).astype(jnp.bfloat16)
        mixed_heads = jnp.einsum('gctj,jgd->tgcd', softmax_rows.astype(jnp.float32), value_block)
        return mixed_heads.astype(jnp.bfloat16).reshape(TOK_DEV, HEADS * HEAD_SIZE)
    blocks = lax.map(one_block, jnp.arange(TOKEN_COUNT // TOK_DEV, dtype=jnp.int32))
    return blocks.reshape(TOKEN_COUNT, HEADS * HEAD_SIZE)

def reference(layer_input_rows, encoded_query_rows, encoded_key_rows, layer_norm_gain, base_value_matrix, adapter_down_panels, adapter_up_panels, request_token_lengths, adapter_per_request, rank_per_adapter, slot_per_adapter):
    positions = jnp.arange(TOKEN_COUNT, dtype=jnp.int32)
    request_lookup = requests_of(positions, request_token_lengths)
    columns = jnp.arange(MAX_RANK, dtype=jnp.int32)
    outputs = []
    for layer_number in range(LAYER_COUNT):
        wide_rows = layer_input_rows[layer_number].astype(jnp.float32)
        normalized_rows = wide_rows * lax.rsqrt(lax.optimization_barrier(jnp.mean(wide_rows * wide_rows, axis=1, keepdims=True)) + norm_eps)
        normalized_rows = (normalized_rows * layer_norm_gain[layer_number][None, :]).astype(jnp.bfloat16)
        value_base_rows = jnp.dot(normalized_rows, base_value_matrix[layer_number], preferred_element_type=jnp.float32)
        reduced_rows = jnp.zeros((TOKEN_COUNT, MAX_RANK), jnp.float32)
        for request_number in range(REQUESTS):
            adapter_id = adapter_per_request[request_number]
            slot_number = slot_per_adapter[adapter_id]
            rank_value = rank_per_adapter[adapter_id]
            keep_mask = (request_lookup == request_number)[:, None] & (columns < rank_value)[None, :]
            matrix_product = jnp.dot(normalized_rows, adapter_down_panels[layer_number, slot_number], preferred_element_type=jnp.float32)
            reduced_rows = reduced_rows + jnp.where(keep_mask, matrix_product, jnp.float32(0.0))
        reduced_rows = reduced_rows.astype(jnp.bfloat16)
        adapter_value = jnp.zeros((TOKEN_COUNT, KEY_VALUE_HEADS * HEAD_SIZE), jnp.float32)
        for request_number in range(REQUESTS):
            adapter_id = adapter_per_request[request_number]
            slot_number = slot_per_adapter[adapter_id]
            adapter_scale = adapter_strength / rank_per_adapter[adapter_id].astype(jnp.float32)
            raised_rows = jnp.dot(reduced_rows, adapter_up_panels[layer_number, slot_number], preferred_element_type=jnp.float32)
            adapter_value = adapter_value + jnp.where((request_lookup == request_number)[:, None], adapter_scale * raised_rows, jnp.float32(0.0))
        value_output_rows = (value_base_rows + adapter_value).astype(jnp.bfloat16)
        outputs.append(attend(encoded_query_rows[layer_number], encoded_key_rows[layer_number], value_output_rows, request_lookup))
    return jnp.stack(outputs)
```

```python
import functools

import jax
import jax.numpy as jnp
from jax import lax
from jax.experimental import pallas as pl
from jax.experimental.pallas import tpu as pltpu
from jax.sharding import PartitionSpec as P

WINDOW = 1024
HEADS = 16
KEY_VALUE_HEADS = 8
HEAD_SIZE = 128


query_scale = 168.0 ** (-0.5)
adapter_strength = 32.0
norm_eps = 1e-06


def broadcast(x, axis, root):
    mine = lax.axis_index(axis) == root
    return lax.psum(jnp.where(mine, x, jnp.zeros_like(x)), axis)


def from_behind(value, axis, steps):
    count = lax.axis_size(axis)
    first, last = (max(0, -steps), min(count, count - steps))
    return lax.ppermute(value, axis, [(source, source + steps) for source in range(first, last)])


def per_device(
    layer_input_rows,
    encoded_query_rows,
    encoded_key_rows,
    layer_norm_gain,
    base_value_matrix,
    adapter_down_panels,
    adapter_up_panels,
    request_token_lengths,
    adapter_per_request,
    rank_per_adapter,
    slot_per_adapter,
):
    hidden = layer_input_rows[0]
    row_count = hidden.shape[0]
    seq_now = lax.axis_index("seq")
    owner_now = lax.axis_index("owner")
    reach_count = min(WINDOW // row_count, lax.axis_size("seq") - 1)
    requests = request_token_lengths.shape[0]
    library = slot_per_adapter.shape[0]
    slots_here = adapter_down_panels.shape[1]
    rows_halved = adapter_down_panels.shape[2]
    rank_span_width = adapter_down_panels.shape[3]
    key_value_halved = adapter_up_panels.shape[3]
    group_size = HEADS // KEY_VALUE_HEADS
    request_ends = jnp.cumsum(request_token_lengths)
    position = seq_now * row_count + jnp.arange(row_count, dtype=jnp.int32)
    context = seq_now * row_count + jnp.arange(-reach_count * row_count, row_count, dtype=jnp.int32)
    request_lookup = jnp.sum((position[:, None] >= request_ends[None, :]).astype(jnp.int32), axis=1)
    request_ctx = jnp.sum((context[:, None] >= request_ends[None, :]).astype(jnp.int32), axis=1)
    live_mask = (context[None, :] <= position[:, None]) & (
        context[None, :] > position[:, None] - WINDOW
    )
    live_mask = (
        live_mask & (context[None, :] >= 0) & (request_ctx[None, :] == request_lookup[:, None])
    )
    choose = adapter_per_request[:, None] == jnp.arange(library, dtype=jnp.int32)[None, :]
    slot_of = jnp.sum(jnp.where(choose, slot_per_adapter[None, :], 0), axis=1)
    rank_lookup = jnp.sum(jnp.where(choose, rank_per_adapter[None, :], 0), axis=1)
    scale_lookup = adapter_strength / rank_lookup.astype(jnp.float32)
    in_request = request_lookup[:, None] == jnp.arange(requests, dtype=jnp.int32)[None, :]
    column_live = jnp.arange(rank_span_width, dtype=jnp.int32)[None, :] < rank_lookup[:, None]
    row_gain_weight = jnp.where(in_request, scale_lookup[None, :], jnp.float32(0.0))
    down_panel_here = adapter_down_panels[0]
    up_panel_here = adapter_up_panels[0]
    queries = encoded_query_rows[0]
    keys_own = encoded_key_rows[0]
    key_heads = keys_own.shape[1] // HEAD_SIZE
    wide_rows = hidden.astype(jnp.float32)
    normalized_rows = wide_rows * lax.rsqrt(
        jnp.mean(wide_rows * wide_rows, axis=1, keepdims=True) + norm_eps
    )
    normalized_rows = (normalized_rows * layer_norm_gain[0][None, :]).astype(jnp.bfloat16)
    normed_half = lax.dynamic_slice_in_dim(normalized_rows, owner_now * rows_halved, rows_halved, 1)
    full_value = jnp.dot(
        normalized_rows,
        lax.all_gather(base_value_matrix[0], ("seq", "owner"), axis=0, tiled=True),
        preferred_element_type=jnp.float32,
    )
    value_base_rows = lax.dynamic_slice_in_dim(
        full_value, owner_now * key_value_halved, key_value_halved, 1
    )

    def fetch_one(reduced_rows, request_index):
        owner_slot = slot_of[request_index]
        holder = owner_slot // slots_here
        local_slot = owner_slot % slots_here
        down_local = lax.dynamic_slice_in_dim(down_panel_here, local_slot, 1, 0)
        up_local = lax.dynamic_slice_in_dim(up_panel_here, local_slot, 1, 0)
        down_piece, up_piece = (
            broadcast(down_local, "seq", holder),
            broadcast(up_local, "seq", holder),
        )
        keep_mask = in_request[:, request_index][:, None] & column_live[request_index][None, :]
        matrix_product = jnp.dot(normed_half, down_piece[0], preferred_element_type=jnp.float32)
        return (reduced_rows + jnp.where(keep_mask, matrix_product, jnp.float32(0.0)), up_piece[0])

    start_low = jnp.zeros((row_count, rank_span_width), jnp.float32)
    reduced_rows, panels_up = lax.scan(fetch_one, start_low, jnp.arange(requests, dtype=jnp.int32))
    reduced_rows = lax.psum(reduced_rows, "owner").astype(jnp.bfloat16)
    raised_rows = jnp.einsum(
        "tr,qrk->qtk", reduced_rows, panels_up, preferred_element_type=jnp.float32
    )
    adapter_value = jnp.sum(row_gain_weight.T[:, :, None] * raised_rows, axis=0)
    value_output_rows = (value_base_rows + adapter_value).astype(jnp.bfloat16)
    key_parts = []
    value_parts = []
    for shift_by in range(reach_count, 0, -1):
        key_piece, value_piece = from_behind((keys_own, value_output_rows), "seq", shift_by)
        key_parts.append(key_piece)
        value_parts.append(value_piece)
    keys_all = jnp.concatenate(key_parts + [keys_own], axis=0)
    values_all = jnp.concatenate(value_parts + [value_output_rows], axis=0)
    query_view = queries.reshape(row_count, key_heads, group_size, HEAD_SIZE)
    key_view = keys_all.reshape(-1, key_heads, HEAD_SIZE)
    value_view = values_all.reshape(-1, key_heads, HEAD_SIZE)
    head_outputs = []
    for head_index in range(key_heads):
        query_head = query_view[:, head_index]
        scores = (
            jnp.einsum(
                "tcd,jd->ctj",
                query_head,
                key_view[:, head_index],
                preferred_element_type=jnp.float32,
            )
            * query_scale
        )
        scores = jnp.where(live_mask[None], scores, jnp.float32(-1e30))
        row_max = jnp.max(scores, axis=-1, keepdims=True)
        weights = jnp.exp(scores - row_max)
        row_total = jnp.sum(weights, axis=-1, keepdims=True)
        softmax_rows = (weights / row_total).astype(jnp.bfloat16)
        mixed = jnp.einsum(
            "ctj,jd->tcd",
            softmax_rows,
            value_view[:, head_index],
            preferred_element_type=jnp.float32,
        )
        head_outputs.append(mixed.astype(jnp.bfloat16).reshape(row_count, group_size * HEAD_SIZE))
    result = jnp.concatenate(head_outputs, axis=1)
    return result[None]


LANES = 128
CHUNKS = 4


def kernel(
    n,
    lengths,
    adapters,
    ranks,
    slots,
    x_hbm,
    q_hbm,
    k_hbm,
    gain_hbm,
    w_hbm,
    down_hbm,
    up_hbm,
    out_hbm,
    xr,
    gain,
    xb,
    wbuf,
    dn,
    hdn,
    ucat,
    qb,
    kb,
    pown,
    pbuf,
    prec,
    sbuf,
    srec,
    vbuf,
    vall,
    prob,
    ob,
    loc_sem,
    xi_send,
    xo_send,
    x_recv,
    ex_send,
    ex_recv,
    ph_send,
    ph_recv,
    uh_send,
    uh_recv,
    k_send,
    k_recv,
    p_send,
    p_recv,
    s_send,
    s_recv,
    v_send,
    vc_send,
    v_recv,
):
    f32, bf16 = jnp.float32, jnp.bfloat16
    s = lax.axis_index("seq")
    o = lax.axis_index("owner")
    g = lax.axis_index("groups")
    tok, width = x_hbm.shape[1], x_hbm.shape[2]
    part = tok // 2
    half = width // 2
    win, vcols2 = wbuf.shape
    vcols = vcols2 // 2
    slab = w_hbm.shape[1]
    panels, rank_width = dn.shape[0], dn.shape[1]
    low_width = panels * rank_width
    chip_rows = width // n
    requests = lengths.shape[0]
    total = n * tok
    group = HEADS // KEY_VALUE_HEADS
    wide = -(-half // (2 * LANES)) * LANES
    sizes = (wide, half - wide)

    low_side = s < n // 2
    end = (s == 0) | (s == n - 1)
    inner = jnp.logical_not(end)
    near_end = jnp.where(low_side, 0, n - 1)
    near_inner = jnp.where(low_side, 1, n - 2)
    far_inner = n - 1 - near_inner
    far_end = n - 1 - near_end
    inward = low_side.astype(jnp.int32)
    outward = 1 - inward
    other = 1 - o
    host_core = inward

    def peer(seq, owner=None, groups=None):
        return {
            "seq": seq,
            "owner": o if owner is None else owner,
            "groups": g if groups is None else groups,
        }

    def remote(src, dst, send, recv, device):
        return pltpu.make_async_remote_copy(
            src_ref=src,
            dst_ref=dst,
            send_sem=send,
            recv_sem=recv,
            device_id=device,
            device_id_type=pl.DeviceIdType.MESH,
        )

    barrier = pltpu.get_barrier_semaphore()

    def greet(device):
        pl.semaphore_signal(barrier, inc=1, device_id=device, device_id_type=pl.DeviceIdType.MESH)

    greet(peer(s, other))

    @pl.when(end)
    def _():
        greet(peer(near_inner))
        greet(peer(near_inner, other))

    @pl.when(inner)
    def _():
        greet(peer(near_end))
        greet(peer(near_end, other))
        greet(peer(far_inner))
        greet(peer(s, o, 1 - g))

    begin = s * chip_rows
    first, pad = 0, 0
    for step in range(n):
        a = min(step * chip_rows // LANES * LANES, width - win)
        first = jnp.where(s == step, a, first)
        pad = jnp.where(s == step, step * chip_rows - a, pad)
    first = pl.multiple_of(first, LANES)
    x_window = pl.ds(first, win)
    w_at = pl.ds(pl.multiple_of(pad + o * slab, 16), slab)
    my_half = pl.ds(pl.multiple_of(o * half, LANES), half)
    my_cols = pl.ds(pl.multiple_of(o * vcols, LANES), vcols)
    other_cols = pl.ds(pl.multiple_of(other * vcols, LANES), vcols)
    kept_half = pl.ds(pl.multiple_of(outward * half, LANES), half)
    host_half = pl.ds(pl.multiple_of(inward * half, LANES), half)
    my_rows = pl.ds(pl.multiple_of(o * part, 16), part)

    local = [
        pltpu.make_async_copy(x_hbm.at[0, my_rows, :], xr, loc_sem.at[0]),
        pltpu.make_async_copy(gain_hbm, gain, loc_sem.at[1]),
        pltpu.make_async_copy(w_hbm.at[0], wbuf.at[w_at], loc_sem.at[2]),
        pltpu.make_async_copy(down_hbm.at[0], dn.at[:, :, my_half], loc_sem.at[3]),
        pltpu.make_async_copy(up_hbm.at[0], ucat.at[pl.ds(0, panels), :, my_cols], loc_sem.at[4]),
        pltpu.make_async_copy(q_hbm.at[0], qb, loc_sem.at[5]),
        pltpu.make_async_copy(k_hbm.at[0], kb.at[s], loc_sem.at[6]),
    ]
    for copy in local:
        copy.start()

    for step in range(n):
        b = step * chip_rows - min(step * chip_rows // LANES * LANES, width - win)

        @pl.when(s == step)
        def _():
            if b:
                wbuf[0:b, :] = jnp.zeros((b, vcols2), bf16)
            rest = win - b - chip_rows
            if rest:
                wbuf[win - rest : win, :] = jnp.zeros((rest, vcols2), bf16)

    for t in range(1, n):

        @pl.when(t > s)
        def _():
            kb[t] = jnp.zeros(kb.shape[1:], bf16)
            vall[t] = jnp.zeros(vall.shape[1:], bf16)

    local[0].wait()
    local[1].wait()
    rows = xr[...].astype(f32)
    inv = lax.rsqrt(jnp.mean(rows * rows, axis=1, keepdims=True) + norm_eps)
    xb[s] = (xr[...].astype(f32) * inv * gain[...]).astype(bf16)

    pl.semaphore_wait(barrier, jnp.where(end, 3, 5))

    def chunk(q, up):
        first_half = q < CHUNKS // 2
        at = (up if first_half else 1 - up) * half + (q % 2) * wide
        return pl.ds(pl.multiple_of(at, LANES), sizes[q % 2])

    def x_copy(t, q, up, sem, device):
        at = xb.at[t, :, chunk(q, up)]
        return remote(at, at, sem, x_recv.at[t, q], device)

    def x_in(which, t, q):
        return x_copy(t, q, inward, xi_send.at[which, q], peer(jnp.where(end, near_inner, far_inner)))

    def x_out(which, t, q):
        return x_copy(t, q, outward, xo_send.at[which, q], peer(near_end))

    def x_arrived(t, q, up):
        x_copy(t, q, up, xi_send.at[0, q], peer(s, other)).wait_recv()

    w_copy = remote(w_hbm.at[0], wbuf.at[w_at], ex_send.at[0], ex_recv.at[0], peer(s, other))
    dn_copy = remote(down_hbm.at[0], dn.at[:, :, my_half], ex_send.at[1], ex_recv.at[1], peer(s, other))
    up_copy = remote(
        up_hbm.at[0], ucat.at[pl.ds(0, panels), :, my_cols], ex_send.at[2], ex_recv.at[2], peer(s, other)
    )

    per_group = panels // 2
    mine = pl.ds(g * per_group, per_group)
    theirs = pl.ds((1 - g) * per_group, per_group)
    my_up = pl.ds(panels + g * per_group, per_group)
    their_up = pl.ds(panels + (1 - g) * per_group, per_group)
    ph_z = remote(down_hbm.at[0, mine], hdn.at[mine], ph_send.at[0], ph_recv.at[0], peer(near_inner))
    ph_y = remote(hdn.at[mine], hdn.at[mine], ph_send.at[1], ph_recv.at[1], peer(s, o, 1 - g))
    ph_c = [
        remote(hdn.at[mine], hdn.at[mine], ph_send.at[2], ph_recv.at[2], peer(s, other)),
        remote(hdn.at[theirs], hdn.at[theirs], ph_send.at[3], ph_recv.at[3], peer(s, other)),
    ]

    def up_ref(which, cols):
        return ucat.at[which, :, cols]

    uh_z = remote(up_hbm.at[0, mine], up_ref(my_up, my_cols), uh_send.at[0], uh_recv.at[0], peer(near_inner))
    uh_y = remote(
        up_ref(my_up, my_cols), up_ref(my_up, my_cols), uh_send.at[1], uh_recv.at[1], peer(s, o, 1 - g)
    )
    uh_y_in = remote(
        up_ref(their_up, my_cols), up_ref(their_up, my_cols), uh_send.at[1], uh_recv.at[1], peer(s, o, 1 - g)
    )
    ph_y_in = remote(hdn.at[theirs], hdn.at[theirs], ph_send.at[1], ph_recv.at[1], peer(s, o, 1 - g))
    uh_c = [
        remote(up_ref(which, my_cols), up_ref(which, my_cols), uh_send.at[2 + at], uh_recv.at[2 + at], peer(s, other))
        for at, which in enumerate((my_up, their_up))
    ]
    uh_c_in = [
        remote(up_ref(which, other_cols), up_ref(which, other_cols), uh_send.at[2 + at], uh_recv.at[2 + at], peer(s, other))
        for at, which in enumerate((my_up, their_up))
    ]

    def k_up(t):
        return remote(kb.at[t], kb.at[t], k_send.at[t], k_recv.at[t], peer(jnp.minimum(s + 1, n - 1)))

    ends, slot_of, rank_of = [], [], []
    run = jnp.int32(0)
    for r in range(requests):
        run = run + lengths[r]
        ends.append(run)
        adapter = adapters[r]
        slot_of.append(slots[adapter])
        rank_of.append(ranks[adapter])

    def request_at(position):
        found = jnp.zeros(position.shape, jnp.int32)
        for r in range(requests):
            found = found + (position >= ends[r]).astype(jnp.int32)
        return found

    def token_facts(t):
        req = request_at(t * tok + o * part + lax.broadcasted_iota(jnp.int32, (part, 1), 0))
        slot_t = jnp.zeros((part, 1), jnp.int32)
        rank_t = jnp.ones((part, 1), jnp.int32)
        for r in range(requests):
            slot_t = jnp.where(req == r, slot_of[r], slot_t)
            rank_t = jnp.where(req == r, rank_of[r], rank_t)
        return slot_t, rank_t

    def masked(low, t, chip):
        slot_t, rank_t = token_facts(t)
        column = lax.broadcasted_iota(jnp.int32, (part, low_width), 1)
        start = (slot_t - chip * panels) * rank_width
        return jnp.where((column >= start) & (column < start + rank_t), low, 0.0).astype(bf16), rank_t

    def contract(a, b):
        return lax.dot_general(a, b, (((1,), (1,)), ((), ())), preferred_element_type=f32)

    def raise_by(low, rank_t, at):
        up = ucat[pl.ds(at, panels)].reshape(low_width, vcols2)
        raised = jnp.dot(low, up, preferred_element_type=f32)
        return raised * (adapter_strength / rank_t.astype(f32))

    def base_of(t):
        return jnp.dot(xb[t, :, x_window], wbuf[...], preferred_element_type=f32)

    def inner_partial(t):
        low, rank_t = masked(contract(xb[t], dn[...].reshape(low_width, width)), t, s)
        pown[t] = base_of(t) + raise_by(low, rank_t, 0)

    def hosted_partial(t):
        low, rank_t = masked(contract(xb[t, :, host_half], hdn[...].reshape(low_width, half)), t, near_end)
        pown[t] = pown[t] + raise_by(low, rank_t, panels)

    def end_partial(t):
        panel = dn[:, :, kept_half].reshape(low_width, half)
        low, rank_t = masked(contract(xb[t, :, kept_half], panel), t, s)
        pbuf[t] = (base_of(t) + raise_by(low, rank_t, 0)).astype(bf16)

    def p_copy(t):
        return remote(pbuf.at[t], prec.at[t], p_send.at[t], p_recv.at[t], peer(near_inner))

    def s_copy(t):
        return remote(sbuf.at[t], srec.at[t], s_send.at[t], s_recv.at[t], peer(far_inner))

    def v_out(t, core):
        cols = pl.ds(pl.multiple_of(core * vcols, LANES), vcols)
        return remote(
            vbuf.at[t, :, cols], vall.at[t, o], v_send.at[t, core], v_recv.at[t, o], peer(near_end, core)
        )

    def v_core(t):
        return remote(vbuf.at[t, :, other_cols], vall.at[t, o], vc_send.at[t], v_recv.at[t, o], peer(s, other))

    def v_arrived(t, core):
        remote(vall.at[t, core], vall.at[t, core], vc_send.at[t], v_recv.at[t, core], peer(s, other)).wait_recv()

    def weights_ready():
        for at in (2, 3, 4):
            local[at].wait()
        w_copy_in = remote(w_hbm.at[0], wbuf.at[w_at], ex_send.at[0], ex_recv.at[0], peer(s, other))
        w_copy_in.wait_recv()
        up_copy.wait_recv()

    def scores_of():
        keys = kb[...].reshape(total, vcols)
        key_at = lax.broadcasted_iota(jnp.int32, (1, total), 1)
        query_at = s * tok + lax.broadcasted_iota(jnp.int32, (tok, 1), 0)
        live = (key_at <= query_at) & (key_at > query_at - WINDOW)
        live = live & (request_at(query_at) == request_at(key_at))
        for h in range(qb.shape[1] // HEAD_SIZE):
            kv = h // group
            scores = (
                contract(qb[:, h * HEAD_SIZE : (h + 1) * HEAD_SIZE], keys[:, kv * HEAD_SIZE : (kv + 1) * HEAD_SIZE])
                * query_scale
            )
            scores = jnp.where(live, scores, -1e30)
            weights = jnp.exp(scores - jnp.max(scores, axis=1, keepdims=True))
            soft = weights / jnp.sum(weights, axis=1, keepdims=True)
            prob[h] = soft.astype(bf16)

    @pl.when(end)
    def _():
        @pl.when(o == host_core)
        def _():
            ph_z.start()

        for q in range(CHUNKS):
            x_in(0, s, q).start()
        w_copy.start()
        up_copy.start()

        @pl.when(o != host_core)
        def _():
            dn_copy.start()

        uh_z.start()
        local[6].wait()

        @pl.when(s == 0)
        def _():
            k_up(s).start()

        weights_ready()

        @pl.when(o == host_core)
        def _():
            dn_kept = dn.at[:, :, kept_half]
            remote(dn_kept, dn_kept, ex_send.at[1], ex_recv.at[1], peer(s, other)).wait_recv()

        end_partial(s)
        p_copy(s).start()
        for t in (near_inner, far_inner, far_end):
            for q in range(CHUNKS // 2):
                x_arrived(t, q, outward)
            end_partial(t)
            p_copy(t).start()

        local[5].wait()

        @pl.when(s == n - 1)
        def _():
            for t in range(n - 1):
                k_up(t).wait_recv()

        scores_of()

        for t in range(n):

            @pl.when((t == 0) | (s == n - 1))
            def _():
                v_arrived(t, 0)
                v_arrived(t, 1)

    def add_end(t):
        p_copy(t).wait_recv()
        total_here = pown[t] + prec[t].astype(f32)
        pown[t] = total_here
        sbuf[t] = total_here.astype(bf16)

        @pl.when(low_side | (t < n // 2))
        def _():
            s_copy(t).start()

    def finish(t):
        s_copy(t).wait_recv()
        value = (pown[t] + srec[t].astype(f32)).astype(bf16)
        vbuf[t] = value

        @pl.when((t == 0) | (s == n - 2))
        def _():
            v_out(t, 0).start()
            v_out(t, 1).start()

        @pl.when(t <= s)
        def _():
            v_core(t).start()
            vall[t, o] = vbuf[t, :, my_cols]

    @pl.when(inner)
    def _():
        for q in range(CHUNKS):
            x_in(0, s, q).start()
            if q < CHUNKS // 2:
                x_out(0, s, q).start()
        w_copy.start()
        dn_copy.start()
        up_copy.start()
        weights_ready()
        dn_other = dn.at[:, :, pl.ds(pl.multiple_of(other * half, LANES), half)]
        remote(dn_other, dn_other, ex_send.at[1], ex_recv.at[1], peer(s, other)).wait_recv()
        inner_partial(s)
        for q in range(CHUNKS):
            x_arrived(far_inner, q, outward)
            if q < CHUNKS // 2:
                x_out(1, far_inner, q).start()
            x_arrived(near_end, q, inward)
            x_in(1, near_end, q).start()
            if q == 1:

                @pl.when(o == host_core)
                def _():
                    ph_z.wait_recv()
                    ph_y.start()
                    ph_c[0].start()

        inner_partial(near_end)
        uh_z.wait_recv()
        uh_y.start()
        uh_c[0].start()
        local[6].wait()

        @pl.when(s == 1)
        def _():
            k_up(0).wait_recv()
            k_up(0).start()

        k_up(s).start()
        x_arrived(far_end, 0, outward)
        x_out(2, far_end, 0).start()
        inner_partial(far_inner)
        x_arrived(far_end, 1, outward)
        x_out(2, far_end, 1).start()
        uh_y_in.wait_recv()
        uh_c[1].start()

        @pl.when(o == host_core)
        def _():
            ph_y_in.wait_recv()
            ph_c[1].start()

        @pl.when(o != host_core)
        def _():
            ph_c[0].wait_recv()
            ph_c[1].wait_recv()

        uh_c_in[0].wait_recv()
        uh_c_in[1].wait_recv()
        for t in (near_end, s, far_inner):
            hosted_partial(t)
            add_end(t)
        for q in range(2, CHUNKS):
            x_arrived(far_end, q, outward)
        inner_partial(far_end)
        hosted_partial(far_end)
        add_end(far_end)
        local[5].wait()

        @pl.when(s == n - 2)
        def _():
            for t in range(n - 2):
                k_up(t).wait_recv()
                k_up(t).start()

        scores_of()

        @pl.when(s == 1)
        def _():
            finish(1)
            finish(0)

        @pl.when(s == n - 2)
        def _():
            for t in range(n):
                finish(t)

        for t in range(n - 1):

            @pl.when(t <= s)
            def _():
                v_arrived(t, other)

    values = vall[...].reshape(total, vcols)
    for h in range(qb.shape[1] // HEAD_SIZE):
        kv = h // group
        ob[:, h * HEAD_SIZE : (h + 1) * HEAD_SIZE] = jnp.dot(
            prob[h], values[:, kv * HEAD_SIZE : (kv + 1) * HEAD_SIZE], preferred_element_type=f32
        ).astype(bf16)
    result = pltpu.make_async_copy(ob, out_hbm.at[0], loc_sem.at[7])
    result.start()

    w_copy.wait_send()
    up_copy.wait_send()

    @pl.when(inner | (o != host_core))
    def _():
        dn_copy.wait_send()

    for q in range(CHUNKS):
        x_in(0, s, q).wait_send()

    @pl.when(s < n - 1)
    def _():
        k_up(s).wait_send()

    @pl.when(end)
    def _():
        @pl.when(o == host_core)
        def _():
            ph_z.wait_send()

        uh_z.wait_send()
        for t in range(n):
            p_copy(t).wait_send()

    @pl.when(inner)
    def _():
        for q in range(CHUNKS):
            x_in(1, near_end, q).wait_send()
        for which in range(3):
            for q in range(CHUNKS // 2):
                x_out(which, s, q).wait_send()

        @pl.when(o == host_core)
        def _():
            ph_y.wait_send()
            ph_c[0].wait_send()
            ph_c[1].wait_send()

        uh_y.wait_send()
        uh_c[0].wait_send()
        uh_c[1].wait_send()
        for t in range(n):

            @pl.when(t < s)
            def _():
                k_up(t).wait_send()

            @pl.when(low_side | (t < n // 2))
            def _():
                s_copy(t).wait_send()

            @pl.when((t == 0) | (s == n - 2))
            def _():
                v_out(t, 0).wait_send()
                v_out(t, 1).wait_send()

            @pl.when(t <= s)
            def _():
                v_core(t).wait_send()

    result.wait()


def fused(
    n,
    layer_input_rows,
    encoded_query_rows,
    encoded_key_rows,
    layer_norm_gain,
    base_value_matrix,
    adapter_down_panels,
    adapter_up_panels,
    request_token_lengths,
    adapter_per_request,
    rank_per_adapter,
    slot_per_adapter,
):
    f32, bf16 = jnp.float32, jnp.bfloat16
    tok, width = layer_input_rows.shape[1:]
    part, half = tok // 2, width // 2
    panels, _, rank_width = adapter_down_panels.shape[1:]
    vcols = adapter_up_panels.shape[3]
    qcols = encoded_query_rows.shape[2]
    chip_rows = width // n
    pads = [i * chip_rows % LANES for i in range(n)]
    win = -(-(max(pads) + chip_rows) // LANES) * LANES
    total = n * tok
    dma = pltpu.SemaphoreType.DMA
    any_spec = pl.BlockSpec(memory_space=pl.ANY)
    smem = pl.BlockSpec(memory_space=pltpu.SMEM)
    return pl.pallas_call(
        functools.partial(kernel, n),
        out_shape=jax.ShapeDtypeStruct(encoded_query_rows.shape, bf16),
        in_specs=[smem] * 4 + [any_spec] * 7,
        out_specs=any_spec,
        scratch_shapes=[
            pltpu.VMEM((part, width), bf16),
            pltpu.VMEM((1, width), f32),
            pltpu.VMEM((n, part, width), bf16),
            pltpu.VMEM((win, 2 * vcols), bf16),
            pltpu.VMEM((panels, rank_width, width), bf16),
            pltpu.VMEM((panels, rank_width, half), bf16),
            pltpu.VMEM((2 * panels, rank_width, 2 * vcols), bf16),
            pltpu.VMEM((tok, qcols), bf16),
            pltpu.VMEM((n, tok, vcols), bf16),
            pltpu.VMEM((n, part, 2 * vcols), f32),
            pltpu.VMEM((n, part, 2 * vcols), bf16),
            pltpu.VMEM((n, part, 2 * vcols), bf16),
            pltpu.VMEM((n, part, 2 * vcols), bf16),
            pltpu.VMEM((n, part, 2 * vcols), bf16),
            pltpu.VMEM((n, part, 2 * vcols), bf16),
            pltpu.VMEM((n, 2, part, vcols), bf16),
            pltpu.VMEM((qcols // HEAD_SIZE, tok, total), bf16),
            pltpu.VMEM((tok, qcols), bf16),
            dma((8,)),
            dma((2, CHUNKS)),
            dma((3, CHUNKS // 2)),
            dma((n, CHUNKS)),
            dma((3,)),
            dma((3,)),
            dma((4,)),
            dma((4,)),
            dma((4,)),
            dma((4,)),
            dma((n,)),
            dma((n,)),
            dma((n,)),
            dma((n,)),
            dma((n,)),
            dma((n,)),
            dma((n, 2)),
            dma((n,)),
            dma((n, 2)),
        ],
        compiler_params=pltpu.CompilerParams(
            collective_id=0, has_side_effects=True, vmem_limit_bytes=56 * 1024 * 1024
        ),
    )(
        request_token_lengths,
        adapter_per_request,
        rank_per_adapter,
        slot_per_adapter,
        layer_input_rows,
        encoded_query_rows,
        encoded_key_rows,
        layer_norm_gain,
        base_value_matrix,
        jnp.swapaxes(adapter_down_panels, 2, 3),
        adapter_up_panels,
    )


def solution(mesh):
    in_specs = (
        P("segment", ("groups", "seq"), None),
        P("segment", ("groups", "seq"), "owner"),
        P("segment", ("groups", "seq"), "owner"),
        P("segment", None),
        P("segment", ("seq", "owner"), None),
        P("segment", "seq", "owner", None),
        P("segment", "seq", None, "owner"),
        P("groups"),
        P("groups"),
        P(),
        P(),
    )
    out_specs = P("segment", ("groups", "seq"), "owner")
    n = mesh.shape["seq"]
    small = mesh.shape["owner"] == 2 and mesh.shape["groups"] == 2 and n == 4
    return jax.shard_map(
        functools.partial(fused, n) if small else per_device, mesh=mesh, in_specs=in_specs, out_specs=out_specs, check_vma=False
    )
```

```python
import functools

import jax
import jax.numpy as jnp
from jax import lax
from jax.experimental import pallas as pl
from jax.experimental.pallas import tpu as pltpu
from jax.sharding import PartitionSpec as P

WINDOW = 1024
HEADS = 16
KEY_VALUE_HEADS = 8
HEAD_SIZE = 128


query_scale = 168.0 ** (-0.5)
adapter_strength = 32.0
norm_eps = 1e-06


def broadcast(x, axis, root):
    mine = lax.axis_index(axis) == root
    return lax.psum(jnp.where(mine, x, jnp.zeros_like(x)), axis)


def from_behind(value, axis, steps):
    count = lax.axis_size(axis)
    first, last = (max(0, -steps), min(count, count - steps))
    return lax.ppermute(value, axis, [(source, source + steps) for source in range(first, last)])


def per_device(
    layer_input_rows,
    encoded_query_rows,
    encoded_key_rows,
    layer_norm_gain,
    base_value_matrix,
    adapter_down_panels,
    adapter_up_panels,
    request_token_lengths,
    adapter_per_request,
    rank_per_adapter,
    slot_per_adapter,
):
    hidden = layer_input_rows[0]
    row_count = hidden.shape[0]
    seq_now = lax.axis_index("seq")
    owner_now = lax.axis_index("owner")
    reach_count = min(WINDOW // row_count, lax.axis_size("seq") - 1)
    requests = request_token_lengths.shape[0]
    library = slot_per_adapter.shape[0]
    slots_here = adapter_down_panels.shape[1]
    rows_halved = adapter_down_panels.shape[2]
    rank_span_width = adapter_down_panels.shape[3]
    key_value_halved = adapter_up_panels.shape[3]
    group_size = HEADS // KEY_VALUE_HEADS
    request_ends = jnp.cumsum(request_token_lengths)
    position = seq_now * row_count + jnp.arange(row_count, dtype=jnp.int32)
    context = seq_now * row_count + jnp.arange(-reach_count * row_count, row_count, dtype=jnp.int32)
    request_lookup = jnp.sum((position[:, None] >= request_ends[None, :]).astype(jnp.int32), axis=1)
    request_ctx = jnp.sum((context[:, None] >= request_ends[None, :]).astype(jnp.int32), axis=1)
    live_mask = (context[None, :] <= position[:, None]) & (
        context[None, :] > position[:, None] - WINDOW
    )
    live_mask = (
        live_mask & (context[None, :] >= 0) & (request_ctx[None, :] == request_lookup[:, None])
    )
    choose = adapter_per_request[:, None] == jnp.arange(library, dtype=jnp.int32)[None, :]
    slot_of = jnp.sum(jnp.where(choose, slot_per_adapter[None, :], 0), axis=1)
    rank_lookup = jnp.sum(jnp.where(choose, rank_per_adapter[None, :], 0), axis=1)
    scale_lookup = adapter_strength / rank_lookup.astype(jnp.float32)
    in_request = request_lookup[:, None] == jnp.arange(requests, dtype=jnp.int32)[None, :]
    column_live = jnp.arange(rank_span_width, dtype=jnp.int32)[None, :] < rank_lookup[:, None]
    row_gain_weight = jnp.where(in_request, scale_lookup[None, :], jnp.float32(0.0))
    down_panel_here = adapter_down_panels[0]
    up_panel_here = adapter_up_panels[0]
    queries = encoded_query_rows[0]
    keys_own = encoded_key_rows[0]
    key_heads = keys_own.shape[1] // HEAD_SIZE
    wide_rows = hidden.astype(jnp.float32)
    normalized_rows = wide_rows * lax.rsqrt(
        jnp.mean(wide_rows * wide_rows, axis=1, keepdims=True) + norm_eps
    )
    normalized_rows = (normalized_rows * layer_norm_gain[0][None, :]).astype(jnp.bfloat16)
    normed_half = lax.dynamic_slice_in_dim(normalized_rows, owner_now * rows_halved, rows_halved, 1)
    full_value = jnp.dot(
        normalized_rows,
        lax.all_gather(base_value_matrix[0], ("seq", "owner"), axis=0, tiled=True),
        preferred_element_type=jnp.float32,
    )
    value_base_rows = lax.dynamic_slice_in_dim(
        full_value, owner_now * key_value_halved, key_value_halved, 1
    )

    def fetch_one(reduced_rows, request_index):
        owner_slot = slot_of[request_index]
        holder = owner_slot // slots_here
        local_slot = owner_slot % slots_here
        down_local = lax.dynamic_slice_in_dim(down_panel_here, local_slot, 1, 0)
        up_local = lax.dynamic_slice_in_dim(up_panel_here, local_slot, 1, 0)
        down_piece, up_piece = (
            broadcast(down_local, "seq", holder),
            broadcast(up_local, "seq", holder),
        )
        keep_mask = in_request[:, request_index][:, None] & column_live[request_index][None, :]
        matrix_product = jnp.dot(normed_half, down_piece[0], preferred_element_type=jnp.float32)
        return (reduced_rows + jnp.where(keep_mask, matrix_product, jnp.float32(0.0)), up_piece[0])

    start_low = jnp.zeros((row_count, rank_span_width), jnp.float32)
    reduced_rows, panels_up = lax.scan(fetch_one, start_low, jnp.arange(requests, dtype=jnp.int32))
    reduced_rows = lax.psum(reduced_rows, "owner").astype(jnp.bfloat16)
    raised_rows = jnp.einsum(
        "tr,qrk->qtk", reduced_rows, panels_up, preferred_element_type=jnp.float32
    )
    adapter_value = jnp.sum(row_gain_weight.T[:, :, None] * raised_rows, axis=0)
    value_output_rows = (value_base_rows + adapter_value).astype(jnp.bfloat16)
    key_parts = []
    value_parts = []
    for shift_by in range(reach_count, 0, -1):
        key_piece, value_piece = from_behind((keys_own, value_output_rows), "seq", shift_by)
        key_parts.append(key_piece)
        value_parts.append(value_piece)
    keys_all = jnp.concatenate(key_parts + [keys_own], axis=0)
    values_all = jnp.concatenate(value_parts + [value_output_rows], axis=0)
    query_view = queries.reshape(row_count, key_heads, group_size, HEAD_SIZE)
    key_view = keys_all.reshape(-1, key_heads, HEAD_SIZE)
    value_view = values_all.reshape(-1, key_heads, HEAD_SIZE)
    head_outputs = []
    for head_index in range(key_heads):
        query_head = query_view[:, head_index]
        scores = (
            jnp.einsum(
                "tcd,jd->ctj",
                query_head,
                key_view[:, head_index],
                preferred_element_type=jnp.float32,
            )
            * query_scale
        )
        scores = jnp.where(live_mask[None], scores, jnp.float32(-1e30))
        row_max = jnp.max(scores, axis=-1, keepdims=True)
        weights = jnp.exp(scores - row_max)
        row_total = jnp.sum(weights, axis=-1, keepdims=True)
        softmax_rows = (weights / row_total).astype(jnp.bfloat16)
        mixed = jnp.einsum(
            "ctj,jd->tcd",
            softmax_rows,
            value_view[:, head_index],
            preferred_element_type=jnp.float32,
        )
        head_outputs.append(mixed.astype(jnp.bfloat16).reshape(row_count, group_size * HEAD_SIZE))
    result = jnp.concatenate(head_outputs, axis=1)
    return result[None]


LANES = 128
CHUNKS = 4


def kernel(
    n,
    x_hbm,
    q_hbm,
    k_hbm,
    gain_hbm,
    w_hbm,
    down_hbm,
    up_hbm,
    lengths_hbm,
    adapters_hbm,
    ranks_hbm,
    slots_hbm,
    out_hbm,
    lengths,
    adapters,
    ranks,
    slots,
    xr,
    gain,
    xb,
    wbuf,
    dn,
    hdn,
    dnt,
    ucat,
    qb,
    kb,
    pown,
    pbuf,
    prec,
    sbuf,
    srec,
    vbuf,
    vall,
    prob,
    ob,
    loc_sem,
    x_send,
    x_recv,
    ex_send,
    ex_recv,
    ph_send,
    ph_recv,
    uh_send,
    uh_recv,
    k_send,
    k_recv,
    p_send,
    p_recv,
    s_send,
    s_recv,
    v_send,
    v_recv,
):
    f32, bf16 = jnp.float32, jnp.bfloat16
    s = lax.axis_index("seq")
    o = lax.axis_index("owner")
    g = lax.axis_index("groups")
    other = 1 - o
    tok, width = x_hbm.shape[1], x_hbm.shape[2]
    part = tok // 2
    half = width // 2
    win, vcols2 = wbuf.shape
    vcols = vcols2 // 2
    slab = w_hbm.shape[1]
    panels, rank_width = dn.shape[0], dn.shape[1]
    low_width = panels * rank_width
    rank_part = rank_width // 2
    chip_rows = width // n
    requests = lengths.shape[0]
    total = n * tok
    group = HEADS // KEY_VALUE_HEADS
    q_heads = qb.shape[1] // HEAD_SIZE
    wide = -(-half // (2 * LANES)) * LANES
    sizes = (wide, half - wide)

    def peer(seq, owner=None, groups=None):
        return {
            "seq": seq,
            "owner": o if owner is None else owner,
            "groups": g if groups is None else groups,
        }

    def remote(src, dst, send, recv, device):
        return pltpu.make_async_remote_copy(
            src_ref=src,
            dst_ref=dst,
            send_sem=send,
            recv_sem=recv,
            device_id=device,
            device_id_type=pl.DeviceIdType.MESH,
        )

    def arrived(ref, sem):
        remote(ref, ref, sem, sem, peer(s, other)).wait_recv()

    def sent(ref, sem):
        remote(ref, ref, sem, sem, peer(s, other)).wait_send()

    barrier = pltpu.get_barrier_semaphore()

    def greet(device):
        pl.semaphore_signal(barrier, inc=1, device_id=device, device_id_type=pl.DeviceIdType.MESH)

    my_rows = pl.ds(pl.multiple_of(o * part, 16), part)
    my_half = pl.ds(pl.multiple_of(o * half, LANES), half)
    other_half = pl.ds(pl.multiple_of(other * half, LANES), half)
    my_cols = pl.ds(pl.multiple_of(o * vcols, LANES), vcols)
    other_cols = pl.ds(pl.multiple_of(other * vcols, LANES), vcols)

    def half_at(which):
        return pl.ds(which * half, half)

    ends, slot_of, rank_of = [], [], []

    def read_tables():
        for at in range(7, 11):
            local[at].wait()
        run = jnp.int32(0)
        for r in range(requests):
            run = run + lengths[r]
            ends.append(run)
            adapter = adapters[r]
            slot_of.append(slots[adapter])
            rank_of.append(ranks[adapter])

    def request_at(position):
        found = jnp.zeros(position.shape, jnp.int32)
        for r in range(requests):
            found = found + (position >= ends[r]).astype(jnp.int32)
        return found

    def token_facts(first, count):
        row = lax.broadcasted_iota(jnp.int32, (count * part, 1), 0)
        position = (first + row // part) * tok + o * part + row % part
        req = request_at(position)
        slot_t = jnp.zeros(row.shape, jnp.int32)
        rank_t = jnp.ones(row.shape, jnp.int32)
        for r in range(requests):
            slot_t = jnp.where(req == r, slot_of[r], slot_t)
            rank_t = jnp.where(req == r, rank_of[r], rank_t)
        return slot_t, rank_t

    def masked(low, slot_t, rank_t, chip):
        column = lax.broadcasted_iota(jnp.int32, low.shape, 1)
        start = (slot_t - chip * panels) * rank_width
        return jnp.where((column >= start) & (column < start + rank_t), low, 0.0).astype(bf16)

    def dot(a, b):
        return jnp.dot(a, b, preferred_element_type=f32)

    def window_of(c):
        at = min(c * chip_rows // LANES * LANES, width - win)
        return at, c * chip_rows - at

    def rows_of(first, count, columns):
        return xb[first : first + count, :, columns].reshape(count * part, columns.size)

    def partial(c, first, count, own, hosted, chip):
        slot_t, rank_t = token_facts(first, count)
        at, _ = window_of(c)
        base = dot(rows_of(first, count, pl.ds(at, win)), wbuf[...])
        if hosted is None:
            low = dot(rows_of(first, count, half_at(own)), dnt[half_at(own), :low_width])
            low = masked(low, slot_t, rank_t, c)
            raised = dot(low, ucat[:panels].reshape(low_width, vcols2))
        else:
            both = dot(rows_of(first, count, half_at(hosted)), dnt[half_at(hosted), :])
            low = both[:, :low_width] + dot(rows_of(first, count, half_at(own)), dnt[half_at(own), :low_width])
            low = jnp.concatenate(
                [masked(low, slot_t, rank_t, c), masked(both[:, low_width:], slot_t, rank_t, chip)], axis=1
            )
            raised = dot(low, ucat[...].reshape(2 * low_width, vcols2))
        value = base + raised * (adapter_strength / rank_t.astype(f32))
        return value.reshape(count, part, vcols2)

    def chunk(q, up):
        at = (up if q < CHUNKS // 2 else 1 - up) * half + (q % 2) * wide
        return pl.ds(at, sizes[q % 2])

    local = [
        pltpu.make_async_copy(x_hbm.at[0, my_rows, :], xr, loc_sem.at[0]),
        pltpu.make_async_copy(gain_hbm, gain, loc_sem.at[1]),
        pltpu.make_async_copy(w_hbm.at[0], wbuf.at[pl.ds(0, slab)], loc_sem.at[2]),
        pltpu.make_async_copy(down_hbm.at[0], dn.at[:, :, my_half], loc_sem.at[3]),
        pltpu.make_async_copy(up_hbm.at[0], ucat.at[pl.ds(0, panels), :, my_cols], loc_sem.at[4]),
        pltpu.make_async_copy(q_hbm.at[0], qb, loc_sem.at[5]),
        pltpu.make_async_copy(k_hbm.at[0], kb.at[s], loc_sem.at[6]),
        pltpu.make_async_copy(lengths_hbm, lengths, loc_sem.at[7]),
        pltpu.make_async_copy(adapters_hbm, adapters, loc_sem.at[8]),
        pltpu.make_async_copy(ranks_hbm, ranks, loc_sem.at[9]),
        pltpu.make_async_copy(slots_hbm, slots, loc_sem.at[10]),
    ]

    def slab_at(c):
        _, pad = window_of(c)
        return pl.ds(pl.multiple_of(pad + o * slab, 16), slab)

    def transpose_panels(source, which, at):
        for piece in range(0, half, half // 3):
            rows = source[:, :, pl.ds(which * half + piece if source.shape[2] == width else piece, half // 3)]
            dnt[pl.ds(which * half + piece, half // 3), at : at + low_width] = rows.reshape(
                low_width, half // 3
            ).T

    def opening(c, greetings, count):
        local[0].start()
        local[1].start()
        w_local = pltpu.make_async_copy(w_hbm.at[0], wbuf.at[slab_at(c)], loc_sem.at[2])
        w_local.start()
        for at in range(3, 11):
            local[at].start()
        for device in greetings:
            greet(device)
        _, pad = window_of(c)
        if pad:
            wbuf[0:pad, :] = jnp.zeros((pad, vcols2), bf16)
        rest = win - pad - chip_rows
        if rest:
            wbuf[win - rest : win, :] = jnp.zeros((rest, vcols2), bf16)
        for t in range(c + 1, n):
            kb[t] = jnp.zeros(kb.shape[1:], bf16)
            vall[t] = jnp.zeros(vall.shape[1:], bf16)
        local[0].wait()
        local[1].wait()
        rows = xr[...].astype(f32)
        inv = lax.rsqrt(jnp.mean(rows * rows, axis=1, keepdims=True) + norm_eps)
        xb[c] = (xr[...].astype(f32) * inv * gain[...]).astype(bf16)
        pl.semaphore_wait(barrier, count)

    def exchange(c, kept):
        w_copy = remote(w_hbm.at[0], wbuf.at[slab_at(c)], ex_send.at[0], ex_recv.at[0], peer(c, other))
        dn_copy = remote(down_hbm.at[0], dn.at[:, :, my_half], ex_send.at[1], ex_recv.at[1], peer(c, other))
        up_copy = remote(
            up_hbm.at[0], ucat.at[pl.ds(0, panels), :, my_cols], ex_send.at[2], ex_recv.at[2], peer(c, other)
        )
        return w_copy, dn_copy, up_copy

    def attend(c):
        keys = kb[...].reshape(total, vcols)
        key_at = lax.broadcasted_iota(jnp.int32, (1, total), 1)
        query_at = c * tok + lax.broadcasted_iota(jnp.int32, (tok, 1), 0)
        live = (key_at <= query_at) & (key_at > query_at - WINDOW)
        live = live & (request_at(query_at) == request_at(key_at))
        for h in range(q_heads):
            kv = h // group
            scores = (
                lax.dot_general(
                    qb[:, h * HEAD_SIZE : (h + 1) * HEAD_SIZE],
                    keys[:, kv * HEAD_SIZE : (kv + 1) * HEAD_SIZE],
                    (((1,), (1,)), ((), ())),
                    preferred_element_type=f32,
                )
                * query_scale
            )
            scores = jnp.where(live, scores, -1e30)
            weights = jnp.exp(scores - jnp.max(scores, axis=1, keepdims=True))
            soft = weights / jnp.sum(weights, axis=1, keepdims=True)
            prob[h] = soft.astype(bf16)

    result = pltpu.make_async_copy(ob, out_hbm.at[0], loc_sem.at[0])

    def mix(c):
        values = vall[...].reshape(total, vcols)
        for h in range(q_heads):
            kv = h // group
            ob[:, h * HEAD_SIZE : (h + 1) * HEAD_SIZE] = dot(
                prob[h], values[:, kv * HEAD_SIZE : (kv + 1) * HEAD_SIZE]
            ).astype(bf16)
        result.start()

    per_group = panels // 2
    mine = pl.ds(g * per_group, per_group)
    theirs = pl.ds((1 - g) * per_group, per_group)
    my_up = pl.ds(panels + g * per_group, per_group)
    their_up = pl.ds(panels + (1 - g) * per_group, per_group)
    my_piece = pl.ds(pl.multiple_of(o * rank_part, 16), rank_part)
    other_piece = pl.ds(pl.multiple_of(other * rank_part, 16), rank_part)

    def x_end(c, t, q, up, to):
        at = xb.at[t, :, chunk(q, up)]
        return remote(at, at, x_send.at[0], x_recv.at[q], peer(to))

    def x_across(t, q, up, to, forwarded):
        at = xb.at[t, :, chunk(q, up)]
        index = (7 if forwarded else 4) + min(q, 2)
        return remote(at, at, x_send.at[0], x_recv.at[index], peer(to))

    def x_outward(t, q, up, to, index):
        at = xb.at[t, :, chunk(q, up)]
        return remote(at, at, x_send.at[1], x_recv.at[index], peer(to))

    def k_up(c, t):
        return remote(kb.at[t], kb.at[t], k_send, k_recv, peer(c + 1))

    def end_program(c):
        low = c < n // 2
        i, j, f = (1, 2, 3) if low else (2, 1, 0)
        inward = int(low)
        kept = 1 - inward
        host_core = inward
        opening(c, [peer(c, other), peer(i), peer(i, other)], 3)
        w_copy, dn_copy, up_copy = exchange(c, kept)
        piece_in = remote(
            down_hbm.at[0, mine, other_piece, :], hdn.at[mine, other_piece, :], ph_send.at[1], ph_recv.at[1], peer(c, other)
        )
        piece_z = remote(
            down_hbm.at[0, mine, my_piece, :], hdn.at[mine, my_piece, :], ph_send.at[0], ph_recv.at[0], peer(i)
        )
        piece_on = remote(
            hdn.at[mine, my_piece, :], hdn.at[mine, my_piece, :], ph_send.at[0], ph_recv.at[0], peer(i)
        )
        up_z = remote(up_hbm.at[0, mine], ucat.at[my_up, :, my_cols], uh_send.at[0], uh_recv.at[0], peer(i))

        @pl.when(o == host_core)
        def _():
            piece_in.start()
            piece_z.start()
            up_z.start()
            x_end(c, c, 0, inward, i).start()

        @pl.when(o != host_core)
        def _():
            up_z.start()
            x_end(c, c, 0, inward, i).start()
            dn_copy.start()

        w_copy.start()
        up_copy.start()

        @pl.when(o != host_core)
        def _():
            arrived(hdn.at[mine, my_piece, :], ph_recv.at[1])
            piece_on.start()

        for q in range(1, CHUNKS):
            x_end(c, c, q, inward, i).start()
        if c == 0:
            local[6].wait()
            k_up(c, c).start()
        for at in (2, 3, 4):
            local[at].wait()
        read_tables()

        @pl.when(o == host_core)
        def _():
            arrived(dn.at[:, :, other_half], ex_recv.at[1])

        transpose_panels(dn, kept, 0)
        arrived(ucat.at[pl.ds(0, panels), :, other_cols], ex_recv.at[2])
        arrived(wbuf.at[pl.ds(0, slab)], ex_recv.at[0])

        def p_copy(t):
            index = 1 if t == f else 2 if t == i and not low else 0
            return remote(pbuf.at[t], prec.at[t], p_send, p_recv.at[index], peer(i))

        p_core = remote(
            pbuf.at[c, :, other_cols], prec.at[c, :, pl.ds(0, vcols)], s_send, s_recv.at[0], peer(c, other)
        )

        def end_partial(t):
            pbuf[t] = partial(c, t, 1, kept, None, c)[0].astype(bf16)

        end_partial(c)
        if low:
            p_copy(c).start()
        else:
            p_core.start()
        for index, t in enumerate((i, j, f)):
            arrived(xb.at[t, :, half_at(kept)], x_recv.at[index])
            end_partial(t)
            if low or t != i:
                p_copy(t).start()
            if not low and t == f:
                p_copy(i).start()
        local[5].wait()
        if low:
            attend(c)
            arrived(vall.at[0], v_recv.at[0])
        else:
            local[6].wait()
            arrived(kb.at[pl.ds(0, n - 1)], k_recv)
            attend(c)
            arrived(prec.at[c, :, pl.ds(0, vcols)], s_recv.at[0])
            for t in range(n):
                arrived(vall.at[t], v_recv.at[t])
            vall[c, o] = (vall[c, o].astype(f32) + pbuf[c, :, my_cols].astype(f32)).astype(bf16)
            vall[c, other] = (vall[c, other].astype(f32) + prec[c, :, 0:vcols].astype(f32)).astype(bf16)
        mix(c)

        sent(wbuf.at[pl.ds(0, slab)], ex_send.at[0])
        sent(ucat.at[pl.ds(0, panels), :, other_cols], ex_send.at[2])
        sent(hdn.at[mine, my_piece, :], ph_send.at[0])

        @pl.when(o == host_core)
        def _():
            sent(hdn.at[mine, my_piece, :], ph_send.at[1])

        @pl.when(o != host_core)
        def _():
            sent(dn.at[:, :, my_half], ex_send.at[1])

        sent(ucat.at[my_up, :, my_cols], uh_send.at[0])
        sent(xb.at[0], x_send.at[0])
        if c == 0:
            sent(kb.at[0], k_send)
            sent(pbuf, p_send)
        else:
            sent(pbuf.at[pl.ds(0, n - 1)], p_send)
            sent(pbuf.at[c, :, other_cols], s_send)
        result.wait()

    def inner_program(c):
        low = c < n // 2
        e, j, f = (0, 2, 3) if low else (3, 1, 0)
        inward = int(low)
        outward = 1 - inward
        first = min(c, e, j)
        opening(c, [peer(c, other), peer(e), peer(e, other), peer(j), peer(c, o, 1 - g)], 5)
        w_copy, dn_copy, up_copy = exchange(c, None)
        for q in range(CHUNKS):
            x_across(c, q, inward, j, False).start()
            if q < CHUNKS // 2:
                x_outward(c, q, outward, e, 0).start()
        w_copy.start()
        dn_copy.start()
        up_copy.start()
        local[6].wait()
        if not low:
            k_up(c, c).start()
        for at in (2, 3, 4):
            local[at].wait()
        read_tables()
        arrived(dn.at[:, :, other_half], ex_recv.at[1])
        transpose_panels(dn, outward, 0)
        transpose_panels(dn, inward, 0)

        def next_e(q):
            arrived(xb.at[e, :, chunk(q, inward)], x_recv.at[q])
            x_across(e, q, inward, j, True).start()

        def next_j(q):
            arrived(xb.at[j, :, chunk(q, outward)], x_recv.at[4 + q])
            x_outward(j, q, outward, e, 1).start()

        def next_f(q):
            arrived(xb.at[f, :, chunk(q, outward)], x_recv.at[7 + q])
            x_outward(f, q, outward, e, 2).start()

        def piece(which, ranks_at):
            return hdn.at[which, ranks_at, :]

        def pass_on(which, ranks_at, sem, recv, device):
            return remote(piece(which, ranks_at), piece(which, ranks_at), ph_send.at[sem], ph_recv.at[recv], device)

        def pass_up(which, sem, recv, device):
            at = ucat.at[which, :, my_cols]
            return remote(at, at, uh_send.at[sem], uh_recv.at[recv], device)

        def host_z():
            arrived(piece(mine, my_piece), ph_recv.at[0])
            pass_on(mine, my_piece, 0, 1, peer(c, o, 1 - g)).start()
            pass_on(mine, my_piece, 1, 2, peer(c, other)).start()
            arrived(ucat.at[my_up, :, my_cols], uh_recv.at[0])
            pass_up(my_up, 0, 1, peer(c, o, 1 - g)).start()
            pass_up(my_up, 1, 2, peer(c, other)).start()

        def host_y():
            arrived(piece(theirs, my_piece), ph_recv.at[1])
            pass_on(theirs, my_piece, 1, 3, peer(c, other)).start()
            arrived(ucat.at[their_up, :, my_cols], uh_recv.at[1])
            pass_up(their_up, 1, 3, peer(c, other)).start()

        def host_done():
            arrived(piece(mine, other_piece), ph_recv.at[2])
            arrived(piece(theirs, other_piece), ph_recv.at[3])
            transpose_panels(hdn, inward, low_width)
            arrived(ucat.at[my_up, :, other_cols], uh_recv.at[2])
            arrived(ucat.at[their_up, :, other_cols], uh_recv.at[3])

        if low:
            host_z()
            next_j(0)
            next_e(0)
            next_j(1)
            next_e(1)
            host_y()
            next_e(2)
            next_e(3)
            k_up(c, c).start()
            arrived(kb.at[0], k_recv)
            k_up(c, 0).start()
            host_done()
            next_f(0)
        else:
            next_j(0)
            next_j(1)
            host_z()
            next_e(0)
            next_f(0)
            next_e(1)
            host_y()
            next_f(1)
            next_e(2)
            host_done()
            next_e(3)
        arrived(ucat.at[pl.ds(0, panels), :, other_cols], ex_recv.at[2])
        arrived(wbuf.at[pl.ds(0, slab)], ex_recv.at[0])
        arrived(xb.at[j, :, half_at(inward)], x_recv.at[6])
        pown[first : first + 3] = partial(c, first, 3, outward, inward, e)
        if low:
            next_f(1)

        def s_copy(t):
            return remote(sbuf.at[t], srec.at[t], s_send, s_recv.at[t], peer(j))

        def add_end(t):
            if low or t != e:
                value = pown[t] + prec[t].astype(f32)
                pown[t] = value
                if low or t < n // 2:
                    sbuf[t] = value.astype(bf16)
                    s_copy(t).start()

        if low:
            arrived(prec.at[pl.ds(0, 3)], p_recv.at[0])
            for t in range(3):
                add_end(t)
        arrived(xb.at[f, :, half_at(inward)], x_recv.at[9])
        pown[f] = partial(c, f, 1, outward, inward, e)[0]
        if not low:
            arrived(prec.at[j], p_recv.at[0])
            add_end(j)
        arrived(prec.at[f], p_recv.at[1])
        add_end(f)
        local[5].wait()
        if not low:
            arrived(kb.at[pl.ds(0, 2)], k_recv)
            for t in range(2):
                k_up(c, t).start()
        attend(c)

        def v_end(t, core):
            cols = pl.ds(core * vcols, vcols)
            return remote(vbuf.at[t, :, cols], vall.at[t, o], v_send.at[0], v_recv.at[t], peer(e, core))

        def v_core(t):
            return remote(vbuf.at[t, :, other_cols], vall.at[t, o], v_send.at[1], v_recv.at[t], peer(c, other))

        def finish(t):
            arrived(srec.at[t], s_recv.at[t])
            vbuf[t] = (pown[t] + srec[t].astype(f32)).astype(bf16)
            if t == 0 or not low:
                v_end(t, 0).start()
                v_end(t, 1).start()
            if t <= c:
                v_core(t).start()
                vall[t, o] = vbuf[t, :, my_cols]

        if low:
            finish(1)
            finish(0)
        else:
            arrived(prec.at[c], p_recv.at[2])
            pown[c] = pown[c] + prec[c].astype(f32)
            for t in range(n):
                finish(t)
        for t in range(c + 1):
            arrived(vall.at[t, other], v_recv.at[t])
        mix(c)

        sent(wbuf.at[pl.ds(0, slab)], ex_send.at[0])
        sent(dn.at[:, :, my_half], ex_send.at[1])
        sent(ucat.at[pl.ds(0, panels), :, other_cols], ex_send.at[2])
        sent(xb.at[pl.ds(0, 2)], x_send.at[0])
        sent(xb.at[pl.ds(0, 3), :, half_at(0)], x_send.at[1])
        sent(piece(mine, my_piece), ph_send.at[0])
        sent(hdn.at[:, my_piece, :], ph_send.at[1])
        sent(ucat.at[my_up, :, my_cols], uh_send.at[0])
        sent(ucat.at[pl.ds(panels, panels), :, my_cols], uh_send.at[1])
        sent(kb.at[pl.ds(0, c + 1)], k_send)
        if low:
            sent(sbuf, s_send)
            sent(vbuf.at[0], v_send.at[0])
        else:
            sent(sbuf.at[pl.ds(0, 2)], s_send)
            sent(vbuf, v_send.at[0])
        sent(vbuf.at[pl.ds(0, c + 1), :, pl.ds(0, vcols)], v_send.at[1])
        result.wait()

    for c in range(n):

        @pl.when(s == c)
        def _():
            ends.clear()
            slot_of.clear()
            rank_of.clear()
            if c in (0, n - 1):
                end_program(c)
            else:
                inner_program(c)


def fused(
    n,
    layer_input_rows,
    encoded_query_rows,
    encoded_key_rows,
    layer_norm_gain,
    base_value_matrix,
    adapter_down_panels,
    adapter_up_panels,
    request_token_lengths,
    adapter_per_request,
    rank_per_adapter,
    slot_per_adapter,
):
    f32, bf16 = jnp.float32, jnp.bfloat16
    tok, width = layer_input_rows.shape[1:]
    part, half = tok // 2, width // 2
    panels, _, rank_width = adapter_down_panels.shape[1:]
    vcols = adapter_up_panels.shape[3]
    qcols = encoded_query_rows.shape[2]
    chip_rows = width // n
    pads = [i * chip_rows % LANES for i in range(n)]
    win = -(-(max(pads) + chip_rows) // LANES) * LANES
    total = n * tok
    dma = pltpu.SemaphoreType.DMA
    any_spec = pl.BlockSpec(memory_space=pl.ANY)
    return pl.pallas_call(
        functools.partial(kernel, n),
        out_shape=jax.ShapeDtypeStruct(encoded_query_rows.shape, bf16),
        in_specs=[any_spec] * 11,
        out_specs=any_spec,
        scratch_shapes=[
            pltpu.SMEM(request_token_lengths.shape, jnp.int32),
            pltpu.SMEM(adapter_per_request.shape, jnp.int32),
            pltpu.SMEM(rank_per_adapter.shape, jnp.int32),
            pltpu.SMEM(slot_per_adapter.shape, jnp.int32),
            pltpu.VMEM((part, width), bf16),
            pltpu.VMEM((1, width), f32),
            pltpu.VMEM((n, part, width), bf16),
            pltpu.VMEM((win, 2 * vcols), bf16),
            pltpu.VMEM((panels, rank_width, width), bf16),
            pltpu.VMEM((panels, rank_width, half), bf16),
            pltpu.VMEM((width, 2 * panels * rank_width), bf16),
            pltpu.VMEM((2 * panels, rank_width, 2 * vcols), bf16),
            pltpu.VMEM((tok, qcols), bf16),
            pltpu.VMEM((n, tok, vcols), bf16),
            pltpu.VMEM((n, part, 2 * vcols), f32),
            pltpu.VMEM((n, part, 2 * vcols), bf16),
            pltpu.VMEM((n, part, 2 * vcols), bf16),
            pltpu.VMEM((n, part, 2 * vcols), bf16),
            pltpu.VMEM((n, part, 2 * vcols), bf16),
            pltpu.VMEM((n, part, 2 * vcols), bf16),
            pltpu.VMEM((n, 2, part, vcols), bf16),
            pltpu.VMEM((qcols // HEAD_SIZE, tok, total), bf16),
            pltpu.VMEM((tok, qcols), bf16),
            dma((11,)),
            dma((2,)),
            dma((10,)),
            dma((3,)),
            dma((3,)),
            dma((2,)),
            dma((4,)),
            dma((2,)),
            dma((4,)),
            dma,
            dma,
            dma,
            dma((3,)),
            dma,
            dma((n,)),
            dma((2,)),
            dma((n,)),
        ],
        compiler_params=pltpu.CompilerParams(
            collective_id=0, has_side_effects=True, vmem_limit_bytes=56 * 1024 * 1024
        ),
    )(
        layer_input_rows,
        encoded_query_rows,
        encoded_key_rows,
        layer_norm_gain,
        base_value_matrix,
        jnp.swapaxes(adapter_down_panels, 2, 3),
        adapter_up_panels,
        request_token_lengths,
        adapter_per_request,
        rank_per_adapter,
        slot_per_adapter,
    )


def solution(mesh):
    in_specs = (
        P("segment", ("groups", "seq"), None),
        P("segment", ("groups", "seq"), "owner"),
        P("segment", ("groups", "seq"), "owner"),
        P("segment", None),
        P("segment", ("seq", "owner"), None),
        P("segment", "seq", "owner", None),
        P("segment", "seq", None, "owner"),
        P("groups"),
        P("groups"),
        P(),
        P(),
    )
    out_specs = P("segment", ("groups", "seq"), "owner")
    n = mesh.shape["seq"]
    small = mesh.shape["owner"] == 2 and mesh.shape["groups"] == 2 and n == 4
    return jax.shard_map(
        functools.partial(fused, n) if small else per_device, mesh=mesh, in_specs=in_specs, out_specs=out_specs, check_vma=False
    )
```

```python
import functools

import jax
import jax.numpy as jnp
from jax import lax
from jax.experimental import pallas as pl
from jax.experimental.pallas import tpu as pltpu
from jax.sharding import PartitionSpec as P

WINDOW = 1024
HEADS = 16
KEY_VALUE_HEADS = 8
HEAD_SIZE = 128


query_scale = 168.0 ** (-0.5)
adapter_strength = 32.0
norm_eps = 1e-06


def broadcast(x, axis, root):
    mine = lax.axis_index(axis) == root
    return lax.psum(jnp.where(mine, x, jnp.zeros_like(x)), axis)


def from_behind(value, axis, steps):
    count = lax.axis_size(axis)
    first, last = (max(0, -steps), min(count, count - steps))
    return lax.ppermute(value, axis, [(source, source + steps) for source in range(first, last)])


def per_device(
    layer_input_rows,
    encoded_query_rows,
    encoded_key_rows,
    layer_norm_gain,
    base_value_matrix,
    adapter_down_panels,
    adapter_up_panels,
    request_token_lengths,
    adapter_per_request,
    rank_per_adapter,
    slot_per_adapter,
):
    hidden = layer_input_rows[0]
    row_count = hidden.shape[0]
    seq_now = lax.axis_index("seq")
    owner_now = lax.axis_index("owner")
    reach_count = min(WINDOW // row_count, lax.axis_size("seq") - 1)
    requests = request_token_lengths.shape[0]
    library = slot_per_adapter.shape[0]
    slots_here = adapter_down_panels.shape[1]
    rows_halved = adapter_down_panels.shape[2]
    rank_span_width = adapter_down_panels.shape[3]
    key_value_halved = adapter_up_panels.shape[3]
    group_size = HEADS // KEY_VALUE_HEADS
    request_ends = jnp.cumsum(request_token_lengths)
    position = seq_now * row_count + jnp.arange(row_count, dtype=jnp.int32)
    context = seq_now * row_count + jnp.arange(-reach_count * row_count, row_count, dtype=jnp.int32)
    request_lookup = jnp.sum((position[:, None] >= request_ends[None, :]).astype(jnp.int32), axis=1)
    request_ctx = jnp.sum((context[:, None] >= request_ends[None, :]).astype(jnp.int32), axis=1)
    live_mask = (context[None, :] <= position[:, None]) & (
        context[None, :] > position[:, None] - WINDOW
    )
    live_mask = (
        live_mask & (context[None, :] >= 0) & (request_ctx[None, :] == request_lookup[:, None])
    )
    choose = adapter_per_request[:, None] == jnp.arange(library, dtype=jnp.int32)[None, :]
    slot_of = jnp.sum(jnp.where(choose, slot_per_adapter[None, :], 0), axis=1)
    rank_lookup = jnp.sum(jnp.where(choose, rank_per_adapter[None, :], 0), axis=1)
    scale_lookup = adapter_strength / rank_lookup.astype(jnp.float32)
    in_request = request_lookup[:, None] == jnp.arange(requests, dtype=jnp.int32)[None, :]
    column_live = jnp.arange(rank_span_width, dtype=jnp.int32)[None, :] < rank_lookup[:, None]
    row_gain_weight = jnp.where(in_request, scale_lookup[None, :], jnp.float32(0.0))
    down_panel_here = adapter_down_panels[0]
    up_panel_here = adapter_up_panels[0]
    queries = encoded_query_rows[0]
    keys_own = encoded_key_rows[0]
    key_heads = keys_own.shape[1] // HEAD_SIZE
    wide_rows = hidden.astype(jnp.float32)
    normalized_rows = wide_rows * lax.rsqrt(
        jnp.mean(wide_rows * wide_rows, axis=1, keepdims=True) + norm_eps
    )
    normalized_rows = (normalized_rows * layer_norm_gain[0][None, :]).astype(jnp.bfloat16)
    normed_half = lax.dynamic_slice_in_dim(normalized_rows, owner_now * rows_halved, rows_halved, 1)
    full_value = jnp.dot(
        normalized_rows,
        lax.all_gather(base_value_matrix[0], ("seq", "owner"), axis=0, tiled=True),
        preferred_element_type=jnp.float32,
    )
    value_base_rows = lax.dynamic_slice_in_dim(
        full_value, owner_now * key_value_halved, key_value_halved, 1
    )

    def fetch_one(reduced_rows, request_index):
        owner_slot = slot_of[request_index]
        holder = owner_slot // slots_here
        local_slot = owner_slot % slots_here
        down_local = lax.dynamic_slice_in_dim(down_panel_here, local_slot, 1, 0)
        up_local = lax.dynamic_slice_in_dim(up_panel_here, local_slot, 1, 0)
        down_piece, up_piece = (
            broadcast(down_local, "seq", holder),
            broadcast(up_local, "seq", holder),
        )
        keep_mask = in_request[:, request_index][:, None] & column_live[request_index][None, :]
        matrix_product = jnp.dot(normed_half, down_piece[0], preferred_element_type=jnp.float32)
        return (reduced_rows + jnp.where(keep_mask, matrix_product, jnp.float32(0.0)), up_piece[0])

    start_low = jnp.zeros((row_count, rank_span_width), jnp.float32)
    reduced_rows, panels_up = lax.scan(fetch_one, start_low, jnp.arange(requests, dtype=jnp.int32))
    reduced_rows = lax.psum(reduced_rows, "owner").astype(jnp.bfloat16)
    raised_rows = jnp.einsum(
        "tr,qrk->qtk", reduced_rows, panels_up, preferred_element_type=jnp.float32
    )
    adapter_value = jnp.sum(row_gain_weight.T[:, :, None] * raised_rows, axis=0)
    value_output_rows = (value_base_rows + adapter_value).astype(jnp.bfloat16)
    key_parts = []
    value_parts = []
    for shift_by in range(reach_count, 0, -1):
        key_piece, value_piece = from_behind((keys_own, value_output_rows), "seq", shift_by)
        key_parts.append(key_piece)
        value_parts.append(value_piece)
    keys_all = jnp.concatenate(key_parts + [keys_own], axis=0)
    values_all = jnp.concatenate(value_parts + [value_output_rows], axis=0)
    query_view = queries.reshape(row_count, key_heads, group_size, HEAD_SIZE)
    key_view = keys_all.reshape(-1, key_heads, HEAD_SIZE)
    value_view = values_all.reshape(-1, key_heads, HEAD_SIZE)
    head_outputs = []
    for head_index in range(key_heads):
        query_head = query_view[:, head_index]
        scores = (
            jnp.einsum(
                "tcd,jd->ctj",
                query_head,
                key_view[:, head_index],
                preferred_element_type=jnp.float32,
            )
            * query_scale
        )
        scores = jnp.where(live_mask[None], scores, jnp.float32(-1e30))
        row_max = jnp.max(scores, axis=-1, keepdims=True)
        weights = jnp.exp(scores - row_max)
        row_total = jnp.sum(weights, axis=-1, keepdims=True)
        softmax_rows = (weights / row_total).astype(jnp.bfloat16)
        mixed = jnp.einsum(
            "ctj,jd->tcd",
            softmax_rows,
            value_view[:, head_index],
            preferred_element_type=jnp.float32,
        )
        head_outputs.append(mixed.astype(jnp.bfloat16).reshape(row_count, group_size * HEAD_SIZE))
    result = jnp.concatenate(head_outputs, axis=1)
    return result[None]


LANES = 128
CHUNKS = 4


def kernel(
    n,
    x_hbm,
    q_hbm,
    k_hbm,
    gain_hbm,
    w_hbm,
    down_hbm,
    up_hbm,
    lengths_hbm,
    adapters_hbm,
    ranks_hbm,
    slots_hbm,
    out,
    lengths,
    adapters,
    ranks,
    slots,
    xr,
    gain,
    xb,
    wbuf,
    dn,
    hdn,
    dnt,
    ucat,
    qb,
    kb,
    pown,
    pbuf,
    prec,
    sbuf,
    srec,
    vbuf,
    vx,
    vall,
    va,
    prob,
    loc_sem,
    x_send,
    x_recv,
    ex_send,
    ex_recv,
    ph_send,
    ph_recv,
    uh_send,
    uh_recv,
    k_send,
    k_recv,
    p_send,
    p_recv,
    s_send,
    s_recv,
    v_send,
    v_recv,
    d_recv,
    ready,
):
    f32, bf16 = jnp.float32, jnp.bfloat16
    s = lax.axis_index("seq")
    o = lax.axis_index("owner")
    g = lax.axis_index("groups")
    other = 1 - o
    tok, width = x_hbm.shape[1], x_hbm.shape[2]
    part = tok // 2
    half = width // 2
    win, vcols2 = wbuf.shape
    vcols = vcols2 // 2
    slab = w_hbm.shape[1]
    panels, rank_width = dn.shape[0], dn.shape[1]
    low_width = panels * rank_width
    rank_part = rank_width // 2
    chip_rows = width // n
    requests = lengths.shape[0]
    total = n * tok
    group = HEADS // KEY_VALUE_HEADS
    q_heads = qb.shape[1] // HEAD_SIZE
    wide = -(-half // (2 * LANES)) * LANES
    sizes = (wide, half - wide)

    def peer(seq, owner=None, groups=None):
        return {
            "seq": seq,
            "owner": o if owner is None else owner,
            "groups": g if groups is None else groups,
        }

    def remote(src, dst, send, recv, device):
        return pltpu.make_async_remote_copy(
            src_ref=src,
            dst_ref=dst,
            send_sem=send,
            recv_sem=recv,
            device_id=device,
            device_id_type=pl.DeviceIdType.MESH,
        )

    def arrived(ref, sem):
        remote(ref, ref, sem, sem, peer(s, other)).wait_recv()

    def sent(ref, sem):
        remote(ref, ref, sem, sem, peer(s, other)).wait_send()

    barrier = pltpu.get_barrier_semaphore()

    def greet(device):
        pl.semaphore_signal(barrier, inc=1, device_id=device, device_id_type=pl.DeviceIdType.MESH)

    my_rows = pl.ds(pl.multiple_of(o * part, 16), part)
    my_half = pl.ds(pl.multiple_of(o * half, LANES), half)
    other_half = pl.ds(pl.multiple_of(other * half, LANES), half)
    my_cols = pl.ds(pl.multiple_of(o * vcols, LANES), vcols)
    other_cols = pl.ds(pl.multiple_of(other * vcols, LANES), vcols)

    def half_at(which):
        return pl.ds(which * half, half)

    ends, slot_of, rank_of = [], [], []

    def read_tables():
        for at in range(7, 11):
            local[at].wait()
        run = jnp.int32(0)
        for r in range(requests):
            run = run + lengths[r]
            ends.append(run)
            adapter = adapters[r]
            slot_of.append(slots[adapter])
            rank_of.append(ranks[adapter])

    def request_at(position):
        found = jnp.zeros(position.shape, jnp.int32)
        for r in range(requests):
            found = found + (position >= ends[r]).astype(jnp.int32)
        return found

    def token_facts(first, count):
        row = lax.broadcasted_iota(jnp.int32, (count * part, 1), 0)
        position = (first + row // part) * tok + o * part + row % part
        req = request_at(position)
        slot_t = jnp.zeros(row.shape, jnp.int32)
        rank_t = jnp.ones(row.shape, jnp.int32)
        for r in range(requests):
            slot_t = jnp.where(req == r, slot_of[r], slot_t)
            rank_t = jnp.where(req == r, rank_of[r], rank_t)
        return slot_t, rank_t

    def masked(low, slot_t, rank_t, chip):
        column = lax.broadcasted_iota(jnp.int32, low.shape, 1)
        start = (slot_t - chip * panels) * rank_width
        return jnp.where((column >= start) & (column < start + rank_t), low, 0.0).astype(bf16)

    def dot(a, b):
        return jnp.dot(a, b, preferred_element_type=f32)

    def window_of(c):
        at = min(c * chip_rows // LANES * LANES, width - win)
        return at, c * chip_rows - at

    def rows_of(first, count, columns):
        return xb[first : first + count, :, columns].reshape(count * part, columns.size)

    def own_partial(c, first, count, columns):
        slot_t, rank_t = token_facts(first, count)
        at, _ = window_of(c)
        base = dot(rows_of(first, count, pl.ds(at, win)), wbuf[...])
        low = dot(rows_of(first, count, columns), dnt[columns, :low_width])
        raised = dot(masked(low, slot_t, rank_t, c), ucat[:panels].reshape(low_width, vcols2))
        value = base + raised * (adapter_strength / rank_t.astype(f32))
        return value.reshape(count, part, vcols2)

    def hosted_partial(first, count, chip, columns):
        slot_t, rank_t = token_facts(first, count)
        low = dot(rows_of(first, count, columns), dnt[columns, low_width:])
        raised = dot(masked(low, slot_t, rank_t, chip), ucat[panels:].reshape(low_width, vcols2))
        value = raised * (adapter_strength / rank_t.astype(f32))
        at = pl.ds(first, count)
        pown[at] = pown[at] + value.reshape(count, part, vcols2)

    def chunk(q, up):
        at = (up if q < CHUNKS // 2 else 1 - up) * half + (q % 2) * wide
        return pl.ds(at, sizes[q % 2])

    local = [
        pltpu.make_async_copy(x_hbm.at[0, my_rows, :], xr, loc_sem.at[0]),
        pltpu.make_async_copy(gain_hbm, gain, loc_sem.at[1]),
        pltpu.make_async_copy(w_hbm.at[0], wbuf.at[pl.ds(0, slab)], loc_sem.at[2]),
        pltpu.make_async_copy(down_hbm.at[0], dn.at[:, :, my_half], loc_sem.at[3]),
        pltpu.make_async_copy(up_hbm.at[0], ucat.at[pl.ds(0, panels), :, my_cols], loc_sem.at[4]),
        pltpu.make_async_copy(q_hbm.at[0], qb, loc_sem.at[5]),
        pltpu.make_async_copy(k_hbm.at[0], kb.at[s], loc_sem.at[6]),
        pltpu.make_async_copy(lengths_hbm, lengths, loc_sem.at[7]),
        pltpu.make_async_copy(adapters_hbm, adapters, loc_sem.at[8]),
        pltpu.make_async_copy(ranks_hbm, ranks, loc_sem.at[9]),
        pltpu.make_async_copy(slots_hbm, slots, loc_sem.at[10]),
    ]

    def slab_at(c):
        _, pad = window_of(c)
        return pl.ds(pl.multiple_of(pad + o * slab, 16), slab)

    def transpose_panels(source, which, at):
        for piece in range(0, half, half // 3):
            rows = source[:, :, pl.ds(which * half + piece if source.shape[2] == width else piece, half // 3)]
            dnt[pl.ds(which * half + piece, half // 3), at : at + low_width] = rows.reshape(
                low_width, half // 3
            ).T

    def opening(c, greetings, count):
        local[0].start()
        local[1].start()
        w_local = pltpu.make_async_copy(w_hbm.at[0], wbuf.at[slab_at(c)], loc_sem.at[2])
        w_local.start()
        for at in range(3, 11):
            local[at].start()
        for device in greetings:
            greet(device)
        _, pad = window_of(c)
        if pad:
            wbuf[0:pad, :] = jnp.zeros((pad, vcols2), bf16)
        rest = win - pad - chip_rows
        if rest:
            wbuf[win - rest : win, :] = jnp.zeros((rest, vcols2), bf16)
        for t in range(c + 1, n):
            kb[t] = jnp.zeros(kb.shape[1:], bf16)
            vall[t] = jnp.zeros(vall.shape[1:], bf16)
        local[0].wait()
        local[1].wait()
        rows = xr[...].astype(f32)
        inv = lax.rsqrt(jnp.mean(rows * rows, axis=1, keepdims=True) + norm_eps)
        xb[c] = (xr[...].astype(f32) * inv * gain[...]).astype(bf16)
        pl.semaphore_wait(barrier, count)

    def exchange(c, kept):
        w_copy = remote(w_hbm.at[0], wbuf.at[slab_at(c)], ex_send.at[0], ex_recv.at[0], peer(c, other))
        dn_copy = remote(down_hbm.at[0], dn.at[:, :, my_half], ex_send.at[1], ex_recv.at[1], peer(c, other))
        up_copy = remote(
            up_hbm.at[0], ucat.at[pl.ds(0, panels), :, my_cols], ex_send.at[2], ex_recv.at[2], peer(c, other)
        )
        return w_copy, dn_copy, up_copy

    def attend(c):
        keys = kb[...].reshape(total, vcols)
        key_at = lax.broadcasted_iota(jnp.int32, (1, total), 1)
        query_at = c * tok + lax.broadcasted_iota(jnp.int32, (tok, 1), 0)
        live = (key_at <= query_at) & (key_at > query_at - WINDOW)
        live = live & (request_at(query_at) == request_at(key_at))
        for h in range(q_heads):
            kv = h // group
            scores = (
                lax.dot_general(
                    qb[:, h * HEAD_SIZE : (h + 1) * HEAD_SIZE],
                    keys[:, kv * HEAD_SIZE : (kv + 1) * HEAD_SIZE],
                    (((1,), (1,)), ((), ())),
                    preferred_element_type=f32,
                )
                * query_scale
            )
            scores = jnp.where(live, scores, -1e30)
            weights = jnp.exp(scores - jnp.max(scores, axis=1, keepdims=True))
            soft = weights / jnp.sum(weights, axis=1, keepdims=True)
            prob[h] = soft.astype(bf16)

    def mix(c):
        values = vall[...].reshape(total, vcols)
        for h in range(q_heads):
            kv = h // group
            out[:, h * HEAD_SIZE : (h + 1) * HEAD_SIZE] = dot(
                prob[h], values[:, kv * HEAD_SIZE : (kv + 1) * HEAD_SIZE]
            ).astype(bf16)

    per_group = panels // 2
    mine = pl.ds(g * per_group, per_group)
    theirs = pl.ds((1 - g) * per_group, per_group)
    my_up = pl.ds(panels + g * per_group, per_group)
    their_up = pl.ds(panels + (1 - g) * per_group, per_group)
    my_piece = pl.ds(pl.multiple_of(o * rank_part, 16), rank_part)
    other_piece = pl.ds(pl.multiple_of(other * rank_part, 16), rank_part)

    def x_end(c, t, q, up, to):
        at = xb.at[t, :, chunk(q, up)]
        return remote(at, at, x_send.at[0], x_recv.at[q], peer(to))

    def x_across(t, q, up, to, forwarded):
        at = xb.at[t, :, chunk(q, up)]
        index = (7 if forwarded else 4) + min(q, 2)
        return remote(at, at, x_send.at[0], x_recv.at[index], peer(to))

    def x_outward(t, q, up, to, index):
        at = xb.at[t, :, chunk(q, up)]
        return remote(at, at, x_send.at[1], x_recv.at[index], peer(to))

    def k_up(c, t):
        return remote(kb.at[t], kb.at[t], k_send, k_recv.at[t if c == 1 else 0], peer(c + 1))

    def end_program(c):
        low = c < n // 2
        i, j, f = (1, 2, 3) if low else (2, 1, 0)
        inward = int(low)
        kept = 1 - inward
        host_core = inward
        greetings = [peer(c, other), peer(i), peer(i, other)]
        if low:
            greetings += [peer(j), peer(j, other)]
        opening(c, greetings, 3 if low else 5)
        w_copy, dn_copy, up_copy = exchange(c, kept)
        piece_in = remote(
            down_hbm.at[0, mine, other_piece, :], hdn.at[mine, other_piece, :], ph_send.at[1], ph_recv.at[1], peer(c, other)
        )
        piece_z = remote(
            down_hbm.at[0, mine, my_piece, :], hdn.at[mine, my_piece, :], ph_send.at[0], ph_recv.at[0], peer(i)
        )
        piece_on = remote(
            hdn.at[mine, my_piece, :], hdn.at[mine, my_piece, :], ph_send.at[0], ph_recv.at[0], peer(i)
        )
        up_z = remote(up_hbm.at[0, mine], ucat.at[my_up, :, my_cols], uh_send.at[0], uh_recv.at[0], peer(i))

        if not low:
            for core in (o, other):
                pl.semaphore_signal(ready, inc=1, device_id=peer(j, core), device_id_type=pl.DeviceIdType.MESH)
        before = 2 if low else 1
        for q in range(before):
            x_end(c, c, q, inward, i).start()

        @pl.when(o == host_core)
        def _():
            piece_in.start()
            piece_z.start()

        @pl.when(o != host_core)
        def _():
            dn_copy.start()

        w_copy.start()
        up_copy.start()

        @pl.when(o != host_core)
        def _():
            arrived(hdn.at[mine, my_piece, :], ph_recv.at[1])
            piece_on.start()

        if low:
            x_end(c, c, before, inward, i).start()
            before += 1
        up_z.start()
        if c == 0:
            local[6].wait()
            k_up(c, c).start()
        for q in range(before, CHUNKS):
            x_end(c, c, q, inward, i).start()
        for at in (2, 3, 4):
            local[at].wait()
        read_tables()

        @pl.when(o == host_core)
        def _():
            arrived(dn.at[:, :, other_half], ex_recv.at[1])

        transpose_panels(dn, kept, 0)
        arrived(ucat.at[pl.ds(0, panels), :, other_cols], ex_recv.at[2])
        arrived(wbuf.at[pl.ds(0, slab)], ex_recv.at[0])

        def p_copy(t):
            return remote(pbuf.at[t], prec.at[t], p_send.at[0], p_recv.at[t], peer(i))

        def p_core(t):
            return remote(
                pbuf.at[t, :, other_cols], prec.at[t, :, pl.ds(0, vcols)], p_send.at[1], s_recv.at[t], peer(c, other)
            )

        def end_partial(t):
            pbuf[t] = own_partial(c, t, 1, half_at(kept))[0].astype(bf16)
            if t == c or not low:
                p_core(t).start()

        end_partial(c)
        if low:
            p_copy(c).start()
        for index, t in enumerate((i, j, f)):
            arrived(xb.at[t, :, half_at(kept)], x_recv.at[index])
            end_partial(t)
            if low:
                p_copy(t).start()
        if not low:
            for t in range(c):
                p_copy(t).start()
        local[5].wait()
        if not low:
            local[6].wait()
            arrived(kb.at[pl.ds(0, n - 1)], k_recv.at[0])
        attend(c)

        def take(t):
            arrived(prec.at[t, :, pl.ds(0, vcols)], s_recv.at[t])
            arrived(vall.at[t], v_recv.at[t])
            own_rows = vall[t, o].astype(f32) + pbuf[t, :, my_cols].astype(f32)
            other_rows = vall[t, other].astype(f32) + prec[t, :, 0:vcols].astype(f32)
            if t == c:
                arrived(va, d_recv)
                own_rows = own_rows + va[o].astype(f32)
                other_rows = other_rows + va[other].astype(f32)
            vall[t, o] = own_rows.astype(bf16)
            vall[t, other] = other_rows.astype(bf16)

        for t in range(c + 1):
            take(t)
        mix(c)

        sent(wbuf.at[pl.ds(0, slab)], ex_send.at[0])
        sent(ucat.at[pl.ds(0, panels), :, other_cols], ex_send.at[2])
        sent(hdn.at[mine, my_piece, :], ph_send.at[0])

        @pl.when(o == host_core)
        def _():
            sent(hdn.at[mine, my_piece, :], ph_send.at[1])

        @pl.when(o != host_core)
        def _():
            sent(dn.at[:, :, my_half], ex_send.at[1])

        sent(ucat.at[my_up, :, my_cols], uh_send.at[0])
        sent(xb.at[0], x_send.at[0])
        if c == 0:
            sent(kb.at[0], k_send)
            sent(pbuf, p_send.at[0])
            sent(pbuf.at[0, :, other_cols], p_send.at[1])
        else:
            sent(pbuf.at[pl.ds(0, n - 1)], p_send.at[0])
            sent(pbuf.at[:, :, other_cols], p_send.at[1])

    def inner_program(c):
        low = c < n // 2
        e, j, f = (0, 2, 3) if low else (3, 1, 0)
        inward = int(low)
        outward = 1 - inward
        first = min(c, e, j)
        greetings = [peer(c, other), peer(e), peer(e, other), peer(j), peer(c, o, 1 - g)]
        if low:
            greetings += [peer(f), peer(f, other)]
        opening(c, greetings, 5 if low else 7)
        w_copy, dn_copy, up_copy = exchange(c, None)

        def own_across(q):
            x_across(c, q, inward, j, False).start()

        for q in range(CHUNKS // 2):
            own_across(q)
            x_outward(c, q, outward, e, 0).start()
        if not low:
            own_across(2)
            own_across(3)
        w_copy.start()
        dn_copy.start()
        up_copy.start()
        local[6].wait()
        for at in (2, 3, 4):
            local[at].wait()
        read_tables()

        def next_e(q):
            arrived(xb.at[e, :, chunk(q, inward)], x_recv.at[q])
            x_across(e, q, inward, j, True).start()

        def next_j(q):
            arrived(xb.at[j, :, chunk(q, outward)], x_recv.at[4 + q])
            x_outward(j, q, outward, e, 1).start()

        def next_f(q):
            arrived(xb.at[f, :, chunk(q, outward)], x_recv.at[7 + q])
            x_outward(f, q, outward, e, 2).start()

        def piece(which, ranks_at):
            return hdn.at[which, ranks_at, :]

        def pass_on(which, ranks_at, sem, recv, device):
            return remote(piece(which, ranks_at), piece(which, ranks_at), ph_send.at[sem], ph_recv.at[recv], device)

        def pass_up(which, sem, recv, device):
            at = ucat.at[which, :, my_cols]
            return remote(at, at, uh_send.at[sem], uh_recv.at[recv], device)

        def host_z():
            arrived(piece(mine, my_piece), ph_recv.at[0])
            pass_on(mine, my_piece, 0, 1, peer(c, o, 1 - g)).start()
            pass_on(mine, my_piece, 1, 2, peer(c, other)).start()

        def host_up():
            arrived(ucat.at[my_up, :, my_cols], uh_recv.at[0])
            pass_up(my_up, 0, 1, peer(c, o, 1 - g)).start()
            pass_up(my_up, 1, 2, peer(c, other)).start()

        def host_y():
            arrived(piece(theirs, my_piece), ph_recv.at[1])
            pass_on(theirs, my_piece, 1, 3, peer(c, other)).start()
            arrived(ucat.at[their_up, :, my_cols], uh_recv.at[1])
            pass_up(their_up, 1, 3, peer(c, other)).start()

        def host_done():
            arrived(piece(mine, other_piece), ph_recv.at[2])
            arrived(piece(theirs, other_piece), ph_recv.at[3])
            transpose_panels(hdn, inward, low_width)
            arrived(ucat.at[my_up, :, other_cols], uh_recv.at[2])
            arrived(ucat.at[their_up, :, other_cols], uh_recv.at[3])

        def own_weights():
            arrived(dn.at[:, :, other_half], ex_recv.at[1])
            transpose_panels(dn, outward, 0)
            transpose_panels(dn, inward, 0)
            arrived(ucat.at[pl.ds(0, panels), :, other_cols], ex_recv.at[2])
            arrived(wbuf.at[pl.ds(0, slab)], ex_recv.at[0])

        def rest_of_j():
            arrived(xb.at[j, :, half_at(inward)], x_recv.at[6])

        def rest_of_f():
            arrived(xb.at[f, :, half_at(inward)], x_recv.at[9])

        def own(at, count):
            pown[at : at + count] = own_partial(c, at, count, pl.ds(0, width))

        def hosted(at, count):
            hosted_partial(at, count, e, half_at(inward))

        def s_copy(t):
            return remote(sbuf.at[t], srec.at[t], s_send, s_recv.at[t], peer(j))

        def s_far(t, core):
            cols = pl.ds(core * vcols, vcols)
            return remote(sbuf.at[t, :, cols], va.at[o], s_send, d_recv, peer(f, core))

        def v_end(t, core):
            cols = pl.ds(core * vcols, vcols)
            return remote(vbuf.at[t, :, cols], vall.at[t, o], v_send.at[0], v_recv.at[t], peer(e, core))

        def v_core(t):
            return remote(vx.at[t, :, other_cols], vall.at[t, o], v_send.at[1], v_recv.at[t], peer(c, other))

        def give_end(t):
            v_end(t, 0).start()
            v_end(t, 1).start()

        def keep(t, value):
            vx[t] = value.astype(bf16)
            v_core(t).start()
            vall[t, o] = vx[t, :, my_cols]

        def early(t):
            vbuf[t] = pown[t].astype(bf16)
            give_end(t)

        def add_end(t):
            arrived(prec.at[t], p_recv.at[t])
            value = pown[t] + prec[t].astype(f32)
            sbuf[t] = value.astype(bf16)
            if t == f:
                if low:
                    pl.semaphore_wait(ready, 2)
                s_far(t, 0).start()
                s_far(t, 1).start()
            if t != f or not low:
                s_copy(t).start()
            return value

        def relay(t):
            arrived(srec.at[t], s_recv.at[t])
            value = pown[t] + srec[t].astype(f32)
            vbuf[t] = value.astype(bf16)
            give_end(t)
            if t == c:
                arrived(prec.at[t], p_recv.at[t])
            keep(t, value + prec[t].astype(f32))

        def next_k(t):
            arrived(kb.at[t], k_recv.at[t])
            k_up(c, t).start()

        if low:
            next_e(0)
            next_e(1)
            k_up(c, c).start()
            own_across(2)
            own_weights()
            next_j(0)
            next_j(1)
            host_z()
            rest_of_j()
            next_e(2)
            own_across(3)
            host_up()
            next_f(0)
            next_k(0)
            next_e(3)
            own(first, 3)
            next_f(1)
            host_y()
            host_done()
            hosted(first, 3)
            early(e)
            for t in range(3):
                pown[t] = add_end(t)
            local[5].wait()
            attend(c)
            rest_of_f()
            own(f, 1)
            hosted(f, 1)
            add_end(f)
            for t in (1, 0):
                arrived(srec.at[t], s_recv.at[t])
                keep(t, pown[t] + srec[t].astype(f32))
        else:
            own_weights()
            next_j(0)
            next_j(1)
            next_e(0)
            next_f(0)
            next_f(1)
            k_up(c, c).start()
            host_z()
            host_up()
            next_e(1)
            next_k(1)
            next_e(2)
            next_e(3)
            host_y()
            own(c, 2)
            host_done()
            hosted(c, 2)
            early(e)
            next_k(0)
            rest_of_f()
            own(f, 1)
            hosted(f, 1)
            add_end(f)
            relay(f)
            rest_of_j()
            own(j, 1)
            hosted(j, 1)
            add_end(j)
            relay(j)
            relay(c)
            local[5].wait()
            attend(c)
        for t in range(c + 1):
            arrived(vall.at[t, other], v_recv.at[t])
        mix(c)

        sent(wbuf.at[pl.ds(0, slab)], ex_send.at[0])
        sent(dn.at[:, :, my_half], ex_send.at[1])
        sent(ucat.at[pl.ds(0, panels), :, other_cols], ex_send.at[2])
        sent(xb.at[pl.ds(0, 2)], x_send.at[0])
        sent(xb.at[pl.ds(0, 3), :, half_at(0)], x_send.at[1])
        sent(piece(mine, my_piece), ph_send.at[0])
        sent(hdn.at[:, my_piece, :], ph_send.at[1])
        sent(ucat.at[my_up, :, my_cols], uh_send.at[0])
        sent(ucat.at[pl.ds(panels, panels), :, my_cols], uh_send.at[1])
        sent(kb.at[pl.ds(0, c + 1)], k_send)
        if low:
            sent(sbuf, s_send)
            sent(vbuf.at[0], v_send.at[0])
        else:
            sent(sbuf.at[pl.ds(0, 3)], s_send)
            sent(vbuf, v_send.at[0])
        sent(vx.at[pl.ds(0, c + 1), :, pl.ds(0, vcols)], v_send.at[1])

    for c in range(n):

        @pl.when(s == c)
        def _():
            ends.clear()
            slot_of.clear()
            rank_of.clear()
            if c in (0, n - 1):
                end_program(c)
            else:
                inner_program(c)


def fused(
    n,
    layer_input_rows,
    encoded_query_rows,
    encoded_key_rows,
    layer_norm_gain,
    base_value_matrix,
    adapter_down_panels,
    adapter_up_panels,
    request_token_lengths,
    adapter_per_request,
    rank_per_adapter,
    slot_per_adapter,
):
    f32, bf16 = jnp.float32, jnp.bfloat16
    tok, width = layer_input_rows.shape[1:]
    part, half = tok // 2, width // 2
    panels, _, rank_width = adapter_down_panels.shape[1:]
    vcols = adapter_up_panels.shape[3]
    qcols = encoded_query_rows.shape[2]
    chip_rows = width // n
    pads = [i * chip_rows % LANES for i in range(n)]
    win = -(-(max(pads) + chip_rows) // LANES) * LANES
    total = n * tok
    dma = pltpu.SemaphoreType.DMA
    any_spec = pl.BlockSpec(memory_space=pl.ANY)
    return pl.pallas_call(
        functools.partial(kernel, n),
        out_shape=pltpu.VMEM(encoded_query_rows.shape[1:], bf16),
        in_specs=[any_spec] * 11,
        out_specs=pl.BlockSpec(memory_space=pltpu.VMEM),
        scratch_shapes=[
            pltpu.SMEM(request_token_lengths.shape, jnp.int32),
            pltpu.SMEM(adapter_per_request.shape, jnp.int32),
            pltpu.SMEM(rank_per_adapter.shape, jnp.int32),
            pltpu.SMEM(slot_per_adapter.shape, jnp.int32),
            pltpu.VMEM((part, width), bf16),
            pltpu.VMEM((1, width), f32),
            pltpu.VMEM((n, part, width), bf16),
            pltpu.VMEM((win, 2 * vcols), bf16),
            pltpu.VMEM((panels, rank_width, width), bf16),
            pltpu.VMEM((panels, rank_width, half), bf16),
            pltpu.VMEM((width, 2 * panels * rank_width), bf16),
            pltpu.VMEM((2 * panels, rank_width, 2 * vcols), bf16),
            pltpu.VMEM((tok, qcols), bf16),
            pltpu.VMEM((n, tok, vcols), bf16),
            pltpu.VMEM((n, part, 2 * vcols), f32),
            pltpu.VMEM((n, part, 2 * vcols), bf16),
            pltpu.VMEM((n, part, 2 * vcols), bf16),
            pltpu.VMEM((n, part, 2 * vcols), bf16),
            pltpu.VMEM((n, part, 2 * vcols), bf16),
            pltpu.VMEM((n, part, 2 * vcols), bf16),
            pltpu.VMEM((n, part, 2 * vcols), bf16),
            pltpu.VMEM((n, 2, part, vcols), bf16),
            pltpu.VMEM((2, part, vcols), bf16),
            pltpu.VMEM((qcols // HEAD_SIZE, tok, total), bf16),
            dma((11,)),
            dma((2,)),
            dma((10,)),
            dma((3,)),
            dma((3,)),
            dma((2,)),
            dma((4,)),
            dma((2,)),
            dma((4,)),
            dma,
            dma((2,)),
            dma((2,)),
            dma((n,)),
            dma,
            dma((n,)),
            dma((2,)),
            dma((n,)),
            dma,
            pltpu.SemaphoreType.REGULAR,
        ],
        compiler_params=pltpu.CompilerParams(
            collective_id=0, has_side_effects=True, vmem_limit_bytes=56 * 1024 * 1024
        ),
    )(
        layer_input_rows,
        encoded_query_rows,
        encoded_key_rows,
        layer_norm_gain,
        base_value_matrix,
        jnp.swapaxes(adapter_down_panels, 2, 3),
        adapter_up_panels,
        request_token_lengths,
        adapter_per_request,
        rank_per_adapter,
        slot_per_adapter,
    )[None]


def solution(mesh):
    in_specs = (
        P("segment", ("groups", "seq"), None),
        P("segment", ("groups", "seq"), "owner"),
        P("segment", ("groups", "seq"), "owner"),
        P("segment", None),
        P("segment", ("seq", "owner"), None),
        P("segment", "seq", "owner", None),
        P("segment", "seq", None, "owner"),
        P("groups"),
        P("groups"),
        P(),
        P(),
    )
    out_specs = P("segment", ("groups", "seq"), "owner")
    n = mesh.shape["seq"]
    small = mesh.shape["owner"] == 2 and mesh.shape["groups"] == 2 and n == 4
    return jax.shard_map(
        functools.partial(fused, n) if small else per_device, mesh=mesh, in_specs=in_specs, out_specs=out_specs, check_vma=False
    )
```

```python
import functools

import jax
import jax.numpy as jnp
from jax import lax
from jax.experimental import pallas as pl
from jax.experimental.pallas import tpu as pltpu
from jax.sharding import PartitionSpec as P

WINDOW = 1024
HEADS = 16
KEY_VALUE_HEADS = 8
HEAD_SIZE = 128


query_scale = 168.0 ** (-0.5)
adapter_strength = 32.0
norm_eps = 1e-06


def broadcast(x, axis, root):
    mine = lax.axis_index(axis) == root
    return lax.psum(jnp.where(mine, x, jnp.zeros_like(x)), axis)


def from_behind(value, axis, steps):
    count = lax.axis_size(axis)
    first, last = (max(0, -steps), min(count, count - steps))
    return lax.ppermute(value, axis, [(source, source + steps) for source in range(first, last)])


def per_device(
    layer_input_rows,
    encoded_query_rows,
    encoded_key_rows,
    layer_norm_gain,
    base_value_matrix,
    adapter_down_panels,
    adapter_up_panels,
    request_token_lengths,
    adapter_per_request,
    rank_per_adapter,
    slot_per_adapter,
):
    hidden = layer_input_rows[0]
    row_count = hidden.shape[0]
    seq_now = lax.axis_index("seq")
    owner_now = lax.axis_index("owner")
    reach_count = min(WINDOW // row_count, lax.axis_size("seq") - 1)
    requests = request_token_lengths.shape[0]
    library = slot_per_adapter.shape[0]
    slots_here = adapter_down_panels.shape[1]
    rows_halved = adapter_down_panels.shape[2]
    rank_span_width = adapter_down_panels.shape[3]
    key_value_halved = adapter_up_panels.shape[3]
    group_size = HEADS // KEY_VALUE_HEADS
    request_ends = jnp.cumsum(request_token_lengths)
    position = seq_now * row_count + jnp.arange(row_count, dtype=jnp.int32)
    context = seq_now * row_count + jnp.arange(-reach_count * row_count, row_count, dtype=jnp.int32)
    request_lookup = jnp.sum((position[:, None] >= request_ends[None, :]).astype(jnp.int32), axis=1)
    request_ctx = jnp.sum((context[:, None] >= request_ends[None, :]).astype(jnp.int32), axis=1)
    live_mask = (context[None, :] <= position[:, None]) & (
        context[None, :] > position[:, None] - WINDOW
    )
    live_mask = (
        live_mask & (context[None, :] >= 0) & (request_ctx[None, :] == request_lookup[:, None])
    )
    choose = adapter_per_request[:, None] == jnp.arange(library, dtype=jnp.int32)[None, :]
    slot_of = jnp.sum(jnp.where(choose, slot_per_adapter[None, :], 0), axis=1)
    rank_lookup = jnp.sum(jnp.where(choose, rank_per_adapter[None, :], 0), axis=1)
    scale_lookup = adapter_strength / rank_lookup.astype(jnp.float32)
    in_request = request_lookup[:, None] == jnp.arange(requests, dtype=jnp.int32)[None, :]
    column_live = jnp.arange(rank_span_width, dtype=jnp.int32)[None, :] < rank_lookup[:, None]
    row_gain_weight = jnp.where(in_request, scale_lookup[None, :], jnp.float32(0.0))
    down_panel_here = adapter_down_panels[0]
    up_panel_here = adapter_up_panels[0]
    queries = encoded_query_rows[0]
    keys_own = encoded_key_rows[0]
    key_heads = keys_own.shape[1] // HEAD_SIZE
    wide_rows = hidden.astype(jnp.float32)
    normalized_rows = wide_rows * lax.rsqrt(
        jnp.mean(wide_rows * wide_rows, axis=1, keepdims=True) + norm_eps
    )
    normalized_rows = (normalized_rows * layer_norm_gain[0][None, :]).astype(jnp.bfloat16)
    normed_half = lax.dynamic_slice_in_dim(normalized_rows, owner_now * rows_halved, rows_halved, 1)
    full_value = jnp.dot(
        normalized_rows,
        lax.all_gather(base_value_matrix[0], ("seq", "owner"), axis=0, tiled=True),
        preferred_element_type=jnp.float32,
    )
    value_base_rows = lax.dynamic_slice_in_dim(
        full_value, owner_now * key_value_halved, key_value_halved, 1
    )

    def fetch_one(reduced_rows, request_index):
        owner_slot = slot_of[request_index]
        holder = owner_slot // slots_here
        local_slot = owner_slot % slots_here
        down_local = lax.dynamic_slice_in_dim(down_panel_here, local_slot, 1, 0)
        up_local = lax.dynamic_slice_in_dim(up_panel_here, local_slot, 1, 0)
        down_piece, up_piece = (
            broadcast(down_local, "seq", holder),
            broadcast(up_local, "seq", holder),
        )
        keep_mask = in_request[:, request_index][:, None] & column_live[request_index][None, :]
        matrix_product = jnp.dot(normed_half, down_piece[0], preferred_element_type=jnp.float32)
        return (reduced_rows + jnp.where(keep_mask, matrix_product, jnp.float32(0.0)), up_piece[0])

    start_low = jnp.zeros((row_count, rank_span_width), jnp.float32)
    reduced_rows, panels_up = lax.scan(fetch_one, start_low, jnp.arange(requests, dtype=jnp.int32))
    reduced_rows = lax.psum(reduced_rows, "owner").astype(jnp.bfloat16)
    raised_rows = jnp.einsum(
        "tr,qrk->qtk", reduced_rows, panels_up, preferred_element_type=jnp.float32
    )
    adapter_value = jnp.sum(row_gain_weight.T[:, :, None] * raised_rows, axis=0)
    value_output_rows = (value_base_rows + adapter_value).astype(jnp.bfloat16)
    key_parts = []
    value_parts = []
    for shift_by in range(reach_count, 0, -1):
        key_piece, value_piece = from_behind((keys_own, value_output_rows), "seq", shift_by)
        key_parts.append(key_piece)
        value_parts.append(value_piece)
    keys_all = jnp.concatenate(key_parts + [keys_own], axis=0)
    values_all = jnp.concatenate(value_parts + [value_output_rows], axis=0)
    query_view = queries.reshape(row_count, key_heads, group_size, HEAD_SIZE)
    key_view = keys_all.reshape(-1, key_heads, HEAD_SIZE)
    value_view = values_all.reshape(-1, key_heads, HEAD_SIZE)
    head_outputs = []
    for head_index in range(key_heads):
        query_head = query_view[:, head_index]
        scores = (
            jnp.einsum(
                "tcd,jd->ctj",
                query_head,
                key_view[:, head_index],
                preferred_element_type=jnp.float32,
            )
            * query_scale
        )
        scores = jnp.where(live_mask[None], scores, jnp.float32(-1e30))
        row_max = jnp.max(scores, axis=-1, keepdims=True)
        weights = jnp.exp(scores - row_max)
        row_total = jnp.sum(weights, axis=-1, keepdims=True)
        softmax_rows = (weights / row_total).astype(jnp.bfloat16)
        mixed = jnp.einsum(
            "ctj,jd->tcd",
            softmax_rows,
            value_view[:, head_index],
            preferred_element_type=jnp.float32,
        )
        head_outputs.append(mixed.astype(jnp.bfloat16).reshape(row_count, group_size * HEAD_SIZE))
    result = jnp.concatenate(head_outputs, axis=1)
    return result[None]


LANES = 128
CHUNKS = 4


def kernel(
    n,
    x_hbm,
    q_hbm,
    k_hbm,
    gain_hbm,
    w_hbm,
    down_hbm,
    up_hbm,
    lengths_hbm,
    adapters_hbm,
    ranks_hbm,
    slots_hbm,
    out,
    lengths,
    adapters,
    ranks,
    slots,
    xr,
    gain,
    xb,
    wbuf,
    dn,
    hdn,
    dnt,
    ucat,
    qb,
    kb,
    pown,
    lowa,
    pbuf,
    prec,
    sbuf,
    srec,
    vbuf,
    vx,
    vall,
    va,
    prob,
    loc_sem,
    x_send,
    x_recv,
    ex_send,
    ex_recv,
    ph_send,
    ph_recv,
    uh_send,
    uh_recv,
    k_send,
    k_recv,
    p_send,
    p_recv,
    s_send,
    s_recv,
    v_send,
    v_recv,
    d_recv,
    d_send,
    ready,
):
    f32, bf16 = jnp.float32, jnp.bfloat16
    s = lax.axis_index("seq")
    o = lax.axis_index("owner")
    g = lax.axis_index("groups")
    other = 1 - o
    tok, width = x_hbm.shape[1], x_hbm.shape[2]
    part = tok // 2
    half = width // 2
    win, vcols2 = wbuf.shape
    vcols = vcols2 // 2
    slab = w_hbm.shape[1]
    panels, rank_width = dn.shape[0], dn.shape[1]
    low_width = panels * rank_width
    rank_part = rank_width // 2
    chip_rows = width // n
    requests = lengths.shape[0]
    total = n * tok
    group = HEADS // KEY_VALUE_HEADS
    q_heads = qb.shape[1] // HEAD_SIZE
    wide = -(-half // (2 * LANES)) * LANES
    sizes = (wide, half - wide)

    def peer(seq, owner=None, groups=None):
        return {
            "seq": seq,
            "owner": o if owner is None else owner,
            "groups": g if groups is None else groups,
        }

    def remote(src, dst, send, recv, device):
        return pltpu.make_async_remote_copy(
            src_ref=src,
            dst_ref=dst,
            send_sem=send,
            recv_sem=recv,
            device_id=device,
            device_id_type=pl.DeviceIdType.MESH,
        )

    def arrived(ref, sem):
        remote(ref, ref, sem, sem, peer(s, other)).wait_recv()

    def sent(ref, sem):
        remote(ref, ref, sem, sem, peer(s, other)).wait_send()

    barrier = pltpu.get_barrier_semaphore()

    def greet(device):
        pl.semaphore_signal(barrier, inc=1, device_id=device, device_id_type=pl.DeviceIdType.MESH)

    my_rows = pl.ds(pl.multiple_of(o * part, 16), part)
    my_half = pl.ds(pl.multiple_of(o * half, LANES), half)
    other_half = pl.ds(pl.multiple_of(other * half, LANES), half)
    my_cols = pl.ds(pl.multiple_of(o * vcols, LANES), vcols)
    other_cols = pl.ds(pl.multiple_of(other * vcols, LANES), vcols)

    def half_at(which):
        return pl.ds(which * half, half)

    ends, slot_of, rank_of = [], [], []

    def read_tables():
        for at in range(7, 11):
            local[at].wait()
        run = jnp.int32(0)
        for r in range(requests):
            run = run + lengths[r]
            ends.append(run)
            adapter = adapters[r]
            slot_of.append(slots[adapter])
            rank_of.append(ranks[adapter])

    def request_at(position):
        found = jnp.zeros(position.shape, jnp.int32)
        for r in range(requests):
            found = found + (position >= ends[r]).astype(jnp.int32)
        return found

    def token_facts(first, count):
        row = lax.broadcasted_iota(jnp.int32, (count * part, 1), 0)
        position = (first + row // part) * tok + o * part + row % part
        req = request_at(position)
        slot_t = jnp.zeros(row.shape, jnp.int32)
        rank_t = jnp.ones(row.shape, jnp.int32)
        for r in range(requests):
            slot_t = jnp.where(req == r, slot_of[r], slot_t)
            rank_t = jnp.where(req == r, rank_of[r], rank_t)
        return slot_t, rank_t

    def masked(low, slot_t, rank_t, chip):
        column = lax.broadcasted_iota(jnp.int32, low.shape, 1)
        start = (slot_t - chip * panels) * rank_width
        return jnp.where((column >= start) & (column < start + rank_t), low, 0.0).astype(bf16)

    def dot(a, b):
        return jnp.dot(a, b, preferred_element_type=f32)

    def window_of(c):
        at = min(c * chip_rows // LANES * LANES, width - win)
        return at, c * chip_rows - at

    def rows_of(first, count, columns):
        return xb[first : first + count, :, columns].reshape(count * part, columns.size)

    def end_value(c, t, columns):
        slot_t, rank_t = token_facts(t, 1)
        at, _ = window_of(c)
        base = dot(xb[t, :, pl.ds(at, win)], wbuf[...])
        low = masked(dot(xb[t, :, columns], dnt[columns, :low_width]), slot_t, rank_t, c)
        raised = dot(low, ucat[:panels].reshape(low_width, vcols2))
        return base + raised * (adapter_strength / rank_t.astype(f32))

    def first_part(c, first, count, columns):
        at, _ = window_of(c)
        base = dot(rows_of(first, count, pl.ds(at, win)), wbuf[...])
        low = dot(rows_of(first, count, columns), dnt[columns, :low_width])
        pown[pl.ds(first, count)] = base.reshape(count, part, vcols2)
        lowa[pl.ds(first, count)] = low.reshape(count, part, low_width)

    def last_part(c, first, count, chip, columns):
        slot_t, rank_t = token_facts(first, count)
        at = pl.ds(first, count)
        both = dot(rows_of(first, count, columns), dnt[columns, :])
        low = lowa[at].reshape(count * part, low_width) + both[:, :low_width]
        low = jnp.concatenate(
            [masked(low, slot_t, rank_t, c), masked(both[:, low_width:], slot_t, rank_t, chip)], axis=1
        )
        raised = dot(low, ucat[...].reshape(2 * low_width, vcols2))
        value = raised * (adapter_strength / rank_t.astype(f32))
        pown[at] = pown[at] + value.reshape(count, part, vcols2)

    def put(ref, t, value):
        for side in range(2):
            ref[t, side] = value[:, side * vcols : (side + 1) * vcols].astype(bf16)

    def get(ref, t):
        return jnp.concatenate([ref[t, 0], ref[t, 1]], axis=1).astype(f32)

    def chunk(q, up):
        at = (up if q < CHUNKS // 2 else 1 - up) * half + (q % 2) * wide
        return pl.ds(at, sizes[q % 2])

    local = [
        pltpu.make_async_copy(x_hbm.at[0, my_rows, :], xr, loc_sem.at[0]),
        pltpu.make_async_copy(gain_hbm, gain, loc_sem.at[1]),
        pltpu.make_async_copy(w_hbm.at[0], wbuf.at[pl.ds(0, slab)], loc_sem.at[2]),
        pltpu.make_async_copy(down_hbm.at[0], dn.at[:, :, my_half], loc_sem.at[3]),
        pltpu.make_async_copy(up_hbm.at[0], ucat.at[pl.ds(0, panels), :, my_cols], loc_sem.at[4]),
        pltpu.make_async_copy(q_hbm.at[0], qb, loc_sem.at[5]),
        pltpu.make_async_copy(k_hbm.at[0], kb.at[s], loc_sem.at[6]),
        pltpu.make_async_copy(lengths_hbm, lengths, loc_sem.at[7]),
        pltpu.make_async_copy(adapters_hbm, adapters, loc_sem.at[8]),
        pltpu.make_async_copy(ranks_hbm, ranks, loc_sem.at[9]),
        pltpu.make_async_copy(slots_hbm, slots, loc_sem.at[10]),
    ]

    def slab_at(c):
        _, pad = window_of(c)
        return pl.ds(pl.multiple_of(pad + o * slab, 16), slab)

    def transpose_panels(source, which, at):
        for piece in range(0, half, half // 3):
            rows = source[:, :, pl.ds(which * half + piece if source.shape[2] == width else piece, half // 3)]
            dnt[pl.ds(which * half + piece, half // 3), at : at + low_width] = rows.reshape(
                low_width, half // 3
            ).T

    def opening(c, greetings, count):
        local[0].start()
        local[1].start()
        w_local = pltpu.make_async_copy(w_hbm.at[0], wbuf.at[slab_at(c)], loc_sem.at[2])
        w_local.start()
        for at in range(3, 11):
            local[at].start()
        for device in greetings:
            greet(device)
        _, pad = window_of(c)
        if pad:
            wbuf[0:pad, :] = jnp.zeros((pad, vcols2), bf16)
        rest = win - pad - chip_rows
        if rest:
            wbuf[win - rest : win, :] = jnp.zeros((rest, vcols2), bf16)
        for t in range(c + 1, n):
            kb[t] = jnp.zeros(kb.shape[1:], bf16)
            vall[t] = jnp.zeros(vall.shape[1:], bf16)
        local[0].wait()
        local[1].wait()
        rows = xr[...].astype(f32)
        inv = lax.rsqrt(jnp.mean(rows * rows, axis=1, keepdims=True) + norm_eps)
        xb[c] = (xr[...].astype(f32) * inv * gain[...]).astype(bf16)
        pl.semaphore_wait(barrier, count)

    def exchange(c, kept):
        w_copy = remote(w_hbm.at[0], wbuf.at[slab_at(c)], ex_send.at[0], ex_recv.at[0], peer(c, other))
        dn_copy = remote(down_hbm.at[0], dn.at[:, :, my_half], ex_send.at[1], ex_recv.at[1], peer(c, other))
        up_copy = remote(
            up_hbm.at[0], ucat.at[pl.ds(0, panels), :, my_cols], ex_send.at[2], ex_recv.at[2], peer(c, other)
        )
        return w_copy, dn_copy, up_copy

    def attend(c):
        keys = kb[...].reshape(total, vcols)
        key_at = lax.broadcasted_iota(jnp.int32, (1, total), 1)
        query_at = c * tok + lax.broadcasted_iota(jnp.int32, (tok, 1), 0)
        live = (key_at <= query_at) & (key_at > query_at - WINDOW)
        live = live & (request_at(query_at) == request_at(key_at))
        for h in range(q_heads):
            kv = h // group
            scores = (
                lax.dot_general(
                    qb[:, h * HEAD_SIZE : (h + 1) * HEAD_SIZE],
                    keys[:, kv * HEAD_SIZE : (kv + 1) * HEAD_SIZE],
                    (((1,), (1,)), ((), ())),
                    preferred_element_type=f32,
                )
                * query_scale
            )
            scores = jnp.where(live, scores, -1e30)
            weights = jnp.exp(scores - jnp.max(scores, axis=1, keepdims=True))
            soft = weights / jnp.sum(weights, axis=1, keepdims=True)
            prob[h] = soft.astype(bf16)

    def mix(c):
        values = vall[...].reshape(total, vcols)
        for h in range(q_heads):
            kv = h // group
            out[:, h * HEAD_SIZE : (h + 1) * HEAD_SIZE] = dot(
                prob[h], values[:, kv * HEAD_SIZE : (kv + 1) * HEAD_SIZE]
            ).astype(bf16)

    per_group = panels // 2
    mine = pl.ds(g * per_group, per_group)
    theirs = pl.ds((1 - g) * per_group, per_group)
    my_up = pl.ds(panels + g * per_group, per_group)
    their_up = pl.ds(panels + (1 - g) * per_group, per_group)
    my_piece = pl.ds(pl.multiple_of(o * rank_part, 16), rank_part)
    other_piece = pl.ds(pl.multiple_of(other * rank_part, 16), rank_part)

    def x_end(c, t, q, up, to):
        at = xb.at[t, :, chunk(q, up)]
        return remote(at, at, x_send.at[0], x_recv.at[q], peer(to))

    def x_across(t, q, up, to, forwarded):
        at = xb.at[t, :, chunk(q, up)]
        index = (7 if forwarded else 4) + min(q, 2)
        return remote(at, at, x_send.at[0], x_recv.at[index], peer(to))

    def x_outward(t, q, up, to, index):
        at = xb.at[t, :, chunk(q, up)]
        return remote(at, at, x_send.at[1], x_recv.at[index], peer(to))

    def k_up(c, t):
        return remote(kb.at[t], kb.at[t], k_send, k_recv.at[t if c == 1 else 0], peer(c + 1))

    def end_program(c):
        low = c < n // 2
        i, j, f = (1, 2, 3) if low else (2, 1, 0)
        inward = int(low)
        kept = 1 - inward
        host_core = inward
        greetings = [peer(c, other), peer(i), peer(i, other)]
        if low:
            greetings += [peer(j), peer(j, other)]
        opening(c, greetings, 3 if low else 5)
        w_copy, dn_copy, up_copy = exchange(c, kept)
        piece_in = remote(
            down_hbm.at[0, mine, other_piece, :], hdn.at[mine, other_piece, :], ph_send.at[1], ph_recv.at[1], peer(c, other)
        )
        piece_z = remote(
            down_hbm.at[0, mine, my_piece, :], hdn.at[mine, my_piece, :], ph_send.at[0], ph_recv.at[0], peer(i)
        )
        piece_on = remote(
            hdn.at[mine, my_piece, :], hdn.at[mine, my_piece, :], ph_send.at[0], ph_recv.at[0], peer(i)
        )
        up_z = remote(up_hbm.at[0, mine], ucat.at[my_up, :, my_cols], uh_send.at[0], uh_recv.at[0], peer(i))

        if not low:
            for core in (o, other):
                pl.semaphore_signal(ready, inc=1, device_id=peer(j, core), device_id_type=pl.DeviceIdType.MESH)
        before = 2 if low else 1

        def open_rows(opening_count=before):
            for q in range(opening_count):
                x_end(c, c, q, inward, i).start()

        if low:
            open_rows()

        @pl.when(o == host_core)
        def _():
            piece_in.start()
            piece_z.start()
            if not low:
                open_rows()

        @pl.when(o != host_core)
        def _():
            if not low:
                open_rows()
            dn_copy.start()

        w_copy.start()
        up_copy.start()

        @pl.when(o != host_core)
        def _():
            arrived(hdn.at[mine, my_piece, :], ph_recv.at[1])
            piece_on.start()

        if low:
            x_end(c, c, before, inward, i).start()
            before += 1
        up_z.start()
        if c == 0:
            local[6].wait()
            k_up(c, c).start()
        for q in range(before, CHUNKS):
            x_end(c, c, q, inward, i).start()
        for at in (2, 3, 4):
            local[at].wait()
        read_tables()

        @pl.when(o == host_core)
        def _():
            arrived(dn.at[:, :, other_half], ex_recv.at[1])

        transpose_panels(dn, kept, 0)
        arrived(ucat.at[pl.ds(0, panels), :, other_cols], ex_recv.at[2])
        arrived(wbuf.at[pl.ds(0, slab)], ex_recv.at[0])

        def p_copy(t):
            return remote(pbuf.at[t], prec.at[t], p_send.at[0], p_recv.at[t], peer(i))

        def p_core(t):
            return remote(
                pbuf.at[t, other], prec.at[t, 0], p_send.at[1], s_recv.at[t], peer(c, other)
            )

        def end_partial(t):
            put(pbuf, t, end_value(c, t, half_at(kept)))
            if t == c or not low:
                p_core(t).start()

        end_partial(c)
        if low:
            p_copy(c).start()
        for index, t in enumerate((i, j, f)):
            arrived(xb.at[t, :, half_at(kept)], x_recv.at[index])
            end_partial(t)
            if low:
                p_copy(t).start()
        if not low:
            for t in range(c):
                p_copy(t).start()
        local[5].wait()
        if not low:
            local[6].wait()
            arrived(kb.at[pl.ds(0, n - 1)], k_recv.at[0])
        attend(c)

        def take(t):
            arrived(prec.at[t, 0], s_recv.at[t])
            arrived(vall.at[t], v_recv.at[t])
            own_rows = vall[t, o].astype(f32) + pbuf[t, o].astype(f32)
            other_rows = vall[t, other].astype(f32) + prec[t, 0].astype(f32)
            if t == c or t == i:
                at = int(t != c)
                arrived(va.at[at], d_recv.at[at])
                own_rows = own_rows + va[at, o].astype(f32)
                other_rows = other_rows + va[at, other].astype(f32)
            vall[t, o] = own_rows.astype(bf16)
            vall[t, other] = other_rows.astype(bf16)

        for t in range(c + 1):
            take(t)
        mix(c)

        sent(wbuf.at[pl.ds(0, slab)], ex_send.at[0])
        sent(ucat.at[pl.ds(0, panels), :, other_cols], ex_send.at[2])
        sent(hdn.at[mine, my_piece, :], ph_send.at[0])

        @pl.when(o == host_core)
        def _():
            sent(hdn.at[mine, my_piece, :], ph_send.at[1])

        @pl.when(o != host_core)
        def _():
            sent(dn.at[:, :, my_half], ex_send.at[1])

        sent(ucat.at[my_up, :, my_cols], uh_send.at[0])
        sent(xb.at[0], x_send.at[0])
        if c == 0:
            sent(kb.at[0], k_send)
            sent(pbuf, p_send.at[0])
            sent(pbuf.at[0, 0], p_send.at[1])
        else:
            sent(pbuf.at[pl.ds(0, n - 1)], p_send.at[0])
            sent(pbuf.at[:, 0], p_send.at[1])

    def inner_program(c):
        low = c < n // 2
        e, j, f = (0, 2, 3) if low else (3, 1, 0)
        inward = int(low)
        outward = 1 - inward
        first = min(c, e, j)
        greetings = [peer(c, other), peer(e), peer(e, other), peer(j), peer(c, o, 1 - g)]
        if low:
            greetings += [peer(f), peer(f, other)]
        opening(c, greetings, 5 if low else 7)
        w_copy, dn_copy, up_copy = exchange(c, None)

        def own_across(q):
            x_across(c, q, inward, j, False).start()

        for q in range(CHUNKS // 2):
            own_across(q)
            x_outward(c, q, outward, e, 0).start()
        if not low:
            own_across(2)
            own_across(3)
        w_copy.start()
        dn_copy.start()
        up_copy.start()
        local[6].wait()
        for at in (2, 3, 4):
            local[at].wait()
        read_tables()

        def next_e(q):
            arrived(xb.at[e, :, chunk(q, inward)], x_recv.at[q])
            x_across(e, q, inward, j, True).start()

        def next_j(q):
            arrived(xb.at[j, :, chunk(q, outward)], x_recv.at[4 + q])
            x_outward(j, q, outward, e, 1).start()

        def next_f(q):
            arrived(xb.at[f, :, chunk(q, outward)], x_recv.at[7 + q])
            x_outward(f, q, outward, e, 2).start()

        def piece(which, ranks_at):
            return hdn.at[which, ranks_at, :]

        def pass_on(which, ranks_at, sem, recv, device):
            return remote(piece(which, ranks_at), piece(which, ranks_at), ph_send.at[sem], ph_recv.at[recv], device)

        def pass_up(which, sem, recv, device):
            at = ucat.at[which, :, my_cols]
            return remote(at, at, uh_send.at[sem], uh_recv.at[recv], device)

        def host_z():
            arrived(piece(mine, my_piece), ph_recv.at[0])
            pass_on(mine, my_piece, 0, 1, peer(c, o, 1 - g)).start()
            pass_on(mine, my_piece, 1, 2, peer(c, other)).start()

        def host_up():
            arrived(ucat.at[my_up, :, my_cols], uh_recv.at[0])
            pass_up(my_up, 0, 1, peer(c, o, 1 - g)).start()
            pass_up(my_up, 1, 2, peer(c, other)).start()

        def host_y():
            arrived(piece(theirs, my_piece), ph_recv.at[1])
            pass_on(theirs, my_piece, 1, 3, peer(c, other)).start()

        def host_yu():
            arrived(ucat.at[their_up, :, my_cols], uh_recv.at[1])
            pass_up(their_up, 1, 3, peer(c, other)).start()

        def host_done():
            arrived(piece(mine, other_piece), ph_recv.at[2])
            arrived(piece(theirs, other_piece), ph_recv.at[3])
            transpose_panels(hdn, inward, low_width)
            arrived(ucat.at[my_up, :, other_cols], uh_recv.at[2])
            arrived(ucat.at[their_up, :, other_cols], uh_recv.at[3])

        def own_weights():
            arrived(dn.at[:, :, other_half], ex_recv.at[1])
            transpose_panels(dn, outward, 0)
            transpose_panels(dn, inward, 0)
            arrived(ucat.at[pl.ds(0, panels), :, other_cols], ex_recv.at[2])
            arrived(wbuf.at[pl.ds(0, slab)], ex_recv.at[0])

        def rest_of_j():
            arrived(xb.at[j, :, half_at(inward)], x_recv.at[6])

        def rest_of_f():
            arrived(xb.at[f, :, half_at(inward)], x_recv.at[9])

        def own(at, count):
            first_part(c, at, count, half_at(outward))

        def hosted(at, count):
            last_part(c, at, count, e, half_at(inward))

        def s_copy(t):
            return remote(sbuf.at[t], srec.at[t], s_send, s_recv.at[t], peer(j))

        def s_far(t, core):
            at = int(t != f)
            return remote(sbuf.at[t, core], va.at[at, o], d_send, d_recv.at[at], peer(f, core))

        def v_end(t, core):
            return remote(vbuf.at[t, core], vall.at[t, o], v_send.at[0], v_recv.at[t], peer(e, core))

        def v_core(t):
            return remote(vx.at[t, other], vall.at[t, o], v_send.at[1], v_recv.at[t], peer(c, other))

        def give_end(t):
            v_end(t, 0).start()
            v_end(t, 1).start()

        def keep(t, value):
            put(vx, t, value)
            v_core(t).start()
            vall[t, o] = vx[t, o]

        def early(t):
            put(vbuf, t, pown[t])
            give_end(t)

        def add_end(t):
            arrived(prec.at[t], p_recv.at[t])
            value = pown[t] + get(prec, t)
            put(sbuf, t, value)
            if t == f or (low and t == j):
                if low and t == j:
                    pl.semaphore_wait(ready, 2)
                s_far(t, 0).start()
                s_far(t, 1).start()
            if t != f or not low:
                s_copy(t).start()
            return value

        def relay(t):
            arrived(srec.at[t], s_recv.at[t])
            value = pown[t] + get(srec, t)
            if t == c:
                arrived(prec.at[t], p_recv.at[t])
            else:
                put(vbuf, t, value)
                give_end(t)
            keep(t, value + get(prec, t))

        def next_k(t):
            arrived(kb.at[t], k_recv.at[t])
            k_up(c, t).start()

        if low:
            next_e(0)
            next_e(1)
            k_up(c, c).start()
            own_across(2)
            own_weights()
            next_j(0)
            next_j(1)
            host_z()
            rest_of_j()
            next_e(2)
            own_across(3)
            host_up()
            next_f(0)
            next_k(0)
            host_y()
            next_e(3)
            host_yu()
            next_f(1)
            own(first, 3)
            host_done()
            hosted(first, 3)
            early(e)
            for t in range(3):
                pown[t] = add_end(t)
            own(f, 1)
            local[5].wait()
            attend(c)
            rest_of_f()
            hosted(f, 1)
            add_end(f)
            for t in (1, 0):
                arrived(srec.at[t], s_recv.at[t])
                keep(t, pown[t] + get(srec, t))
        else:
            own_weights()
            next_j(0)
            next_j(1)
            host_z()
            next_f(0)
            next_e(0)
            next_f(1)
            k_up(c, c).start()
            host_up()
            next_k(1)
            own(f, 2)
            next_e(1)
            host_y()
            next_e(2)
            host_yu()
            next_e(3)
            own(c, 2)
            host_done()
            hosted(c, 2)
            early(c)
            early(e)
            next_k(0)
            rest_of_f()
            hosted(f, 1)
            add_end(f)
            rest_of_j()
            hosted(j, 1)
            add_end(j)
            relay(f)
            relay(j)
            relay(c)
            local[5].wait()
            attend(c)
        for t in range(c + 1):
            arrived(vall.at[t, other], v_recv.at[t])
        mix(c)

        sent(wbuf.at[pl.ds(0, slab)], ex_send.at[0])
        sent(dn.at[:, :, my_half], ex_send.at[1])
        sent(ucat.at[pl.ds(0, panels), :, other_cols], ex_send.at[2])
        sent(xb.at[pl.ds(0, 2)], x_send.at[0])
        sent(xb.at[pl.ds(0, 3), :, half_at(0)], x_send.at[1])
        sent(piece(mine, my_piece), ph_send.at[0])
        sent(hdn.at[:, my_piece, :], ph_send.at[1])
        sent(ucat.at[my_up, :, my_cols], uh_send.at[0])
        sent(ucat.at[pl.ds(panels, panels), :, my_cols], uh_send.at[1])
        sent(kb.at[pl.ds(0, c + 1)], k_send)
        if low:
            sent(sbuf.at[pl.ds(0, 3)], s_send)
            sent(sbuf.at[pl.ds(0, 2)], d_send)
            sent(vbuf.at[0], v_send.at[0])
        else:
            sent(sbuf.at[pl.ds(0, 2)], s_send)
            sent(sbuf.at[0], d_send)
            sent(vbuf, v_send.at[0])
        sent(vx.at[pl.ds(0, c + 1), 0], v_send.at[1])

    for c in range(n):

        @pl.when(s == c)
        def _():
            ends.clear()
            slot_of.clear()
            rank_of.clear()
            if c in (0, n - 1):
                end_program(c)
            else:
                inner_program(c)


def fused(
    n,
    layer_input_rows,
    encoded_query_rows,
    encoded_key_rows,
    layer_norm_gain,
    base_value_matrix,
    adapter_down_panels,
    adapter_up_panels,
    request_token_lengths,
    adapter_per_request,
    rank_per_adapter,
    slot_per_adapter,
):
    f32, bf16 = jnp.float32, jnp.bfloat16
    tok, width = layer_input_rows.shape[1:]
    part, half = tok // 2, width // 2
    panels, _, rank_width = adapter_down_panels.shape[1:]
    vcols = adapter_up_panels.shape[3]
    qcols = encoded_query_rows.shape[2]
    chip_rows = width // n
    pads = [i * chip_rows % LANES for i in range(n)]
    win = -(-(max(pads) + chip_rows) // LANES) * LANES
    total = n * tok
    dma = pltpu.SemaphoreType.DMA
    any_spec = pl.BlockSpec(memory_space=pl.ANY)
    return pl.pallas_call(
        functools.partial(kernel, n),
        out_shape=pltpu.VMEM(encoded_query_rows.shape[1:], bf16),
        in_specs=[any_spec] * 11,
        out_specs=pl.BlockSpec(memory_space=pltpu.VMEM),
        scratch_shapes=[
            pltpu.SMEM(request_token_lengths.shape, jnp.int32),
            pltpu.SMEM(adapter_per_request.shape, jnp.int32),
            pltpu.SMEM(rank_per_adapter.shape, jnp.int32),
            pltpu.SMEM(slot_per_adapter.shape, jnp.int32),
            pltpu.VMEM((part, width), bf16),
            pltpu.VMEM((1, width), f32),
            pltpu.VMEM((n, part, width), bf16),
            pltpu.VMEM((win, 2 * vcols), bf16),
            pltpu.VMEM((panels, rank_width, width), bf16),
            pltpu.VMEM((panels, rank_width, half), bf16),
            pltpu.VMEM((width, 2 * panels * rank_width), bf16),
            pltpu.VMEM((2 * panels, rank_width, 2 * vcols), bf16),
            pltpu.VMEM((tok, qcols), bf16),
            pltpu.VMEM((n, tok, vcols), bf16),
            pltpu.VMEM((n, part, 2 * vcols), f32),
            pltpu.VMEM((n, part, panels * rank_width), f32),
            pltpu.VMEM((n, 2, part, vcols), bf16),
            pltpu.VMEM((n, 2, part, vcols), bf16),
            pltpu.VMEM((n, 2, part, vcols), bf16),
            pltpu.VMEM((n, 2, part, vcols), bf16),
            pltpu.VMEM((n, 2, part, vcols), bf16),
            pltpu.VMEM((n, 2, part, vcols), bf16),
            pltpu.VMEM((n, 2, part, vcols), bf16),
            pltpu.VMEM((2, 2, part, vcols), bf16),
            pltpu.VMEM((qcols // HEAD_SIZE, tok, total), bf16),
            dma((11,)),
            dma((2,)),
            dma((10,)),
            dma((3,)),
            dma((3,)),
            dma((2,)),
            dma((4,)),
            dma((2,)),
            dma((4,)),
            dma,
            dma((2,)),
            dma((2,)),
            dma((n,)),
            dma,
            dma((n,)),
            dma((2,)),
            dma((n,)),
            dma((2,)),
            dma,
            pltpu.SemaphoreType.REGULAR,
        ],
        compiler_params=pltpu.CompilerParams(
            collective_id=0, has_side_effects=True, vmem_limit_bytes=56 * 1024 * 1024
        ),
    )(
        layer_input_rows,
        encoded_query_rows,
        encoded_key_rows,
        layer_norm_gain,
        base_value_matrix,
        jnp.swapaxes(adapter_down_panels, 2, 3),
        adapter_up_panels,
        request_token_lengths,
        adapter_per_request,
        rank_per_adapter,
        slot_per_adapter,
    )[None]


def solution(mesh):
    in_specs = (
        P("segment", ("groups", "seq"), None),
        P("segment", ("groups", "seq"), "owner"),
        P("segment", ("groups", "seq"), "owner"),
        P("segment", None),
        P("segment", ("seq", "owner"), None),
        P("segment", "seq", "owner", None),
        P("segment", "seq", None, "owner"),
        P("groups"),
        P("groups"),
        P(),
        P(),
    )
    out_specs = P("segment", ("groups", "seq"), "owner")
    n = mesh.shape["seq"]
    small = mesh.shape["owner"] == 2 and mesh.shape["groups"] == 2 and n == 4
    return jax.shard_map(
        functools.partial(fused, n) if small else per_device, mesh=mesh, in_specs=in_specs, out_specs=out_specs, check_vma=False
    )
```

```python
import functools

import jax
import jax.numpy as jnp
from jax import lax
from jax.experimental import pallas as pl
from jax.experimental.pallas import tpu as pltpu
from jax.sharding import PartitionSpec as P

WINDOW = 1024
HEADS = 16
KEY_VALUE_HEADS = 8
HEAD_SIZE = 128


query_scale = 168.0 ** (-0.5)
adapter_strength = 32.0
norm_eps = 1e-06


def broadcast(x, axis, root):
    mine = lax.axis_index(axis) == root
    return lax.psum(jnp.where(mine, x, jnp.zeros_like(x)), axis)


def from_behind(value, axis, steps):
    count = lax.axis_size(axis)
    first, last = (max(0, -steps), min(count, count - steps))
    return lax.ppermute(value, axis, [(source, source + steps) for source in range(first, last)])


def per_device(
    layer_input_rows,
    encoded_query_rows,
    encoded_key_rows,
    layer_norm_gain,
    base_value_matrix,
    adapter_down_panels,
    adapter_up_panels,
    request_token_lengths,
    adapter_per_request,
    rank_per_adapter,
    slot_per_adapter,
):
    hidden = layer_input_rows[0]
    row_count = hidden.shape[0]
    seq_now = lax.axis_index("seq")
    owner_now = lax.axis_index("owner")
    reach_count = min(WINDOW // row_count, lax.axis_size("seq") - 1)
    requests = request_token_lengths.shape[0]
    library = slot_per_adapter.shape[0]
    slots_here = adapter_down_panels.shape[1]
    rows_halved = adapter_down_panels.shape[2]
    rank_span_width = adapter_down_panels.shape[3]
    key_value_halved = adapter_up_panels.shape[3]
    group_size = HEADS // KEY_VALUE_HEADS
    request_ends = jnp.cumsum(request_token_lengths)
    position = seq_now * row_count + jnp.arange(row_count, dtype=jnp.int32)
    context = seq_now * row_count + jnp.arange(-reach_count * row_count, row_count, dtype=jnp.int32)
    request_lookup = jnp.sum((position[:, None] >= request_ends[None, :]).astype(jnp.int32), axis=1)
    request_ctx = jnp.sum((context[:, None] >= request_ends[None, :]).astype(jnp.int32), axis=1)
    live_mask = (context[None, :] <= position[:, None]) & (
        context[None, :] > position[:, None] - WINDOW
    )
    live_mask = (
        live_mask & (context[None, :] >= 0) & (request_ctx[None, :] == request_lookup[:, None])
    )
    choose = adapter_per_request[:, None] == jnp.arange(library, dtype=jnp.int32)[None, :]
    slot_of = jnp.sum(jnp.where(choose, slot_per_adapter[None, :], 0), axis=1)
    rank_lookup = jnp.sum(jnp.where(choose, rank_per_adapter[None, :], 0), axis=1)
    scale_lookup = adapter_strength / rank_lookup.astype(jnp.float32)
    in_request = request_lookup[:, None] == jnp.arange(requests, dtype=jnp.int32)[None, :]
    column_live = jnp.arange(rank_span_width, dtype=jnp.int32)[None, :] < rank_lookup[:, None]
    row_gain_weight = jnp.where(in_request, scale_lookup[None, :], jnp.float32(0.0))
    down_panel_here = adapter_down_panels[0]
    up_panel_here = adapter_up_panels[0]
    queries = encoded_query_rows[0]
    keys_own = encoded_key_rows[0]
    key_heads = keys_own.shape[1] // HEAD_SIZE
    wide_rows = hidden.astype(jnp.float32)
    normalized_rows = wide_rows * lax.rsqrt(
        jnp.mean(wide_rows * wide_rows, axis=1, keepdims=True) + norm_eps
    )
    normalized_rows = (normalized_rows * layer_norm_gain[0][None, :]).astype(jnp.bfloat16)
    normed_half = lax.dynamic_slice_in_dim(normalized_rows, owner_now * rows_halved, rows_halved, 1)
    full_value = jnp.dot(
        normalized_rows,
        lax.all_gather(base_value_matrix[0], ("seq", "owner"), axis=0, tiled=True),
        preferred_element_type=jnp.float32,
    )
    value_base_rows = lax.dynamic_slice_in_dim(
        full_value, owner_now * key_value_halved, key_value_halved, 1
    )

    def fetch_one(reduced_rows, request_index):
        owner_slot = slot_of[request_index]
        holder = owner_slot // slots_here
        local_slot = owner_slot % slots_here
        down_local = lax.dynamic_slice_in_dim(down_panel_here, local_slot, 1, 0)
        up_local = lax.dynamic_slice_in_dim(up_panel_here, local_slot, 1, 0)
        down_piece, up_piece = (
            broadcast(down_local, "seq", holder),
            broadcast(up_local, "seq", holder),
        )
        keep_mask = in_request[:, request_index][:, None] & column_live[request_index][None, :]
        matrix_product = jnp.dot(normed_half, down_piece[0], preferred_element_type=jnp.float32)
        return (reduced_rows + jnp.where(keep_mask, matrix_product, jnp.float32(0.0)), up_piece[0])

    start_low = jnp.zeros((row_count, rank_span_width), jnp.float32)
    reduced_rows, panels_up = lax.scan(fetch_one, start_low, jnp.arange(requests, dtype=jnp.int32))
    reduced_rows = lax.psum(reduced_rows, "owner").astype(jnp.bfloat16)
    raised_rows = jnp.einsum(
        "tr,qrk->qtk", reduced_rows, panels_up, preferred_element_type=jnp.float32
    )
    adapter_value = jnp.sum(row_gain_weight.T[:, :, None] * raised_rows, axis=0)
    value_output_rows = (value_base_rows + adapter_value).astype(jnp.bfloat16)
    key_parts = []
    value_parts = []
    for shift_by in range(reach_count, 0, -1):
        key_piece, value_piece = from_behind((keys_own, value_output_rows), "seq", shift_by)
        key_parts.append(key_piece)
        value_parts.append(value_piece)
    keys_all = jnp.concatenate(key_parts + [keys_own], axis=0)
    values_all = jnp.concatenate(value_parts + [value_output_rows], axis=0)
    query_view = queries.reshape(row_count, key_heads, group_size, HEAD_SIZE)
    key_view = keys_all.reshape(-1, key_heads, HEAD_SIZE)
    value_view = values_all.reshape(-1, key_heads, HEAD_SIZE)
    head_outputs = []
    for head_index in range(key_heads):
        query_head = query_view[:, head_index]
        scores = (
            jnp.einsum(
                "tcd,jd->ctj",
                query_head,
                key_view[:, head_index],
                preferred_element_type=jnp.float32,
            )
            * query_scale
        )
        scores = jnp.where(live_mask[None], scores, jnp.float32(-1e30))
        row_max = jnp.max(scores, axis=-1, keepdims=True)
        weights = jnp.exp(scores - row_max)
        row_total = jnp.sum(weights, axis=-1, keepdims=True)
        softmax_rows = (weights / row_total).astype(jnp.bfloat16)
        mixed = jnp.einsum(
            "ctj,jd->tcd",
            softmax_rows,
            value_view[:, head_index],
            preferred_element_type=jnp.float32,
        )
        head_outputs.append(mixed.astype(jnp.bfloat16).reshape(row_count, group_size * HEAD_SIZE))
    result = jnp.concatenate(head_outputs, axis=1)
    return result[None]


LANES = 128
CHUNKS = 4


def kernel(
    n,
    x_hbm,
    q_hbm,
    k_hbm,
    gain_hbm,
    w_hbm,
    down_hbm,
    up_hbm,
    lengths_hbm,
    adapters_hbm,
    ranks_hbm,
    slots_hbm,
    out,
    lengths,
    adapters,
    ranks,
    slots,
    xr,
    gain,
    xb,
    wbuf,
    dn,
    hdn,
    dnt,
    ucat,
    qb,
    kb,
    pown,
    lowa,
    pbuf,
    prec,
    sbuf,
    srec,
    vbuf,
    vx,
    vall,
    va,
    prob,
    loc_sem,
    x_send,
    x_recv,
    ex_send,
    ex_recv,
    ph_send,
    ph_recv,
    uh_send,
    uh_recv,
    k_send,
    k_recv,
    p_send,
    p_recv,
    s_send,
    s_recv,
    v_send,
    v_recv,
    d_recv,
    d_send,
    ready,
):
    f32, bf16 = jnp.float32, jnp.bfloat16
    s = lax.axis_index("seq")
    o = lax.axis_index("owner")
    g = lax.axis_index("groups")
    other = 1 - o
    tok, width = x_hbm.shape[1], x_hbm.shape[2]
    part = tok // 2
    half = width // 2
    win, vcols2 = wbuf.shape
    vcols = vcols2 // 2
    slab = w_hbm.shape[1]
    panels, rank_width = dn.shape[0], dn.shape[1]
    low_width = panels * rank_width
    rank_part = rank_width // 2
    chip_rows = width // n
    requests = lengths.shape[0]
    total = n * tok
    group = HEADS // KEY_VALUE_HEADS
    q_heads = qb.shape[1] // HEAD_SIZE
    wide = -(-half // (2 * LANES)) * LANES
    sizes = (wide, half - wide)

    def peer(seq, owner=None, groups=None):
        return {
            "seq": seq,
            "owner": o if owner is None else owner,
            "groups": g if groups is None else groups,
        }

    def remote(src, dst, send, recv, device):
        return pltpu.make_async_remote_copy(
            src_ref=src,
            dst_ref=dst,
            send_sem=send,
            recv_sem=recv,
            device_id=device,
            device_id_type=pl.DeviceIdType.MESH,
        )

    def arrived(ref, sem):
        remote(ref, ref, sem, sem, peer(s, other)).wait_recv()

    def sent(ref, sem):
        remote(ref, ref, sem, sem, peer(s, other)).wait_send()

    barrier = pltpu.get_barrier_semaphore()

    def greet(device):
        pl.semaphore_signal(barrier, inc=1, device_id=device, device_id_type=pl.DeviceIdType.MESH)

    my_rows = pl.ds(pl.multiple_of(o * part, 16), part)
    my_half = pl.ds(pl.multiple_of(o * half, LANES), half)
    other_half = pl.ds(pl.multiple_of(other * half, LANES), half)
    my_cols = pl.ds(pl.multiple_of(o * vcols, LANES), vcols)
    other_cols = pl.ds(pl.multiple_of(other * vcols, LANES), vcols)

    def half_at(which):
        return pl.ds(which * half, half)

    ends, slot_of, rank_of = [], [], []

    def read_tables():
        for at in range(7, 11):
            local[at].wait()
        run = jnp.int32(0)
        for r in range(requests):
            run = run + lengths[r]
            ends.append(run)
            adapter = adapters[r]
            slot_of.append(slots[adapter])
            rank_of.append(ranks[adapter])

    def request_at(position):
        found = jnp.zeros(position.shape, jnp.int32)
        for r in range(requests):
            found = found + (position >= ends[r]).astype(jnp.int32)
        return found

    def token_facts(first, count):
        row = lax.broadcasted_iota(jnp.int32, (count * part, 1), 0)
        position = (first + row // part) * tok + o * part + row % part
        req = request_at(position)
        slot_t = jnp.zeros(row.shape, jnp.int32)
        rank_t = jnp.ones(row.shape, jnp.int32)
        for r in range(requests):
            slot_t = jnp.where(req == r, slot_of[r], slot_t)
            rank_t = jnp.where(req == r, rank_of[r], rank_t)
        return slot_t, rank_t

    def masked(low, slot_t, rank_t, chip):
        column = lax.broadcasted_iota(jnp.int32, low.shape, 1)
        start = (slot_t - chip * panels) * rank_width
        return jnp.where((column >= start) & (column < start + rank_t), low, 0.0).astype(bf16)

    def dot(a, b):
        return jnp.dot(a, b, preferred_element_type=f32)

    def window_of(c):
        at = min(c * chip_rows // LANES * LANES, width - win)
        return at, c * chip_rows - at

    def rows_of(first, count, columns):
        return xb[first : first + count, :, columns].reshape(count * part, columns.size)

    def end_value(c, t, columns):
        slot_t, rank_t = token_facts(t, 1)
        at, _ = window_of(c)
        base = dot(xb[t, :, pl.ds(at, win)], wbuf[...])
        low = masked(dot(xb[t, :, columns], dnt[columns, :low_width]), slot_t, rank_t, c)
        raised = dot(low, ucat[:panels].reshape(low_width, vcols2))
        return base + raised * (adapter_strength / rank_t.astype(f32))

    def first_part(c, first, count, columns):
        at, _ = window_of(c)
        base = dot(rows_of(first, count, pl.ds(at, win)), wbuf[...])
        low = dot(rows_of(first, count, columns), dnt[columns, :low_width])
        pown[pl.ds(first, count)] = base.reshape(count, part, vcols2)
        lowa[pl.ds(first, count)] = low.reshape(count, part, low_width)

    def last_part(c, first, count, chip, columns):
        slot_t, rank_t = token_facts(first, count)
        at = pl.ds(first, count)
        both = dot(rows_of(first, count, columns), dnt[columns, :])
        low = lowa[at].reshape(count * part, low_width) + both[:, :low_width]
        low = jnp.concatenate(
            [masked(low, slot_t, rank_t, c), masked(both[:, low_width:], slot_t, rank_t, chip)], axis=1
        )
        raised = dot(low, ucat[...].reshape(2 * low_width, vcols2))
        value = raised * (adapter_strength / rank_t.astype(f32))
        pown[at] = pown[at] + value.reshape(count, part, vcols2)

    def put(ref, t, value):
        for side in range(2):
            ref[t, side] = value[:, side * vcols : (side + 1) * vcols].astype(bf16)

    def get(ref, t):
        return jnp.concatenate([ref[t, 0], ref[t, 1]], axis=1).astype(f32)

    def chunk(q, up):
        at = (up if q < CHUNKS // 2 else 1 - up) * half + (q % 2) * wide
        return pl.ds(at, sizes[q % 2])

    local = [
        pltpu.make_async_copy(x_hbm.at[0, my_rows, :], xr, loc_sem.at[0]),
        pltpu.make_async_copy(gain_hbm, gain, loc_sem.at[1]),
        pltpu.make_async_copy(w_hbm.at[0], wbuf.at[pl.ds(0, slab)], loc_sem.at[2]),
        pltpu.make_async_copy(down_hbm.at[0], dn.at[:, :, my_half], loc_sem.at[3]),
        pltpu.make_async_copy(up_hbm.at[0], ucat.at[pl.ds(0, panels), :, my_cols], loc_sem.at[4]),
        pltpu.make_async_copy(q_hbm.at[0], qb, loc_sem.at[5]),
        pltpu.make_async_copy(k_hbm.at[0], kb.at[s], loc_sem.at[6]),
        pltpu.make_async_copy(lengths_hbm, lengths, loc_sem.at[7]),
        pltpu.make_async_copy(adapters_hbm, adapters, loc_sem.at[8]),
        pltpu.make_async_copy(ranks_hbm, ranks, loc_sem.at[9]),
        pltpu.make_async_copy(slots_hbm, slots, loc_sem.at[10]),
    ]

    def slab_at(c):
        _, pad = window_of(c)
        return pl.ds(pl.multiple_of(pad + o * slab, 16), slab)

    def transpose_panels(source, which, at):
        for piece in range(0, half, half // 3):
            rows = source[:, :, pl.ds(which * half + piece if source.shape[2] == width else piece, half // 3)]
            dnt[pl.ds(which * half + piece, half // 3), at : at + low_width] = rows.reshape(
                low_width, half // 3
            ).T

    def opening(c, greetings, count, at_once=None):
        local[0].start()
        local[1].start()
        w_local = pltpu.make_async_copy(w_hbm.at[0], wbuf.at[slab_at(c)], loc_sem.at[2])
        w_local.start()
        for at in range(3, 11):
            local[at].start()
        for device in greetings:
            greet(device)
        _, pad = window_of(c)
        if pad:
            wbuf[0:pad, :] = jnp.zeros((pad, vcols2), bf16)
        rest = win - pad - chip_rows
        if rest:
            wbuf[win - rest : win, :] = jnp.zeros((rest, vcols2), bf16)
        for t in range(c + 1, n):
            kb[t] = jnp.zeros(kb.shape[1:], bf16)
            vall[t] = jnp.zeros(vall.shape[1:], bf16)
        if at_once is not None:
            pl.semaphore_wait(barrier, count)
            at_once()
        local[0].wait()
        local[1].wait()
        rows = xr[...].astype(f32)
        inv = lax.rsqrt(jnp.mean(rows * rows, axis=1, keepdims=True) + norm_eps)
        xb[c] = (xr[...].astype(f32) * inv * gain[...]).astype(bf16)
        if at_once is None:
            pl.semaphore_wait(barrier, count)

    def exchange(c, kept):
        w_copy = remote(w_hbm.at[0], wbuf.at[slab_at(c)], ex_send.at[0], ex_recv.at[0], peer(c, other))
        dn_copy = remote(down_hbm.at[0], dn.at[:, :, my_half], ex_send.at[1], ex_recv.at[1], peer(c, other))
        up_copy = remote(
            up_hbm.at[0], ucat.at[pl.ds(0, panels), :, my_cols], ex_send.at[2], ex_recv.at[2], peer(c, other)
        )
        return w_copy, dn_copy, up_copy

    def attend(c):
        keys = kb[...].reshape(total, vcols)
        key_at = lax.broadcasted_iota(jnp.int32, (1, total), 1)
        query_at = c * tok + lax.broadcasted_iota(jnp.int32, (tok, 1), 0)
        live = (key_at <= query_at) & (key_at > query_at - WINDOW)
        live = live & (request_at(query_at) == request_at(key_at))
        for h in range(q_heads):
            kv = h // group
            scores = (
                lax.dot_general(
                    qb[:, h * HEAD_SIZE : (h + 1) * HEAD_SIZE],
                    keys[:, kv * HEAD_SIZE : (kv + 1) * HEAD_SIZE],
                    (((1,), (1,)), ((), ())),
                    preferred_element_type=f32,
                )
                * query_scale
            )
            scores = jnp.where(live, scores, -1e30)
            weights = jnp.exp(scores - jnp.max(scores, axis=1, keepdims=True))
            soft = weights / jnp.sum(weights, axis=1, keepdims=True)
            prob[h] = soft.astype(bf16)

    def mix(c):
        values = vall[...].reshape(total, vcols)
        for h in range(q_heads):
            kv = h // group
            out[:, h * HEAD_SIZE : (h + 1) * HEAD_SIZE] = dot(
                prob[h], values[:, kv * HEAD_SIZE : (kv + 1) * HEAD_SIZE]
            ).astype(bf16)

    per_group = panels // 2
    mine = pl.ds(g * per_group, per_group)
    theirs = pl.ds((1 - g) * per_group, per_group)
    my_up = pl.ds(panels + g * per_group, per_group)
    their_up = pl.ds(panels + (1 - g) * per_group, per_group)
    my_piece = pl.ds(pl.multiple_of(o * rank_part, 16), rank_part)
    other_piece = pl.ds(pl.multiple_of(other * rank_part, 16), rank_part)

    def x_end(c, t, q, up, to):
        at = xb.at[t, :, chunk(q, up)]
        return remote(at, at, x_send.at[0], x_recv.at[q], peer(to))

    def x_across(t, q, up, to, forwarded):
        at = xb.at[t, :, chunk(q, up)]
        index = (7 if forwarded else 4) + min(q, 2)
        return remote(at, at, x_send.at[0], x_recv.at[index], peer(to))

    def x_outward(t, q, up, to, index):
        at = xb.at[t, :, chunk(q, up)]
        return remote(at, at, x_send.at[1], x_recv.at[index], peer(to))

    def k_up(c, t):
        return remote(kb.at[t], kb.at[t], k_send, k_recv.at[t if c == 1 else 0], peer(c + 1))

    def end_program(c):
        low = c < n // 2
        i, j, f = (1, 2, 3) if low else (2, 1, 0)
        inward = int(low)
        kept = 1 - inward
        host_core = inward
        greetings = [peer(c, other), peer(i), peer(i, other)]
        if low:
            greetings += [peer(j), peer(j, other)]
        w_copy, dn_copy, up_copy = exchange(c, kept)
        piece_in = remote(
            down_hbm.at[0, mine, other_piece, :], hdn.at[mine, other_piece, :], ph_send.at[1], ph_recv.at[1], peer(c, other)
        )
        piece_z = remote(
            down_hbm.at[0, mine, my_piece, :], hdn.at[mine, my_piece, :], ph_send.at[0], ph_recv.at[0], peer(i)
        )
        piece_on = remote(
            hdn.at[mine, my_piece, :], hdn.at[mine, my_piece, :], ph_send.at[0], ph_recv.at[0], peer(i)
        )
        up_z = remote(up_hbm.at[0, mine], ucat.at[my_up, :, my_cols], uh_send.at[0], uh_recv.at[0], peer(i))

        def panels_out():
            @pl.when(o == host_core)
            def _():
                piece_in.start()
                piece_z.start()

            @pl.when(o != host_core)
            def _():
                dn_copy.start()

            w_copy.start()
            up_copy.start()

        opening(c, greetings, 3 if low else 5, None if low else panels_out)

        if not low:
            for core in (o, other):
                pl.semaphore_signal(ready, inc=1, device_id=peer(j, core), device_id_type=pl.DeviceIdType.MESH)
        before = 2 if low else 1

        def open_rows(opening_count=before):
            for q in range(opening_count):
                x_end(c, c, q, inward, i).start()

        open_rows()
        if low:
            panels_out()

        @pl.when(o != host_core)
        def _():
            arrived(hdn.at[mine, my_piece, :], ph_recv.at[1])
            piece_on.start()

        if low:
            x_end(c, c, before, inward, i).start()
            before += 1
        up_z.start()
        if c == 0:
            local[6].wait()
            k_up(c, c).start()
        for q in range(before, CHUNKS):
            x_end(c, c, q, inward, i).start()
        for at in (2, 3, 4):
            local[at].wait()
        read_tables()

        @pl.when(o == host_core)
        def _():
            arrived(dn.at[:, :, other_half], ex_recv.at[1])

        transpose_panels(dn, kept, 0)
        arrived(ucat.at[pl.ds(0, panels), :, other_cols], ex_recv.at[2])
        arrived(wbuf.at[pl.ds(0, slab)], ex_recv.at[0])

        def p_copy(t):
            return remote(pbuf.at[t], prec.at[t], p_send.at[0], p_recv.at[t], peer(i))

        def p_core(t):
            return remote(
                pbuf.at[t, other], prec.at[t, 0], p_send.at[1], s_recv.at[t], peer(c, other)
            )

        def end_partial(t):
            put(pbuf, t, end_value(c, t, half_at(kept)))
            if t == c or not low:
                p_core(t).start()

        end_partial(c)
        if low:
            p_copy(c).start()
        for index, t in enumerate((i, j, f)):
            arrived(xb.at[t, :, half_at(kept)], x_recv.at[index])
            end_partial(t)
            if low:
                p_copy(t).start()
        if not low:
            for t in range(c):
                p_copy(t).start()
        local[5].wait()
        if not low:
            local[6].wait()
            arrived(kb.at[pl.ds(0, n - 1)], k_recv.at[0])
        attend(c)

        def take(t):
            arrived(prec.at[t, 0], s_recv.at[t])
            arrived(vall.at[t], v_recv.at[t])
            own_rows = vall[t, o].astype(f32) + pbuf[t, o].astype(f32)
            other_rows = vall[t, other].astype(f32) + prec[t, 0].astype(f32)
            if t == c or t == i:
                at = int(t != c)
                arrived(va.at[at], d_recv.at[at])
                own_rows = own_rows + va[at, o].astype(f32)
                other_rows = other_rows + va[at, other].astype(f32)
            vall[t, o] = own_rows.astype(bf16)
            vall[t, other] = other_rows.astype(bf16)

        for t in (0,) if low else (0, i, c, j):
            take(t)
        mix(c)

        sent(wbuf.at[pl.ds(0, slab)], ex_send.at[0])
        sent(ucat.at[pl.ds(0, panels), :, other_cols], ex_send.at[2])
        sent(hdn.at[mine, my_piece, :], ph_send.at[0])

        @pl.when(o == host_core)
        def _():
            sent(hdn.at[mine, my_piece, :], ph_send.at[1])

        @pl.when(o != host_core)
        def _():
            sent(dn.at[:, :, my_half], ex_send.at[1])

        sent(ucat.at[my_up, :, my_cols], uh_send.at[0])
        sent(xb.at[0], x_send.at[0])
        if c == 0:
            sent(kb.at[0], k_send)
            sent(pbuf, p_send.at[0])
            sent(pbuf.at[0, 0], p_send.at[1])
        else:
            sent(pbuf.at[pl.ds(0, n - 1)], p_send.at[0])
            sent(pbuf.at[:, 0], p_send.at[1])

    def inner_program(c):
        low = c < n // 2
        e, j, f = (0, 2, 3) if low else (3, 1, 0)
        inward = int(low)
        outward = 1 - inward
        first = min(c, e, j)
        greetings = [peer(c, other), peer(e), peer(e, other), peer(j), peer(c, o, 1 - g)]
        if low:
            greetings += [peer(f), peer(f, other)]
        opening(c, greetings, 5 if low else 7)
        w_copy, dn_copy, up_copy = exchange(c, None)

        def own_across(q):
            x_across(c, q, inward, j, False).start()

        for q in range(CHUNKS // 2):
            own_across(q)
            x_outward(c, q, outward, e, 0).start()
        if not low:
            own_across(2)
            own_across(3)
        w_copy.start()
        dn_copy.start()
        up_copy.start()
        local[6].wait()
        for at in (2, 3, 4):
            local[at].wait()
        read_tables()

        def next_e(q):
            arrived(xb.at[e, :, chunk(q, inward)], x_recv.at[q])
            x_across(e, q, inward, j, True).start()

        def next_j(q):
            arrived(xb.at[j, :, chunk(q, outward)], x_recv.at[4 + q])
            x_outward(j, q, outward, e, 1).start()

        def next_f(q):
            arrived(xb.at[f, :, chunk(q, outward)], x_recv.at[7 + q])
            x_outward(f, q, outward, e, 2).start()

        def piece(which, ranks_at):
            return hdn.at[which, ranks_at, :]

        def pass_on(which, ranks_at, sem, recv, device):
            return remote(piece(which, ranks_at), piece(which, ranks_at), ph_send.at[sem], ph_recv.at[recv], device)

        def pass_up(which, sem, recv, device):
            at = ucat.at[which, :, my_cols]
            return remote(at, at, uh_send.at[sem], uh_recv.at[recv], device)

        def host_z():
            arrived(piece(mine, my_piece), ph_recv.at[0])
            pass_on(mine, my_piece, 0, 1, peer(c, o, 1 - g)).start()
            pass_on(mine, my_piece, 1, 2, peer(c, other)).start()

        def host_up():
            arrived(ucat.at[my_up, :, my_cols], uh_recv.at[0])
            pass_up(my_up, 0, 1, peer(c, o, 1 - g)).start()
            pass_up(my_up, 1, 2, peer(c, other)).start()

        def host_y():
            arrived(piece(theirs, my_piece), ph_recv.at[1])
            pass_on(theirs, my_piece, 1, 3, peer(c, other)).start()

        def host_yu():
            arrived(ucat.at[their_up, :, my_cols], uh_recv.at[1])
            pass_up(their_up, 1, 3, peer(c, other)).start()

        def host_done():
            arrived(piece(mine, other_piece), ph_recv.at[2])
            arrived(piece(theirs, other_piece), ph_recv.at[3])
            transpose_panels(hdn, inward, low_width)
            arrived(ucat.at[my_up, :, other_cols], uh_recv.at[2])
            arrived(ucat.at[their_up, :, other_cols], uh_recv.at[3])

        def own_weights():
            arrived(dn.at[:, :, other_half], ex_recv.at[1])
            transpose_panels(dn, outward, 0)
            transpose_panels(dn, inward, 0)
            arrived(ucat.at[pl.ds(0, panels), :, other_cols], ex_recv.at[2])
            arrived(wbuf.at[pl.ds(0, slab)], ex_recv.at[0])

        def rest_of_j():
            arrived(xb.at[j, :, half_at(inward)], x_recv.at[6])

        def rest_of_f():
            arrived(xb.at[f, :, half_at(inward)], x_recv.at[9])

        def own(at, count):
            first_part(c, at, count, half_at(outward))

        def hosted(at, count):
            last_part(c, at, count, e, half_at(inward))

        def s_copy(t):
            return remote(sbuf.at[t], srec.at[t], s_send, s_recv.at[t], peer(j))

        def s_far(t, core):
            at = int(t != f)
            return remote(sbuf.at[t, core], va.at[at, o], d_send, d_recv.at[at], peer(f, core))

        def v_end(t, core):
            return remote(vbuf.at[t, core], vall.at[t, o], v_send.at[0], v_recv.at[t], peer(e, core))

        def v_core(t):
            return remote(vx.at[t, other], vall.at[t, o], v_send.at[1], v_recv.at[t], peer(c, other))

        def give_end(t):
            v_end(t, 0).start()
            v_end(t, 1).start()

        def keep(t, value):
            put(vx, t, value)
            v_core(t).start()
            vall[t, o] = vx[t, o]

        def early(t):
            put(vbuf, t, pown[t])
            give_end(t)

        def add_end(t):
            arrived(prec.at[t], p_recv.at[t])
            value = pown[t] + get(prec, t)
            put(sbuf, t, value)
            if t == f or (low and t == j):
                if low and t == j:
                    pl.semaphore_wait(ready, 2)
                s_far(t, 0).start()
                s_far(t, 1).start()
            if t != f or not low:
                s_copy(t).start()
            return value

        def relay(t):
            arrived(srec.at[t], s_recv.at[t])
            value = pown[t] + get(srec, t)
            if t == c:
                arrived(prec.at[t], p_recv.at[t])
            else:
                put(vbuf, t, value)
                give_end(t)
            keep(t, value + get(prec, t))

        def next_k(t):
            arrived(kb.at[t], k_recv.at[t])
            k_up(c, t).start()

        if low:
            next_e(0)
            next_e(1)
            k_up(c, c).start()
            own_across(2)
            own_weights()
            next_j(0)
            next_j(1)
            host_z()
            rest_of_j()
            next_e(2)
            own_across(3)
            host_up()
            next_f(0)
            next_k(0)
            host_y()
            next_e(3)
            host_yu()
            next_f(1)
            own(first, 3)
            host_done()
            hosted(first, 3)
            early(e)
            for t in range(3):
                pown[t] = add_end(t)
            own(f, 1)
            local[5].wait()
            attend(c)
            rest_of_f()
            hosted(f, 1)
            add_end(f)
            for t in (1, 0):
                arrived(srec.at[t], s_recv.at[t])
                keep(t, pown[t] + get(srec, t))
        else:
            own_weights()
            next_j(0)
            next_j(1)
            host_z()
            next_f(0)
            next_e(0)
            next_f(1)
            k_up(c, c).start()
            host_up()
            next_k(1)
            own(f, 2)
            next_e(1)
            host_y()
            next_e(2)
            host_yu()
            next_e(3)
            own(c, 2)
            host_done()
            hosted(c, 2)
            early(c)
            early(e)
            next_k(0)
            rest_of_f()
            hosted(f, 1)
            add_end(f)
            rest_of_j()
            hosted(j, 1)
            add_end(j)
            relay(f)
            relay(j)
            local[5].wait()
            attend(c)
            relay(c)
        for t in range(c + 1):
            arrived(vall.at[t, other], v_recv.at[t])
        mix(c)

        sent(wbuf.at[pl.ds(0, slab)], ex_send.at[0])
        sent(dn.at[:, :, my_half], ex_send.at[1])
        sent(ucat.at[pl.ds(0, panels), :, other_cols], ex_send.at[2])
        sent(xb.at[pl.ds(0, 2)], x_send.at[0])
        sent(xb.at[pl.ds(0, 3), :, half_at(0)], x_send.at[1])
        sent(piece(mine, my_piece), ph_send.at[0])
        sent(hdn.at[:, my_piece, :], ph_send.at[1])
        sent(ucat.at[my_up, :, my_cols], uh_send.at[0])
        sent(ucat.at[pl.ds(panels, panels), :, my_cols], uh_send.at[1])
        sent(kb.at[pl.ds(0, c + 1)], k_send)
        if low:
            sent(sbuf.at[pl.ds(0, 3)], s_send)
            sent(sbuf.at[pl.ds(0, 2)], d_send)
            sent(vbuf.at[0], v_send.at[0])
        else:
            sent(sbuf.at[pl.ds(0, 2)], s_send)
            sent(sbuf.at[0], d_send)
            sent(vbuf, v_send.at[0])
        sent(vx.at[pl.ds(0, c + 1), 0], v_send.at[1])

    for c in range(n):

        @pl.when(s == c)
        def _():
            ends.clear()
            slot_of.clear()
            rank_of.clear()
            if c in (0, n - 1):
                end_program(c)
            else:
                inner_program(c)


def fused(
    n,
    layer_input_rows,
    encoded_query_rows,
    encoded_key_rows,
    layer_norm_gain,
    base_value_matrix,
    adapter_down_panels,
    adapter_up_panels,
    request_token_lengths,
    adapter_per_request,
    rank_per_adapter,
    slot_per_adapter,
):
    f32, bf16 = jnp.float32, jnp.bfloat16
    tok, width = layer_input_rows.shape[1:]
    part, half = tok // 2, width // 2
    panels, _, rank_width = adapter_down_panels.shape[1:]
    vcols = adapter_up_panels.shape[3]
    qcols = encoded_query_rows.shape[2]
    chip_rows = width // n
    pads = [i * chip_rows % LANES for i in range(n)]
    win = -(-(max(pads) + chip_rows) // LANES) * LANES
    total = n * tok
    dma = pltpu.SemaphoreType.DMA
    any_spec = pl.BlockSpec(memory_space=pl.ANY)
    return pl.pallas_call(
        functools.partial(kernel, n),
        out_shape=pltpu.VMEM(encoded_query_rows.shape[1:], bf16),
        in_specs=[any_spec] * 11,
        out_specs=pl.BlockSpec(memory_space=pltpu.VMEM),
        scratch_shapes=[
            pltpu.SMEM(request_token_lengths.shape, jnp.int32),
            pltpu.SMEM(adapter_per_request.shape, jnp.int32),
            pltpu.SMEM(rank_per_adapter.shape, jnp.int32),
            pltpu.SMEM(slot_per_adapter.shape, jnp.int32),
            pltpu.VMEM((part, width), bf16),
            pltpu.VMEM((1, width), f32),
            pltpu.VMEM((n, part, width), bf16),
            pltpu.VMEM((win, 2 * vcols), bf16),
            pltpu.VMEM((panels, rank_width, width), bf16),
            pltpu.VMEM((panels, rank_width, half), bf16),
            pltpu.VMEM((width, 2 * panels * rank_width), bf16),
            pltpu.VMEM((2 * panels, rank_width, 2 * vcols), bf16),
            pltpu.VMEM((tok, qcols), bf16),
            pltpu.VMEM((n, tok, vcols), bf16),
            pltpu.VMEM((n, part, 2 * vcols), f32),
            pltpu.VMEM((n, part, panels * rank_width), f32),
            pltpu.VMEM((n, 2, part, vcols), bf16),
            pltpu.VMEM((n, 2, part, vcols), bf16),
            pltpu.VMEM((n, 2, part, vcols), bf16),
            pltpu.VMEM((n, 2, part, vcols), bf16),
            pltpu.VMEM((n, 2, part, vcols), bf16),
            pltpu.VMEM((n, 2, part, vcols), bf16),
            pltpu.VMEM((n, 2, part, vcols), bf16),
            pltpu.VMEM((2, 2, part, vcols), bf16),
            pltpu.VMEM((qcols // HEAD_SIZE, tok, total), bf16),
            dma((11,)),
            dma((2,)),
            dma((10,)),
            dma((3,)),
            dma((3,)),
            dma((2,)),
            dma((4,)),
            dma((2,)),
            dma((4,)),
            dma,
            dma((2,)),
            dma((2,)),
            dma((n,)),
            dma,
            dma((n,)),
            dma((2,)),
            dma((n,)),
            dma((2,)),
            dma,
            pltpu.SemaphoreType.REGULAR,
        ],
        compiler_params=pltpu.CompilerParams(
            collective_id=0, has_side_effects=True, vmem_limit_bytes=56 * 1024 * 1024
        ),
    )(
        layer_input_rows,
        encoded_query_rows,
        encoded_key_rows,
        layer_norm_gain,
        base_value_matrix,
        jnp.swapaxes(adapter_down_panels, 2, 3),
        adapter_up_panels,
        request_token_lengths,
        adapter_per_request,
        rank_per_adapter,
        slot_per_adapter,
    )[None]


def solution(mesh):
    in_specs = (
        P("segment", ("groups", "seq"), None),
        P("segment", ("groups", "seq"), "owner"),
        P("segment", ("groups", "seq"), "owner"),
        P("segment", None),
        P("segment", ("seq", "owner"), None),
        P("segment", "seq", "owner", None),
        P("segment", "seq", None, "owner"),
        P("groups"),
        P("groups"),
        P(),
        P(),
    )
    out_specs = P("segment", ("groups", "seq"), "owner")
    n = mesh.shape["seq"]
    small = mesh.shape["owner"] == 2 and mesh.shape["groups"] == 2 and n == 4
    return jax.shard_map(
        functools.partial(fused, n) if small else per_device, mesh=mesh, in_specs=in_specs, out_specs=out_specs, check_vma=False
    )
```

```python
import functools

import jax
import jax.numpy as jnp
from jax import lax
from jax.experimental import pallas as pl
from jax.experimental.pallas import tpu as pltpu
from jax.sharding import PartitionSpec as P

WINDOW = 1024
HEADS = 16
KEY_VALUE_HEADS = 8
HEAD_SIZE = 128


query_scale = 168.0 ** (-0.5)
adapter_strength = 32.0
norm_eps = 1e-06


def broadcast(x, axis, root):
    mine = lax.axis_index(axis) == root
    return lax.psum(jnp.where(mine, x, jnp.zeros_like(x)), axis)


def from_behind(value, axis, steps):
    count = lax.axis_size(axis)
    first, last = (max(0, -steps), min(count, count - steps))
    return lax.ppermute(value, axis, [(source, source + steps) for source in range(first, last)])


def per_device(
    layer_input_rows,
    encoded_query_rows,
    encoded_key_rows,
    layer_norm_gain,
    base_value_matrix,
    adapter_down_panels,
    adapter_up_panels,
    request_token_lengths,
    adapter_per_request,
    rank_per_adapter,
    slot_per_adapter,
):
    hidden = layer_input_rows[0]
    row_count = hidden.shape[0]
    seq_now = lax.axis_index("seq")
    owner_now = lax.axis_index("owner")
    reach_count = min(WINDOW // row_count, lax.axis_size("seq") - 1)
    requests = request_token_lengths.shape[0]
    library = slot_per_adapter.shape[0]
    slots_here = adapter_down_panels.shape[1]
    rows_halved = adapter_down_panels.shape[2]
    rank_span_width = adapter_down_panels.shape[3]
    key_value_halved = adapter_up_panels.shape[3]
    group_size = HEADS // KEY_VALUE_HEADS
    request_ends = jnp.cumsum(request_token_lengths)
    position = seq_now * row_count + jnp.arange(row_count, dtype=jnp.int32)
    context = seq_now * row_count + jnp.arange(-reach_count * row_count, row_count, dtype=jnp.int32)
    request_lookup = jnp.sum((position[:, None] >= request_ends[None, :]).astype(jnp.int32), axis=1)
    request_ctx = jnp.sum((context[:, None] >= request_ends[None, :]).astype(jnp.int32), axis=1)
    live_mask = (context[None, :] <= position[:, None]) & (
        context[None, :] > position[:, None] - WINDOW
    )
    live_mask = (
        live_mask & (context[None, :] >= 0) & (request_ctx[None, :] == request_lookup[:, None])
    )
    choose = adapter_per_request[:, None] == jnp.arange(library, dtype=jnp.int32)[None, :]
    slot_of = jnp.sum(jnp.where(choose, slot_per_adapter[None, :], 0), axis=1)
    rank_lookup = jnp.sum(jnp.where(choose, rank_per_adapter[None, :], 0), axis=1)
    scale_lookup = adapter_strength / rank_lookup.astype(jnp.float32)
    in_request = request_lookup[:, None] == jnp.arange(requests, dtype=jnp.int32)[None, :]
    column_live = jnp.arange(rank_span_width, dtype=jnp.int32)[None, :] < rank_lookup[:, None]
    row_gain_weight = jnp.where(in_request, scale_lookup[None, :], jnp.float32(0.0))
    down_panel_here = adapter_down_panels[0]
    up_panel_here = adapter_up_panels[0]
    queries = encoded_query_rows[0]
    keys_own = encoded_key_rows[0]
    key_heads = keys_own.shape[1] // HEAD_SIZE
    wide_rows = hidden.astype(jnp.float32)
    normalized_rows = wide_rows * lax.rsqrt(
        jnp.mean(wide_rows * wide_rows, axis=1, keepdims=True) + norm_eps
    )
    normalized_rows = (normalized_rows * layer_norm_gain[0][None, :]).astype(jnp.bfloat16)
    normed_half = lax.dynamic_slice_in_dim(normalized_rows, owner_now * rows_halved, rows_halved, 1)
    full_value = jnp.dot(
        normalized_rows,
        lax.all_gather(base_value_matrix[0], ("seq", "owner"), axis=0, tiled=True),
        preferred_element_type=jnp.float32,
    )
    value_base_rows = lax.dynamic_slice_in_dim(
        full_value, owner_now * key_value_halved, key_value_halved, 1
    )

    def fetch_one(reduced_rows, request_index):
        owner_slot = slot_of[request_index]
        holder = owner_slot // slots_here
        local_slot = owner_slot % slots_here
        down_local = lax.dynamic_slice_in_dim(down_panel_here, local_slot, 1, 0)
        up_local = lax.dynamic_slice_in_dim(up_panel_here, local_slot, 1, 0)
        down_piece, up_piece = (
            broadcast(down_local, "seq", holder),
            broadcast(up_local, "seq", holder),
        )
        keep_mask = in_request[:, request_index][:, None] & column_live[request_index][None, :]
        matrix_product = jnp.dot(normed_half, down_piece[0], preferred_element_type=jnp.float32)
        return (reduced_rows + jnp.where(keep_mask, matrix_product, jnp.float32(0.0)), up_piece[0])

    start_low = jnp.zeros((row_count, rank_span_width), jnp.float32)
    reduced_rows, panels_up = lax.scan(fetch_one, start_low, jnp.arange(requests, dtype=jnp.int32))
    reduced_rows = lax.psum(reduced_rows, "owner").astype(jnp.bfloat16)
    raised_rows = jnp.einsum(
        "tr,qrk->qtk", reduced_rows, panels_up, preferred_element_type=jnp.float32
    )
    adapter_value = jnp.sum(row_gain_weight.T[:, :, None] * raised_rows, axis=0)
    value_output_rows = (value_base_rows + adapter_value).astype(jnp.bfloat16)
    key_parts = []
    value_parts = []
    for shift_by in range(reach_count, 0, -1):
        key_piece, value_piece = from_behind((keys_own, value_output_rows), "seq", shift_by)
        key_parts.append(key_piece)
        value_parts.append(value_piece)
    keys_all = jnp.concatenate(key_parts + [keys_own], axis=0)
    values_all = jnp.concatenate(value_parts + [value_output_rows], axis=0)
    query_view = queries.reshape(row_count, key_heads, group_size, HEAD_SIZE)
    key_view = keys_all.reshape(-1, key_heads, HEAD_SIZE)
    value_view = values_all.reshape(-1, key_heads, HEAD_SIZE)
    head_outputs = []
    for head_index in range(key_heads):
        query_head = query_view[:, head_index]
        scores = (
            jnp.einsum(
                "tcd,jd->ctj",
                query_head,
                key_view[:, head_index],
                preferred_element_type=jnp.float32,
            )
            * query_scale
        )
        scores = jnp.where(live_mask[None], scores, jnp.float32(-1e30))
        row_max = jnp.max(scores, axis=-1, keepdims=True)
        weights = jnp.exp(scores - row_max)
        row_total = jnp.sum(weights, axis=-1, keepdims=True)
        softmax_rows = (weights / row_total).astype(jnp.bfloat16)
        mixed = jnp.einsum(
            "ctj,jd->tcd",
            softmax_rows,
            value_view[:, head_index],
            preferred_element_type=jnp.float32,
        )
        head_outputs.append(mixed.astype(jnp.bfloat16).reshape(row_count, group_size * HEAD_SIZE))
    result = jnp.concatenate(head_outputs, axis=1)
    return result[None]


LANES = 128
CHUNKS = 4


def kernel(
    n,
    x_hbm,
    q_hbm,
    k_hbm,
    gain_hbm,
    w_hbm,
    down_hbm,
    up_hbm,
    lengths_hbm,
    adapters_hbm,
    ranks_hbm,
    slots_hbm,
    out,
    lengths,
    adapters,
    ranks,
    slots,
    xr,
    gain,
    xb,
    wbuf,
    dn,
    hdn,
    dnt,
    ucat,
    qb,
    kb,
    pown,
    lowa,
    pbuf,
    prec,
    sbuf,
    srec,
    vbuf,
    vx,
    vall,
    va,
    prob,
    loc_sem,
    x_send,
    x_recv,
    ex_send,
    ex_recv,
    ph_send,
    ph_recv,
    uh_send,
    uh_recv,
    k_send,
    k_recv,
    p_send,
    p_recv,
    s_send,
    s_recv,
    v_send,
    v_recv,
    d_recv,
    d_send,
    ready,
):
    f32, bf16 = jnp.float32, jnp.bfloat16
    s = lax.axis_index("seq")
    o = lax.axis_index("owner")
    g = lax.axis_index("groups")
    other = 1 - o
    tok, width = x_hbm.shape[1], x_hbm.shape[2]
    part = tok // 2
    half = width // 2
    win, vcols2 = wbuf.shape
    vcols = vcols2 // 2
    slab = w_hbm.shape[1]
    panels, rank_width = dn.shape[0], dn.shape[1]
    low_width = panels * rank_width
    rank_part = rank_width // 2
    chip_rows = width // n
    requests = lengths.shape[0]
    total = n * tok
    group = HEADS // KEY_VALUE_HEADS
    q_heads = qb.shape[1] // HEAD_SIZE
    wide = -(-half // (2 * LANES)) * LANES
    sizes = (wide, half - wide)

    def peer(seq, owner=None, groups=None):
        return {
            "seq": seq,
            "owner": o if owner is None else owner,
            "groups": g if groups is None else groups,
        }

    def remote(src, dst, send, recv, device):
        return pltpu.make_async_remote_copy(
            src_ref=src,
            dst_ref=dst,
            send_sem=send,
            recv_sem=recv,
            device_id=device,
            device_id_type=pl.DeviceIdType.MESH,
        )

    def arrived(ref, sem):
        remote(ref, ref, sem, sem, peer(s, other)).wait_recv()

    def sent(ref, sem):
        remote(ref, ref, sem, sem, peer(s, other)).wait_send()

    barrier = pltpu.get_barrier_semaphore()

    def greet(device):
        pl.semaphore_signal(barrier, inc=1, device_id=device, device_id_type=pl.DeviceIdType.MESH)

    my_rows = pl.ds(pl.multiple_of(o * part, 16), part)
    my_half = pl.ds(pl.multiple_of(o * half, LANES), half)
    other_half = pl.ds(pl.multiple_of(other * half, LANES), half)
    my_cols = pl.ds(pl.multiple_of(o * vcols, LANES), vcols)
    other_cols = pl.ds(pl.multiple_of(other * vcols, LANES), vcols)

    def half_at(which):
        return pl.ds(which * half, half)

    ends, slot_of, rank_of = [], [], []

    def read_tables():
        for at in range(7, 11):
            local[at].wait()
        run = jnp.int32(0)
        for r in range(requests):
            run = run + lengths[r]
            ends.append(run)
            adapter = adapters[r]
            slot_of.append(slots[adapter])
            rank_of.append(ranks[adapter])

    def request_at(position):
        found = jnp.zeros(position.shape, jnp.int32)
        for r in range(requests):
            found = found + (position >= ends[r]).astype(jnp.int32)
        return found

    def token_facts(first, count):
        row = lax.broadcasted_iota(jnp.int32, (count * part, 1), 0)
        position = (first + row // part) * tok + o * part + row % part
        req = request_at(position)
        slot_t = jnp.zeros(row.shape, jnp.int32)
        rank_t = jnp.ones(row.shape, jnp.int32)
        for r in range(requests):
            slot_t = jnp.where(req == r, slot_of[r], slot_t)
            rank_t = jnp.where(req == r, rank_of[r], rank_t)
        return slot_t, rank_t

    def masked(low, slot_t, rank_t, chip):
        column = lax.broadcasted_iota(jnp.int32, low.shape, 1)
        start = (slot_t - chip * panels) * rank_width
        return jnp.where((column >= start) & (column < start + rank_t), low, 0.0).astype(bf16)

    def dot(a, b):
        return jnp.dot(a, b, preferred_element_type=f32)

    def window_of(c):
        at = min(c * chip_rows // LANES * LANES, width - win)
        return at, c * chip_rows - at

    def rows_of(first, count, columns):
        return xb[first : first + count, :, columns].reshape(count * part, columns.size)

    def end_value(c, t, columns):
        slot_t, rank_t = token_facts(t, 1)
        at, _ = window_of(c)
        base = dot(xb[t, :, pl.ds(at, win)], wbuf[...])
        low = masked(dot(xb[t, :, columns], dnt[columns, :low_width]), slot_t, rank_t, c)
        raised = dot(low, ucat[:panels].reshape(low_width, vcols2))
        return base + raised * (adapter_strength / rank_t.astype(f32))

    def first_part(c, first, count, columns):
        at, _ = window_of(c)
        base = dot(rows_of(first, count, pl.ds(at, win)), wbuf[...])
        low = dot(rows_of(first, count, columns), dnt[columns, :low_width])
        pown[pl.ds(first, count)] = base.reshape(count, part, vcols2)
        lowa[pl.ds(first, count)] = low.reshape(count, part, low_width)

    def last_part(c, first, count, chip, columns):
        slot_t, rank_t = token_facts(first, count)
        at = pl.ds(first, count)
        both = dot(rows_of(first, count, columns), dnt[columns, :])
        low = lowa[at].reshape(count * part, low_width) + both[:, :low_width]
        low = jnp.concatenate(
            [masked(low, slot_t, rank_t, c), masked(both[:, low_width:], slot_t, rank_t, chip)], axis=1
        )
        raised = dot(low, ucat[...].reshape(2 * low_width, vcols2))
        value = raised * (adapter_strength / rank_t.astype(f32))
        pown[at] = pown[at] + value.reshape(count, part, vcols2)

    def put(ref, t, value):
        for side in range(2):
            ref[t, side] = value[:, side * vcols : (side + 1) * vcols].astype(bf16)

    def get(ref, t):
        return jnp.concatenate([ref[t, 0], ref[t, 1]], axis=1).astype(f32)

    def chunk(q, up):
        at = (up if q < CHUNKS // 2 else 1 - up) * half + (q % 2) * wide
        return pl.ds(at, sizes[q % 2])

    local = [
        pltpu.make_async_copy(x_hbm.at[0, my_rows, :], xr, loc_sem.at[0]),
        pltpu.make_async_copy(gain_hbm, gain, loc_sem.at[1]),
        pltpu.make_async_copy(w_hbm.at[0], wbuf.at[pl.ds(0, slab)], loc_sem.at[2]),
        pltpu.make_async_copy(down_hbm.at[0], dn.at[:, :, my_half], loc_sem.at[3]),
        pltpu.make_async_copy(up_hbm.at[0], ucat.at[pl.ds(0, panels), :, my_cols], loc_sem.at[4]),
        pltpu.make_async_copy(q_hbm.at[0], qb, loc_sem.at[5]),
        pltpu.make_async_copy(k_hbm.at[0], kb.at[s], loc_sem.at[6]),
        pltpu.make_async_copy(lengths_hbm, lengths, loc_sem.at[7]),
        pltpu.make_async_copy(adapters_hbm, adapters, loc_sem.at[8]),
        pltpu.make_async_copy(ranks_hbm, ranks, loc_sem.at[9]),
        pltpu.make_async_copy(slots_hbm, slots, loc_sem.at[10]),
    ]

    def slab_at(c):
        _, pad = window_of(c)
        return pl.ds(pl.multiple_of(pad + o * slab, 16), slab)

    def transpose_panels(source, which, at):
        for piece in range(0, half, half // 3):
            rows = source[:, :, pl.ds(which * half + piece if source.shape[2] == width else piece, half // 3)]
            dnt[pl.ds(which * half + piece, half // 3), at : at + low_width] = rows.reshape(
                low_width, half // 3
            ).T

    def opening(c, greetings, count, at_once=None):
        local[0].start()
        local[1].start()
        w_local = pltpu.make_async_copy(w_hbm.at[0], wbuf.at[slab_at(c)], loc_sem.at[2])
        w_local.start()
        for at in range(3, 11):
            local[at].start()
        for device in greetings:
            greet(device)
        _, pad = window_of(c)
        if pad:
            wbuf[0:pad, :] = jnp.zeros((pad, vcols2), bf16)
        rest = win - pad - chip_rows
        if rest:
            wbuf[win - rest : win, :] = jnp.zeros((rest, vcols2), bf16)
        for t in range(c + 1, n):
            kb[t] = jnp.zeros(kb.shape[1:], bf16)
            vall[t] = jnp.zeros(vall.shape[1:], bf16)
        if at_once is not None:
            pl.semaphore_wait(barrier, count)
            at_once()
        local[0].wait()
        local[1].wait()
        rows = xr[...].astype(f32)
        inv = lax.rsqrt(jnp.mean(rows * rows, axis=1, keepdims=True) + norm_eps)
        xb[c] = (xr[...].astype(f32) * inv * gain[...]).astype(bf16)
        if at_once is None:
            pl.semaphore_wait(barrier, count)

    def exchange(c, kept):
        w_copy = remote(w_hbm.at[0], wbuf.at[slab_at(c)], ex_send.at[0], ex_recv.at[0], peer(c, other))
        dn_copy = remote(down_hbm.at[0], dn.at[:, :, my_half], ex_send.at[1], ex_recv.at[1], peer(c, other))
        up_copy = remote(
            up_hbm.at[0], ucat.at[pl.ds(0, panels), :, my_cols], ex_send.at[2], ex_recv.at[2], peer(c, other)
        )
        return w_copy, dn_copy, up_copy

    def attend(c):
        keys = kb[...].reshape(total, vcols)
        key_at = lax.broadcasted_iota(jnp.int32, (1, total), 1)
        query_at = c * tok + lax.broadcasted_iota(jnp.int32, (tok, 1), 0)
        live = (key_at <= query_at) & (key_at > query_at - WINDOW)
        live = live & (request_at(query_at) == request_at(key_at))
        for h in range(q_heads):
            kv = h // group
            scores = (
                lax.dot_general(
                    qb[:, h * HEAD_SIZE : (h + 1) * HEAD_SIZE],
                    keys[:, kv * HEAD_SIZE : (kv + 1) * HEAD_SIZE],
                    (((1,), (1,)), ((), ())),
                    preferred_element_type=f32,
                )
                * query_scale
            )
            scores = jnp.where(live, scores, -1e30)
            weights = jnp.exp(scores - jnp.max(scores, axis=1, keepdims=True))
            soft = weights / jnp.sum(weights, axis=1, keepdims=True)
            prob[h] = soft.astype(bf16)

    def mix(c):
        values = vall[...].reshape(total, vcols)
        for h in range(q_heads):
            kv = h // group
            out[:, h * HEAD_SIZE : (h + 1) * HEAD_SIZE] = dot(
                prob[h], values[:, kv * HEAD_SIZE : (kv + 1) * HEAD_SIZE]
            ).astype(bf16)

    per_group = panels // 2
    mine = pl.ds(g * per_group, per_group)
    theirs = pl.ds((1 - g) * per_group, per_group)
    my_up = pl.ds(panels + g * per_group, per_group)
    their_up = pl.ds(panels + (1 - g) * per_group, per_group)
    my_piece = pl.ds(pl.multiple_of(o * rank_part, 16), rank_part)
    other_piece = pl.ds(pl.multiple_of(other * rank_part, 16), rank_part)

    def x_end(c, t, q, up, to):
        at = xb.at[t, :, chunk(q, up)]
        return remote(at, at, x_send.at[0], x_recv.at[q], peer(to))

    def x_across(t, q, up, to, forwarded):
        at = xb.at[t, :, chunk(q, up)]
        index = (7 if forwarded else 4) + min(q, 2)
        return remote(at, at, x_send.at[0], x_recv.at[index], peer(to))

    def x_outward(t, q, up, to, index):
        at = xb.at[t, :, chunk(q, up)]
        return remote(at, at, x_send.at[1], x_recv.at[index], peer(to))

    def k_up(c, t):
        return remote(kb.at[t], kb.at[t], k_send, k_recv.at[t if c == 1 else 0], peer(c + 1))

    def end_program(c):
        low = c < n // 2
        i, j, f = (1, 2, 3) if low else (2, 1, 0)
        inward = int(low)
        kept = 1 - inward
        host_core = inward
        greetings = [peer(c, other), peer(i), peer(i, other)]
        if low:
            greetings += [peer(j), peer(j, other)]
        w_copy, dn_copy, up_copy = exchange(c, kept)
        piece_in = remote(
            down_hbm.at[0, mine, other_piece, :], hdn.at[mine, other_piece, :], ph_send.at[1], ph_recv.at[1], peer(c, other)
        )
        piece_z = remote(
            down_hbm.at[0, mine, my_piece, :], hdn.at[mine, my_piece, :], ph_send.at[0], ph_recv.at[0], peer(i)
        )
        piece_on = remote(
            hdn.at[mine, my_piece, :], hdn.at[mine, my_piece, :], ph_send.at[0], ph_recv.at[0], peer(i)
        )
        up_z = remote(up_hbm.at[0, mine], ucat.at[my_up, :, my_cols], uh_send.at[0], uh_recv.at[0], peer(i))

        def panels_out():
            @pl.when(o == host_core)
            def _():
                piece_in.start()
                piece_z.start()

            @pl.when(o != host_core)
            def _():
                dn_copy.start()

            w_copy.start()
            up_copy.start()

        opening(c, greetings, 3 if low else 5, None if low else panels_out)

        if not low:
            for core in (o, other):
                pl.semaphore_signal(ready, inc=1, device_id=peer(j, core), device_id_type=pl.DeviceIdType.MESH)
        before = 2 if low else 1

        def open_rows(opening_count=before):
            for q in range(opening_count):
                x_end(c, c, q, inward, i).start()

        open_rows()
        if low:
            panels_out()

        @pl.when(o != host_core)
        def _():
            arrived(hdn.at[mine, my_piece, :], ph_recv.at[1])
            piece_on.start()

        if low:
            x_end(c, c, before, inward, i).start()
            before += 1
        up_z.start()
        if c == 0:
            local[6].wait()
            k_up(c, c).start()
        for q in range(before, CHUNKS):
            x_end(c, c, q, inward, i).start()
        for at in (2, 3, 4):
            local[at].wait()
        read_tables()

        @pl.when(o == host_core)
        def _():
            arrived(dn.at[:, :, other_half], ex_recv.at[1])

        transpose_panels(dn, kept, 0)
        arrived(ucat.at[pl.ds(0, panels), :, other_cols], ex_recv.at[2])
        arrived(wbuf.at[pl.ds(0, slab)], ex_recv.at[0])

        def p_copy(t):
            return remote(pbuf.at[t], prec.at[t], p_send.at[0], p_recv.at[t], peer(i))

        def p_core(t):
            return remote(
                pbuf.at[t, other], prec.at[t, 0], p_send.at[1], s_recv.at[t], peer(c, other)
            )

        def end_partial(t):
            put(pbuf, t, end_value(c, t, half_at(kept)))
            if t == c or not low:
                p_core(t).start()

        end_partial(c)
        if low:
            p_copy(c).start()
        for index, t in enumerate((i, j, f)):
            arrived(xb.at[t, :, half_at(kept)], x_recv.at[index])
            end_partial(t)
            if low:
                p_copy(t).start()
        if not low:
            for t in range(c):
                p_copy(t).start()
        local[5].wait()
        if not low:
            local[6].wait()
            arrived(kb.at[pl.ds(0, n - 1)], k_recv.at[0])
        attend(c)

        def take(t):
            arrived(prec.at[t, 0], s_recv.at[t])
            arrived(vall.at[t], v_recv.at[t])
            own_rows = vall[t, o].astype(f32) + pbuf[t, o].astype(f32)
            other_rows = vall[t, other].astype(f32) + prec[t, 0].astype(f32)
            if t == c or t == i:
                at = int(t != c)
                arrived(va.at[at], d_recv.at[at])
                own_rows = own_rows + va[at, o].astype(f32)
                other_rows = other_rows + va[at, other].astype(f32)
            vall[t, o] = own_rows.astype(bf16)
            vall[t, other] = other_rows.astype(bf16)

        for t in (0,) if low else (0, i, c, j):
            take(t)
        mix(c)

        sent(wbuf.at[pl.ds(0, slab)], ex_send.at[0])
        sent(ucat.at[pl.ds(0, panels), :, other_cols], ex_send.at[2])
        sent(hdn.at[mine, my_piece, :], ph_send.at[0])

        @pl.when(o == host_core)
        def _():
            sent(hdn.at[mine, my_piece, :], ph_send.at[1])

        @pl.when(o != host_core)
        def _():
            sent(dn.at[:, :, my_half], ex_send.at[1])

        sent(ucat.at[my_up, :, my_cols], uh_send.at[0])
        sent(xb.at[0], x_send.at[0])
        if c == 0:
            sent(kb.at[0], k_send)
            sent(pbuf, p_send.at[0])
            sent(pbuf.at[0, 0], p_send.at[1])
        else:
            sent(pbuf.at[pl.ds(0, n - 1)], p_send.at[0])
            sent(pbuf.at[:, 0], p_send.at[1])

    def inner_program(c):
        low = c < n // 2
        e, j, f = (0, 2, 3) if low else (3, 1, 0)
        inward = int(low)
        outward = 1 - inward
        first = min(c, e, j)
        greetings = [peer(c, other), peer(e), peer(e, other), peer(j), peer(c, o, 1 - g)]
        if low:
            greetings += [peer(f), peer(f, other)]
        opening(c, greetings, 5 if low else 7)
        w_copy, dn_copy, up_copy = exchange(c, None)

        def own_across(q):
            x_across(c, q, inward, j, False).start()

        for q in range(CHUNKS // 2):
            own_across(q)
            x_outward(c, q, outward, e, 0).start()
        if not low:
            own_across(2)
            own_across(3)
        w_copy.start()
        dn_copy.start()
        up_copy.start()
        local[6].wait()
        for at in (2, 3, 4):
            local[at].wait()
        read_tables()

        def next_e(q):
            arrived(xb.at[e, :, chunk(q, inward)], x_recv.at[q])
            x_across(e, q, inward, j, True).start()

        def next_j(q):
            arrived(xb.at[j, :, chunk(q, outward)], x_recv.at[4 + q])
            x_outward(j, q, outward, e, 1).start()

        def next_f(q):
            arrived(xb.at[f, :, chunk(q, outward)], x_recv.at[7 + q])
            x_outward(f, q, outward, e, 2).start()

        def piece(which, ranks_at):
            return hdn.at[which, ranks_at, :]

        def pass_on(which, ranks_at, sem, recv, device):
            return remote(piece(which, ranks_at), piece(which, ranks_at), ph_send.at[sem], ph_recv.at[recv], device)

        def pass_up(which, sem, recv, device):
            at = ucat.at[which, :, my_cols]
            return remote(at, at, uh_send.at[sem], uh_recv.at[recv], device)

        def host_z():
            arrived(piece(mine, my_piece), ph_recv.at[0])
            pass_on(mine, my_piece, 0, 1, peer(c, o, 1 - g)).start()
            pass_on(mine, my_piece, 1, 2, peer(c, other)).start()

        def host_up():
            arrived(ucat.at[my_up, :, my_cols], uh_recv.at[0])
            pass_up(my_up, 0, 1, peer(c, o, 1 - g)).start()
            pass_up(my_up, 1, 2, peer(c, other)).start()

        def host_y():
            arrived(piece(theirs, my_piece), ph_recv.at[1])
            pass_on(theirs, my_piece, 1, 3, peer(c, other)).start()

        def host_yu():
            arrived(ucat.at[their_up, :, my_cols], uh_recv.at[1])
            pass_up(their_up, 1, 3, peer(c, other)).start()

        def host_done():
            arrived(piece(mine, other_piece), ph_recv.at[2])
            arrived(piece(theirs, other_piece), ph_recv.at[3])
            transpose_panels(hdn, inward, low_width)
            arrived(ucat.at[my_up, :, other_cols], uh_recv.at[2])
            arrived(ucat.at[their_up, :, other_cols], uh_recv.at[3])

        def own_weights():
            arrived(dn.at[:, :, other_half], ex_recv.at[1])
            transpose_panels(dn, outward, 0)
            transpose_panels(dn, inward, 0)
            arrived(ucat.at[pl.ds(0, panels), :, other_cols], ex_recv.at[2])
            arrived(wbuf.at[pl.ds(0, slab)], ex_recv.at[0])

        def rest_of_j():
            arrived(xb.at[j, :, half_at(inward)], x_recv.at[6])

        def rest_of_f():
            arrived(xb.at[f, :, half_at(inward)], x_recv.at[9])

        def own(at, count):
            first_part(c, at, count, half_at(outward))

        def hosted(at, count):
            last_part(c, at, count, e, half_at(inward))

        def s_copy(t):
            return remote(sbuf.at[t], srec.at[t], s_send, s_recv.at[t], peer(j))

        def s_far(t, core):
            at = int(t != f)
            return remote(sbuf.at[t, core], va.at[at, o], d_send, d_recv.at[at], peer(f, core))

        def v_end(t, core):
            return remote(vbuf.at[t, core], vall.at[t, o], v_send.at[0], v_recv.at[t], peer(e, core))

        def v_core(t):
            return remote(vx.at[t, other], vall.at[t, o], v_send.at[1], v_recv.at[t], peer(c, other))

        def give_end(t):
            v_end(t, o).start()
            v_end(t, other).start()

        def keep(t, value):
            put(vx, t, value)
            v_core(t).start()
            vall[t, o] = vx[t, o]

        def early(t):
            put(vbuf, t, pown[t])
            give_end(t)

        def add_end(t):
            arrived(prec.at[t], p_recv.at[t])
            value = pown[t] + get(prec, t)
            put(sbuf, t, value)
            if t == f or (low and t == j):
                if low and t == j:
                    pl.semaphore_wait(ready, 2)
                s_far(t, 0).start()
                s_far(t, 1).start()
            if t != f or not low:
                s_copy(t).start()
            return value

        def relay(t):
            arrived(srec.at[t], s_recv.at[t])
            value = pown[t] + get(srec, t)
            if t == c:
                arrived(prec.at[t], p_recv.at[t])
            else:
                put(vbuf, t, value)
                give_end(t)
            keep(t, value + get(prec, t))

        def next_k(t):
            arrived(kb.at[t], k_recv.at[t])
            k_up(c, t).start()

        if low:
            next_e(0)
            next_e(1)
            k_up(c, c).start()
            own_across(2)
            own_weights()
            next_j(0)
            next_j(1)
            host_z()
            rest_of_j()
            next_e(2)
            own_across(3)
            host_up()
            next_f(0)
            next_k(0)
            host_y()
            next_e(3)
            host_yu()
            next_f(1)
            own(first, 3)
            host_done()
            hosted(first, 3)
            early(e)
            for t in range(3):
                pown[t] = add_end(t)
            own(f, 1)
            local[5].wait()
            attend(c)
            rest_of_f()
            hosted(f, 1)
            add_end(f)
            for t in (1, 0):
                arrived(srec.at[t], s_recv.at[t])
                keep(t, pown[t] + get(srec, t))
        else:
            own_weights()
            next_j(0)
            next_j(1)
            host_z()
            next_f(0)
            next_e(0)
            next_f(1)
            k_up(c, c).start()
            host_up()
            next_k(1)
            own(f, 2)
            next_e(1)
            host_y()
            next_e(2)
            host_yu()
            next_e(3)
            own(c, 2)
            host_done()
            hosted(c, 2)
            early(c)
            early(e)
            next_k(0)
            rest_of_f()
            hosted(f, 1)
            add_end(f)
            rest_of_j()
            hosted(j, 1)
            add_end(j)
            relay(f)
            relay(j)
            local[5].wait()
            attend(c)
            relay(c)
        for t in range(c + 1):
            arrived(vall.at[t, other], v_recv.at[t])
        mix(c)

        sent(wbuf.at[pl.ds(0, slab)], ex_send.at[0])
        sent(dn.at[:, :, my_half], ex_send.at[1])
        sent(ucat.at[pl.ds(0, panels), :, other_cols], ex_send.at[2])
        sent(xb.at[pl.ds(0, 2)], x_send.at[0])
        sent(xb.at[pl.ds(0, 3), :, half_at(0)], x_send.at[1])
        sent(piece(mine, my_piece), ph_send.at[0])
        sent(hdn.at[:, my_piece, :], ph_send.at[1])
        sent(ucat.at[my_up, :, my_cols], uh_send.at[0])
        sent(ucat.at[pl.ds(panels, panels), :, my_cols], uh_send.at[1])
        sent(kb.at[pl.ds(0, c + 1)], k_send)
        if low:
            sent(sbuf.at[pl.ds(0, 3)], s_send)
            sent(sbuf.at[pl.ds(0, 2)], d_send)
            sent(vbuf.at[0], v_send.at[0])
        else:
            sent(sbuf.at[pl.ds(0, 2)], s_send)
            sent(sbuf.at[0], d_send)
            sent(vbuf, v_send.at[0])
        sent(vx.at[pl.ds(0, c + 1), 0], v_send.at[1])

    for c in range(n):

        @pl.when(s == c)
        def _():
            ends.clear()
            slot_of.clear()
            rank_of.clear()
            if c in (0, n - 1):
                end_program(c)
            else:
                inner_program(c)


def fused(
    n,
    layer_input_rows,
    encoded_query_rows,
    encoded_key_rows,
    layer_norm_gain,
    base_value_matrix,
    adapter_down_panels,
    adapter_up_panels,
    request_token_lengths,
    adapter_per_request,
    rank_per_adapter,
    slot_per_adapter,
):
    f32, bf16 = jnp.float32, jnp.bfloat16
    tok, width = layer_input_rows.shape[1:]
    part, half = tok // 2, width // 2
    panels, _, rank_width = adapter_down_panels.shape[1:]
    vcols = adapter_up_panels.shape[3]
    qcols = encoded_query_rows.shape[2]
    chip_rows = width // n
    pads = [i * chip_rows % LANES for i in range(n)]
    win = -(-(max(pads) + chip_rows) // LANES) * LANES
    total = n * tok
    dma = pltpu.SemaphoreType.DMA
    any_spec = pl.BlockSpec(memory_space=pl.ANY)
    return pl.pallas_call(
        functools.partial(kernel, n),
        out_shape=pltpu.VMEM(encoded_query_rows.shape[1:], bf16),
        in_specs=[any_spec] * 11,
        out_specs=pl.BlockSpec(memory_space=pltpu.VMEM),
        scratch_shapes=[
            pltpu.SMEM(request_token_lengths.shape, jnp.int32),
            pltpu.SMEM(adapter_per_request.shape, jnp.int32),
            pltpu.SMEM(rank_per_adapter.shape, jnp.int32),
            pltpu.SMEM(slot_per_adapter.shape, jnp.int32),
            pltpu.VMEM((part, width), bf16),
            pltpu.VMEM((1, width), f32),
            pltpu.VMEM((n, part, width), bf16),
            pltpu.VMEM((win, 2 * vcols), bf16),
            pltpu.VMEM((panels, rank_width, width), bf16),
            pltpu.VMEM((panels, rank_width, half), bf16),
            pltpu.VMEM((width, 2 * panels * rank_width), bf16),
            pltpu.VMEM((2 * panels, rank_width, 2 * vcols), bf16),
            pltpu.VMEM((tok, qcols), bf16),
            pltpu.VMEM((n, tok, vcols), bf16),
            pltpu.VMEM((n, part, 2 * vcols), f32),
            pltpu.VMEM((n, part, panels * rank_width), f32),
            pltpu.VMEM((n, 2, part, vcols), bf16),
            pltpu.VMEM((n, 2, part, vcols), bf16),
            pltpu.VMEM((n, 2, part, vcols), bf16),
            pltpu.VMEM((n, 2, part, vcols), bf16),
            pltpu.VMEM((n, 2, part, vcols), bf16),
            pltpu.VMEM((n, 2, part, vcols), bf16),
            pltpu.VMEM((n, 2, part, vcols), bf16),
            pltpu.VMEM((2, 2, part, vcols), bf16),
            pltpu.VMEM((qcols // HEAD_SIZE, tok, total), bf16),
            dma((11,)),
            dma((2,)),
            dma((10,)),
            dma((3,)),
            dma((3,)),
            dma((2,)),
            dma((4,)),
            dma((2,)),
            dma((4,)),
            dma,
            dma((2,)),
            dma((2,)),
            dma((n,)),
            dma,
            dma((n,)),
            dma((2,)),
            dma((n,)),
            dma((2,)),
            dma,
            pltpu.SemaphoreType.REGULAR,
        ],
        compiler_params=pltpu.CompilerParams(
            collective_id=0, has_side_effects=True, vmem_limit_bytes=56 * 1024 * 1024
        ),
    )(
        layer_input_rows,
        encoded_query_rows,
        encoded_key_rows,
        layer_norm_gain,
        base_value_matrix,
        jnp.swapaxes(adapter_down_panels, 2, 3),
        adapter_up_panels,
        request_token_lengths,
        adapter_per_request,
        rank_per_adapter,
        slot_per_adapter,
    )[None]


def solution(mesh):
    in_specs = (
        P("segment", ("groups", "seq"), None),
        P("segment", ("groups", "seq"), "owner"),
        P("segment", ("groups", "seq"), "owner"),
        P("segment", None),
        P("segment", ("seq", "owner"), None),
        P("segment", "seq", "owner", None),
        P("segment", "seq", None, "owner"),
        P("groups"),
        P("groups"),
        P(),
        P(),
    )
    out_specs = P("segment", ("groups", "seq"), "owner")
    n = mesh.shape["seq"]
    small = mesh.shape["owner"] == 2 and mesh.shape["groups"] == 2 and n == 4
    return jax.shard_map(
        functools.partial(fused, n) if small else per_device, mesh=mesh, in_specs=in_specs, out_specs=out_specs, check_vma=False
    )
```
